32 devices in a mesh: ctx: 8 (over z, y), fsdp: 4 (over x, core).
Axes of the slice: x: 2, y: 2, z: 4, core: 2. Of those that a mesh axis runs over, the one named last changes fastest.
Arguments:
- tokens: bfloat16 [4, 2048, 1024], P('fsdp', 'ctx'), may hold values from -6 to 6
- out_grad: bfloat16 [4, 2048, 1024], P('fsdp', 'ctx'), may hold values from -6 to 6
- lengths: int32 [4, 1], P('fsdp'), may hold values from 512 to 2048, as said below
- norm1_gain: bfloat16 [1024], P('fsdp'), may hold values from 0.5 to 1.5
- w_query: bfloat16 [1024, 1024], P('fsdp'), may hold values from -0.1875 to 0.1875
- w_latent: bfloat16 [1024, 512], P('fsdp'), may hold values from -0.1875 to 0.1875
- w_key_up: bfloat16 [1024, 256], P('fsdp'), may hold values from -0.75 to 0.75
- w_value_up: bfloat16 [1024, 256], P('fsdp'), may hold values from -0.375 to 0.375
- w_output: bfloat16 [1024, 1024], P('fsdp'), may hold values from -1.5 to 1.5
- norm2_gain: bfloat16 [1024], P('fsdp'), may hold values from 0.5 to 1.5
- w_gate: bfloat16 [1024, 2816], P(None, 'fsdp'), may hold values from -0.1875 to 0.1875
- w_up: bfloat16 [1024, 2816], P(None, 'fsdp'), may hold values from -0.1875 to 0.1875
- w_down: bfloat16 [2816, 1024], P('fsdp'), may hold values from -0.109375 to 0.109375
Outputs:
- result: bfloat16 [4, 2048, 1024], P('fsdp', 'ctx')
- token_grad: float32 [4, 2048, 1024], P('fsdp', 'ctx')
- norm1_gain_grad: float32 [1024], P('fsdp')
- w_query_grad: float32 [1024, 1024], P('fsdp')
- w_latent_grad: float32 [1024, 512], P('fsdp')
- w_key_up_grad: float32 [1024, 256], P('fsdp')
- w_value_up_grad: float32 [1024, 256], P('fsdp')
- w_output_grad: float32 [1024, 1024], P('fsdp')
- norm2_gain_grad: float32 [1024], P('fsdp')
- w_gate_grad: float32 [1024, 2816], P(None, 'fsdp')
- w_up_grad: float32 [1024, 2816], P(None, 'fsdp')
- w_down_grad: float32 [2816, 1024], P('fsdp')
The draws below stay inside these ranges and needn't reach their ends.
Inputs may be any that keep to these rules, and one draw needn't show every extreme that they name: lengths[g, j] valid tokens stand at the start of slot j of group g; the rest of the slot of 2048 rows is padding.
All inputs are finite; a program needn't handle non-finite values.
Results may differ from the reference program's by a relative error of at most 0.025.
Values may be sent and summed in bfloat16 or wider, within the bound.
No kernel may reach another device: no remote copies, remote signals or barrier semaphores. Data moves between devices by JAX's collectives and lax.ppermute only.
A program may use at most 192 MiB of HBM per device.

```python
from functools import partial
import jax
import jax.numpy as jnp
from jax import lax

D = 1024
NH = 16
HD = 64
LAT = 256
GRP = 2
FF = 2816
TOK_G = 2048
SEQ = 2048
SEQS_G = 1
GROUPS = 4


def draw_lengths(key, part):
    values = jax.random.randint(key, (GROUPS, SEQS_G), SEQ // 4, SEQ + 1, dtype=jnp.int32)
    return values.at[0, 0].set(SEQ)


def level_of(stream_key, extent, pieces, least, largest):
    loudness, own = 1.0, jax.random.fold_in(stream_key, 6)
    for dim, blocks in pieces:
        draws = jnp.exp(jax.random.uniform(jax.random.fold_in(own, dim), (blocks,), jnp.float32, least / len(pieces), largest / len(pieces)))
        loudness = loudness * jnp.repeat(draws, extent[dim] // blocks).reshape([-1 if axis == dim else 1 for axis in range(len(extent))])
    return loudness


def scatter_about(stream_key, dims, spread, reach, shards=(), kind=jnp.bfloat16):
    entries = spread * jax.random.normal(stream_key, dims, jnp.float32)
    if shards:
        entries = entries * level_of(stream_key, dims, shards, -0.22, 0.18)
    return jnp.clip(entries, -reach, reach).astype(kind)


def setup_inputs(seed: int = 0) -> dict:
    key_of = jax.random.split(jax.random.key(seed), 14)
    tokens = scatter_about(key_of[0], (GROUPS, TOK_G, D), 1.0, 6.0, ((0, 4), (1, 8)))
    out_grad = scatter_about(key_of[1], (GROUPS, TOK_G, D), 1.0, 6.0, ((0, 4), (1, 8)))
    lengths = draw_lengths(jax.random.fold_in(key_of[13], 71), 0)
    norm1_gain = jnp.clip(1.0 + 0.1 * jax.random.normal(key_of[3], (D,), jnp.float32), 0.5, 1.5).astype(jnp.bfloat16)
    w_query = scatter_about(key_of[4], (D, NH * HD), D ** -0.5, 0.1875, ((0, 4),))
    w_latent = scatter_about(key_of[5], (D, GRP * LAT), D ** -0.5, 0.1875, ((0, 4),))
    w_key_up = scatter_about(key_of[6], (NH * HD, LAT), HD ** -0.5, 0.75, ((0, 4),))
    w_value_up = scatter_about(key_of[7], (NH * HD, LAT), LAT ** -0.5, 0.375, ((0, 4),))
    w_output = scatter_about(key_of[8], (NH * HD, D), 16 ** -0.5, 1.5, ((0, 4),))
    norm2_gain = jnp.clip(1.0 + 0.1 * jax.random.normal(key_of[9], (D,), jnp.float32), 0.5, 1.5).astype(jnp.bfloat16)
    w_gate = scatter_about(key_of[10], (D, FF), D ** -0.5, 0.1875, ((1, 4),))
    w_up = scatter_about(key_of[11], (D, FF), D ** -0.5, 0.1875, ((1, 4),))
    w_down = scatter_about(key_of[12], (FF, D), FF ** -0.5, 0.109375, ((0, 4),))
    return dict(tokens=tokens, out_grad=out_grad, lengths=lengths, norm1_gain=norm1_gain, w_query=w_query, w_latent=w_latent, w_key_up=w_key_up, w_value_up=w_value_up, w_output=w_output, norm2_gain=norm2_gain, w_gate=w_gate, w_up=w_up, w_down=w_down)


EPS = 1e-06
NEGATIVE = -1e+30

@jax.custom_vjp
def low(v):
    return lax.optimization_barrier(v.astype(jnp.bfloat16)).astype(jnp.float32)

@jax.custom_vjp
def low_back(v):
    return v

def low_keep(v):
    return (low(v), None)

def low_pass(kept, grad):
    return (grad,)

def back_keep(v):
    return (v, None)

def back_low(kept, grad):
    return (low(grad),)
low.defvjp(low_keep, low_pass)
low_back.defvjp(back_keep, back_low)

def product(left, right):
    return jnp.dot(left, right, precision=lax.Precision.HIGHEST, preferred_element_type=jnp.float32)

def norm_scale(values):
    return lax.rsqrt(lax.optimization_barrier(jnp.mean(values * values, axis=-1, keepdims=True)) + EPS)

def attend_block(latent, key_valid, score_scale, block_args):
    query_block, query_pos = block_args
    grouped = latent.reshape(latent.shape[0], GRP, LAT)
    scores = jnp.einsum('gpql,kgl->gpqk', query_block, grouped, precision=lax.Precision.HIGHEST) * score_scale
    scores = low_back(scores)
    key_pos = jnp.arange(latent.shape[0], dtype=jnp.int32)
    allowed = (key_pos[None, :] <= query_pos[:, None]) & key_valid[None, :]
    masked = jnp.where(allowed[None, None], scores, NEGATIVE)
    weights = low(jax.nn.softmax(masked, axis=-1))
    return jnp.einsum('gpqk,kgl->gpql', weights, grouped, precision=lax.Precision.HIGHEST)

def block_layer(inputs, length, params):
    gain_one, w_query, w_latent, w_key_up, w_value_up, w_output, gain_two, w_gate, w_up, w_down = params
    row_count = inputs.shape[0]
    positions = jnp.arange(row_count, dtype=jnp.int32)
    key_valid = positions < length
    normed = low(inputs * norm_scale(inputs) * gain_one)
    queries = low_back(low(product(normed, w_query)))
    latent = low_back(low(product(normed, w_latent)))
    per_head = queries.reshape(row_count, NH, HD)
    query_latent = low_back(low(jnp.einsum('shd,hdl->hsl', per_head, w_key_up.reshape(NH, HD, LAT), precision=lax.Precision.HIGHEST)))
    block_rows = min(512, row_count)
    blocks = row_count // block_rows
    grouped_q = query_latent.reshape(GRP, NH // GRP, blocks, block_rows, LAT).transpose(2, 0, 1, 3, 4)
    pos_blocks = positions.reshape(blocks, block_rows)
    attend = jax.checkpoint(partial(attend_block, latent, key_valid, HD ** (-0.5)))
    mixture = lax.map(attend, (grouped_q, pos_blocks))
    mixture = mixture.transpose(1, 2, 0, 3, 4).reshape(NH, row_count, LAT)
    mixture = low_back(low(mixture))
    attended = jnp.einsum('hsl,hdl->shd', mixture, w_value_up.reshape(NH, HD, LAT), precision=lax.Precision.HIGHEST)
    attended = low_back(low(attended.reshape(row_count, NH * HD)))
    branch = low_back(product(attended, w_output))
    middle = inputs + branch
    normed_two = low(middle * norm_scale(middle) * gain_two)
    gate_value = low_back(product(normed_two, w_gate))
    upward = low_back(product(normed_two, w_up))
    hidden = low(jax.nn.silu(gate_value) * upward)
    feed_out = low_back(product(hidden, w_down))
    return (middle + feed_out) * key_valid[:, None].astype(jnp.float32)

def reference(tokens, out_grad, lengths, norm1_gain, w_query, w_latent, w_key_up, w_value_up, w_output, norm2_gain, w_gate, w_up, w_down):
    params = tuple((weight_in.astype(jnp.float32) for weight_in in (norm1_gain, w_query, w_latent, w_key_up, w_value_up, w_output, norm2_gain, w_gate, w_up, w_down)))
    seq_count = tokens.shape[0] * tokens.shape[1] // SEQ
    inputs_all = tokens.astype(jnp.float32).reshape(seq_count, SEQ, D)
    grads_all = out_grad.astype(jnp.float32).reshape(seq_count, SEQ, D)
    lengths_all = lengths.reshape(seq_count).astype(jnp.int32)

    def step_fn(totals, seq_item):
        inputs, cotangent, length = seq_item
        output_now, pull_back = jax.vjp(lambda values, weights: block_layer(values, length, weights), inputs, params)
        input_grad, weight_grads = pull_back(cotangent)
        totals = jax.tree.map(lambda running, addend: running + addend, totals, weight_grads)
        return (totals, (output_now.astype(jnp.bfloat16), input_grad))
    zeros_init = jax.tree.map(jnp.zeros_like, params)
    totals, (outputs, input_grads) = lax.scan(step_fn, zeros_init, (inputs_all, grads_all, lengths_all))
    full_shape = tokens.shape
    return (outputs.reshape(full_shape), input_grads.reshape(full_shape), totals[0], totals[1], totals[2], totals[3], totals[4], totals[5], totals[6], totals[7], totals[8], totals[9])
```

```python
import functools

import jax
import jax.numpy as jnp
from jax import lax
from jax.experimental import pallas as pl
from jax.experimental.pallas import tpu as pltpu
from jax.sharding import PartitionSpec as P

NH = 16
HD = 64
LAT = 256
GRP = 2
SEQ_MAX = 4096
EPS = 1e-06
NEGATIVE = -1e30
HPG = NH // GRP
HB = 2
ORDER = (0, 2, 1, 3)
F32 = jnp.float32
BF16 = jnp.bfloat16


def dot(left, right, contract=((1,), (0,))):
    return lax.dot_general(left, right, (contract, ((), ())), preferred_element_type=F32)


def norm_scale(values):
    return lax.rsqrt(jnp.mean(values * values, axis=-1, keepdims=True) + EPS)


def norm_back(grad_in, normed, scale_rows, gain_full):
    scaled = grad_in * gain_full
    return scale_rows * (scaled - normed * jnp.mean(scaled * normed, axis=-1, keepdims=True))


def swap(value, axis, mask):
    size = lax.axis_size(axis)
    return lax.ppermute(value, axis, [(s, s ^ mask) for s in range(size)])


def gather_four(value):
    across = swap(value, "fsdp", 2)
    beside = swap(value, "fsdp", 1)
    both = swap(across, "fsdp", 1)
    return [value, across, beside, both]


def scatter_four(first_two, last_two):
    got = swap(last_two, "fsdp", 1)
    near = first_two.astype(F32) + got.astype(F32)
    far = swap(near[1].astype(BF16), "fsdp", 2)
    return near[0] + far.astype(F32)


def ring_members(count):
    return list(range(0, count, 2)) + list(range(count - 1, 0, -2)) if count > 1 else [0]


def ring_shift(value, slot_blocks, step):
    size = lax.axis_size("ctx")
    order = ring_members(slot_blocks)
    pairs = []
    for base in range(0, size, slot_blocks):
        for place in range(slot_blocks):
            pairs.append((base + order[place], base + order[(place + step) % slot_blocks]))
    return lax.ppermute(value, "ctx", pairs)


def ring_gather(block, slot_blocks):
    rows = block.shape[0]
    half = slot_blocks // 2
    out = [block]
    from_left, from_right = block, block
    for _ in range(half - 1):
        from_left = ring_shift(from_left, slot_blocks, 1)
        from_right = ring_shift(from_right, slot_blocks, -1)
        out += [from_left, from_right]
    top = ring_shift(from_left[: rows // 2], slot_blocks, 1)
    low = ring_shift(from_right[rows // 2 :], slot_blocks, -1)
    out.append(jnp.concatenate([top, low], axis=0))
    return out


def ring_scatter(terms, slot_blocks):
    rows = terms.shape[1]
    half = slot_blocks // 2
    zero = jnp.zeros((rows // 2, terms.shape[2]), F32)
    last = terms[slot_blocks - 1]
    right = ring_shift(last[: rows // 2], slot_blocks, 1).astype(F32)
    left = ring_shift(last[rows // 2 :], slot_blocks, -1).astype(F32)
    right = jnp.concatenate([right, zero], axis=0)
    left = jnp.concatenate([zero, left], axis=0)
    for k in range(half - 1, 0, -1):
        right = (right + terms[2 * k].astype(F32)).astype(BF16)
        left = (left + terms[2 * k - 1].astype(F32)).astype(BF16)
        right = ring_shift(right, slot_blocks, 1).astype(F32)
        left = ring_shift(left, slot_blocks, -1).astype(F32)
    return terms[0].astype(F32) + right + left


def sum_over_ctx(value, order):
    me = lax.axis_index("ctx")
    cur = value
    for bit in order:
        mine = (me >> bit) & 1
        pair = cur.reshape((2, cur.shape[0] // 2) + cur.shape[1:])
        send = lax.dynamic_index_in_dim(pair, 1 - mine, 0, keepdims=False)
        keep = lax.dynamic_index_in_dim(pair, mine, 0, keepdims=False)
        got = swap(send, "ctx", 1 << bit)
        cur = (keep.astype(F32) + got.astype(F32)).astype(BF16)
    for bit in reversed(order):
        mine = (me >> bit) & 1
        got = swap(cur, "ctx", 1 << bit)
        pair = jnp.zeros((2,) + cur.shape, BF16)
        pair = lax.dynamic_update_index_in_dim(pair, cur, mine, 0)
        pair = lax.dynamic_update_index_in_dim(pair, got, 1 - mine, 0)
        cur = pair.reshape((2 * cur.shape[0],) + cur.shape[1:])
    return cur


def place_of(rank, slots):
    return jnp.where(rank % 2 == 0, rank // 2, slots - 1 - rank // 2)


def member_at(place, slots):
    place = lax.rem(place + slots, slots)
    return jnp.where(place < slots // 2, 2 * place, 2 * (slots - 1 - place) + 1)


def block_start(rank, slot, slots, rows):
    steps = (slot + 1) // 2
    signed = jnp.where(slot % 2 == 1, -steps, steps)
    return member_at(place_of(rank, slots) + signed, slots) * rows


def score_mask(first_key, first_query, length, rows, width):
    key = first_key + lax.broadcasted_iota(jnp.int32, (rows, width), 0)
    query = first_query + lax.rem(lax.broadcasted_iota(jnp.int32, (rows, width), 1), rows)
    return (key <= query) & (key < length)


def forward_kernel(slots, meta, q_ref, wk_ref, wv_ref, c_ref, att_ref, ol_ref, lse_ref,
                   ct_ref, ql_ref, m_ref, l_ref, acc_ref):
    rows = q_ref.shape[1]
    rank, length = meta[0], meta[1]
    first_query = rank * rows
    step = pl.program_id(0)

    def needed(start):
        return (start <= first_query) & (start < length) & (first_query < length)

    @pl.when(step % (HPG // HB) == 0)
    def _():
        def turn(slot, carry):
            @pl.when(needed(block_start(rank, slot, slots, rows)))
            def _():
                ct_ref[slot] = c_ref[slot].T
            return carry

        lax.fori_loop(0, slots, turn, 0)

    for i in range(HB):
        part = pl.ds(i * HD, HD)
        latent_q = dot(wk_ref[part, :], q_ref[part, :], ((0,), (0,))).astype(BF16)
        ql_ref[:, i * rows : (i + 1) * rows] = latent_q * jnp.asarray(HD ** -0.5, BF16)
    m_ref[...] = jnp.full_like(m_ref, NEGATIVE)
    l_ref[...] = jnp.zeros_like(l_ref)
    acc_ref[...] = jnp.zeros_like(acc_ref)

    def block(slot, start, masked):
        scores = dot(c_ref[slot], ql_ref[...])
        if masked:
            allowed = score_mask(start, first_query, length, rows, HB * rows)
            scores = jnp.where(allowed, scores, NEGATIVE)
        best = jnp.maximum(m_ref[...], jnp.max(scores, axis=0, keepdims=True))
        weights = jnp.exp(scores - best)
        if masked:
            weights = jnp.where(allowed, weights, 0.0)
        factor = jnp.exp(m_ref[...] - best)
        m_ref[...] = best
        l_ref[...] = l_ref[...] * factor + jnp.sum(weights, axis=0, keepdims=True)
        acc_ref[...] = acc_ref[...] * factor + dot(ct_ref[slot], weights.astype(BF16))

    def loop(slot, carry):
        start = block_start(rank, slot, slots, rows)
        plain = (start + rows <= first_query + 1) & (start + rows <= length)

        @pl.when(needed(start) & plain)
        def _():
            block(slot, start, False)

        @pl.when(needed(start) & jnp.logical_not(plain))
        def _():
            block(slot, start, True)

        return carry

    lax.fori_loop(0, slots, loop, 0)
    total = l_ref[...]
    seen = total > 0.0
    safe = jnp.where(seen, total, 1.0)
    lse_all = jnp.where(seen, m_ref[...] + jnp.log(safe), 0.0)
    mixture = (acc_ref[...] * (1.0 / safe)).astype(BF16)
    for i in range(HB):
        part = pl.ds(i * HD, HD)
        cols = slice(i * rows, (i + 1) * rows)
        lse_ref[i] = lse_all[:, cols]
        ol_ref[i] = mixture[:, cols]
        att_ref[part, :] = dot(wv_ref[part, :], mixture[:, cols]).astype(BF16)


def backward_kernel(slots, meta, q_ref, da_ref, wk_ref, wv_ref, c_ref, ol_ref, lse_ref,
                    dq_ref, dwk_ref, dwv_ref, dc_ref,
                    ct_ref, dc_acc, qlt_ref, dot_ref, both_ref, dql_ref, delta_ref):
    rows = q_ref.shape[1]
    rank, length = meta[0], meta[1]
    first_query = rank * rows
    step = pl.program_id(0)
    steps = HPG // HB
    scale = jnp.asarray(HD ** -0.5, BF16)

    def needed(start):
        return (start <= first_query) & (start < length) & (first_query < length)

    @pl.when(step % steps == 0)
    def _():
        dc_acc[...] = jnp.zeros_like(dc_acc)

        def turn(slot, carry):
            @pl.when(needed(block_start(rank, slot, slots, rows)))
            def _():
                ct_ref[slot] = c_ref[slot].T
            return carry

        lax.fori_loop(0, slots, turn, 0)

    for i in range(HB):
        part = pl.ds(i * HD, HD)
        q_t, da_t, wk, wv = q_ref[part, :], da_ref[part, :], wk_ref[part, :], wv_ref[part, :]
        qlt_ref[i] = dot(wk, q_t, ((0,), (0,))).astype(BF16) * scale
        both_ref[i, :rows] = dot(q_t, wk, ((0,), (0,))).astype(BF16) * scale
        dol_t = dot(wv, da_t, ((0,), (0,))).astype(BF16)
        dot_ref[i] = dol_t
        both_ref[i, rows:] = dot(da_t, wv, ((0,), (0,))).astype(BF16)
        delta_ref[i] = jnp.sum(dol_t.astype(F32) * ol_ref[i].astype(F32), axis=0, keepdims=True)
    dql_ref[...] = jnp.zeros_like(dql_ref)

    def block(slot, start, masked):
        keys = c_ref[slot]
        keys_t = ct_ref[slot]
        if masked:
            allowed = score_mask(start, first_query, length, rows, rows)
        total = dc_acc[slot]
        for i in range(HB):
            scores = dot(keys, qlt_ref[i])
            probs = jnp.exp(scores - lse_ref[i])
            if masked:
                probs = jnp.where(allowed, probs, 0.0)
            grads = dot(keys, dot_ref[i])
            score_grad = (probs * (grads - delta_ref[i])).astype(BF16)
            dql_ref[i] += dot(keys_t, score_grad)
            pair = jnp.concatenate([score_grad, probs.astype(BF16)], axis=1)
            total = total + dot(pair, both_ref[i])
        dc_acc[slot] = total

    def loop(slot, carry):
        start = block_start(rank, slot, slots, rows)
        plain = (start + rows <= first_query + 1) & (start + rows <= length)

        @pl.when(needed(start) & plain)
        def _():
            block(slot, start, False)

        @pl.when(needed(start) & jnp.logical_not(plain))
        def _():
            block(slot, start, True)

        return carry

    lax.fori_loop(0, slots, loop, 0)
    for i in range(HB):
        part = pl.ds(i * HD, HD)
        latent_grad = (dql_ref[i] * (HD ** -0.5)).astype(BF16)
        dq_ref[part, :] = dot(wk_ref[part, :], latent_grad).astype(BF16)
        dwk_ref[part, :] = dot(q_ref[part, :], latent_grad, ((1,), (1,))).astype(BF16)
        dwv_ref[part, :] = dot(da_ref[part, :], ol_ref[i], ((1,), (1,))).astype(BF16)

    @pl.when(step % steps == steps - 1)
    def _():
        dc_ref[...] = dc_acc[...].astype(BF16)


def head_place(step, member):
    per_piece = NH // 4 // HB
    mask = (step // per_piece) ^ member
    return ((mask & 1) * 2 + (mask >> 1)) * per_piece + step % per_piece


def attention_forward(meta, q_t, wk, wv, blocks):
    slots, rows, _ = blocks.shape
    own = lambda s, meta: (s, 0)
    placed = lambda s, meta: (head_place(s, meta[2]), 0)
    width = HB * HD
    return pl.pallas_call(
        functools.partial(forward_kernel, slots),
        name="attention_forward",
        grid_spec=pltpu.PrefetchScalarGridSpec(
            num_scalar_prefetch=1,
            grid=(NH // HB,),
            in_specs=[
                pl.BlockSpec((width, rows), own),
                pl.BlockSpec((width, LAT), placed),
                pl.BlockSpec((width, LAT), placed),
                pl.BlockSpec((slots, rows, LAT), lambda s, meta: (0, 0, s // (HPG // HB))),
            ],
            out_specs=[
                pl.BlockSpec((width, rows), placed),
                pl.BlockSpec((HB, LAT, rows), lambda s, meta: (s, 0, 0)),
                pl.BlockSpec((HB, 1, rows), lambda s, meta: (s, 0, 0)),
            ],
            scratch_shapes=[
                pltpu.VMEM((slots, LAT, rows), BF16),
                pltpu.VMEM((LAT, HB * rows), BF16),
                pltpu.VMEM((1, HB * rows), F32),
                pltpu.VMEM((1, HB * rows), F32),
                pltpu.VMEM((LAT, HB * rows), F32),
            ],
        ),
        out_shape=[
            jax.ShapeDtypeStruct((NH * HD, rows), BF16),
            jax.ShapeDtypeStruct((NH, LAT, rows), BF16),
            jax.ShapeDtypeStruct((NH, 1, rows), F32),
        ],
        compiler_params=pltpu.CompilerParams(
            dimension_semantics=("arbitrary",), vmem_limit_bytes=32 << 20
        ),
    )(meta, q_t, wk, wv, blocks)


def attention_backward(meta, q_t, da_t, wk, wv, blocks, ol, lse):
    slots, rows, _ = blocks.shape
    own = lambda s, meta: (s, 0)
    placed = lambda s, meta: (head_place(s, meta[2]), 0)
    whole = lambda s, meta: (0, 0, s // (HPG // HB))
    width = HB * HD
    return pl.pallas_call(
        functools.partial(backward_kernel, slots),
        name="attention_backward",
        grid_spec=pltpu.PrefetchScalarGridSpec(
            num_scalar_prefetch=1,
            grid=(NH // HB,),
            in_specs=[
                pl.BlockSpec((width, rows), own),
                pl.BlockSpec((width, rows), placed),
                pl.BlockSpec((width, LAT), placed),
                pl.BlockSpec((width, LAT), placed),
                pl.BlockSpec((slots, rows, LAT), whole),
                pl.BlockSpec((HB, LAT, rows), lambda s, meta: (s, 0, 0)),
                pl.BlockSpec((HB, 1, rows), lambda s, meta: (s, 0, 0)),
            ],
            out_specs=[
                pl.BlockSpec((width, rows), own),
                pl.BlockSpec((width, LAT), placed),
                pl.BlockSpec((width, LAT), placed),
                pl.BlockSpec((slots, rows, LAT), whole),
            ],
            scratch_shapes=[
                pltpu.VMEM((slots, LAT, rows), BF16),
                pltpu.VMEM((slots, rows, LAT), F32),
                pltpu.VMEM((HB, LAT, rows), BF16),
                pltpu.VMEM((HB, LAT, rows), BF16),
                pltpu.VMEM((HB, 2 * rows, LAT), BF16),
                pltpu.VMEM((HB, LAT, rows), F32),
                pltpu.VMEM((HB, 1, rows), F32),
            ],
        ),
        out_shape=[
            jax.ShapeDtypeStruct((NH * HD, rows), BF16),
            jax.ShapeDtypeStruct((NH * HD, LAT), BF16),
            jax.ShapeDtypeStruct((NH * HD, LAT), BF16),
            jax.ShapeDtypeStruct(blocks.shape, BF16),
        ],
        compiler_params=pltpu.CompilerParams(
            dimension_semantics=("arbitrary",), vmem_limit_bytes=40 << 20
        ),
    )(meta, q_t, da_t, wk, wv, blocks, ol, lse)


def on_device(
    tokens,
    out_grad,
    lengths,
    norm1_gain,
    w_query,
    w_latent,
    w_key_up,
    w_value_up,
    w_output,
    norm2_gain,
    w_gate,
    w_up,
    w_down,
):
    ctx_size = lax.axis_size("ctx")
    tok_rows, width = tokens.shape[1], tokens.shape[2]
    ff = w_gate.shape[1]
    group_rows = tok_rows * ctx_size
    seq_rows = min(SEQ_MAX, group_rows)
    slots = seq_rows // tok_rows
    ctx_rank = lax.axis_index("ctx")
    member = lax.axis_index("fsdp")
    slot_number = ctx_rank // slots
    rank = ctx_rank % slots
    length = jnp.sum(
        jnp.where(jnp.arange(lengths.shape[1], dtype=jnp.int32) == slot_number, lengths[0], 0)
    )
    meta = jnp.stack([rank, length, member]).astype(jnp.int32)
    query_pos = rank * tok_rows + jnp.arange(tok_rows, dtype=jnp.int32)
    row_valid = (query_pos < length).astype(F32)[:, None]
    piece = width // 4
    bits = ctx_size.bit_length() - 1

    def reorder(value):
        return jnp.concatenate(
            [lax.dynamic_slice_in_dim(value, (member ^ m) * piece, piece, 1) for m in ORDER], axis=1
        )

    def restore(value):
        back = {m: t for t, m in enumerate(ORDER)}
        parts = [value[:, back[m] * piece : (back[m] + 1) * piece] for m in range(4)]
        low = (member & 1) == 1
        parts = [jnp.where(low, parts[j ^ 1], parts[j]) for j in range(4)]
        high = (member & 2) == 2
        parts = [jnp.where(high, parts[j ^ 2], parts[j]) for j in range(4)]
        return jnp.concatenate(parts, axis=1)

    gains = jnp.stack([norm1_gain, norm2_gain])
    gain_pieces = gather_four(gains)
    latent_pieces = gather_four(w_latent)
    gate_order = lax.optimization_barrier((latent_pieces[1], w_query, w_key_up, w_value_up))
    latent_pieces[1] = gate_order[0]
    query_pieces = gather_four(gate_order[1])
    side = jnp.concatenate([gate_order[2], gate_order[3]], axis=1)
    side_pieces = gather_four(side)
    gate_order = lax.optimization_barrier((query_pieces[1], side_pieces[1], w_output))
    query_pieces[1], side_pieces[1] = gate_order[0], gate_order[1]
    output_pieces = gather_four(gate_order[2])
    cotangent = out_grad[0].astype(F32) * row_valid
    gate_order = lax.optimization_barrier((output_pieces[1], cotangent.astype(BF16)))
    output_pieces[1] = gate_order[0]
    feed_grad = jnp.concatenate(gather_four(gate_order[1]), axis=0)

    gain_one = jnp.concatenate([g[0] for g in gain_pieces])
    gain_two = restore(jnp.concatenate([g[1:] for g in gain_pieces], axis=1))
    gain_one_f = gain_one.astype(F32)
    gain_two_f = gain_two.astype(F32)
    query_full = jnp.concatenate(query_pieces, axis=0)
    latent_full = jnp.concatenate(latent_pieces, axis=0)
    side_full = jnp.concatenate(side_pieces, axis=0)
    key_full, value_full = side_full[:, :LAT], side_full[:, LAT:]
    output_full = jnp.concatenate(output_pieces, axis=0)

    inputs = tokens[0].astype(F32)
    mixed = reorder(tokens[0]).astype(F32)
    scale_one = norm_scale(inputs)
    normed_one = mixed * scale_one
    normed = (normed_one * gain_one_f).astype(BF16)
    latent = dot(normed, latent_full).astype(BF16)
    blocks = jnp.stack(ring_gather(latent, slots))
    q_t = dot(query_full, normed, ((0,), (1,))).astype(BF16)
    att_t, mixture, log_total = attention_forward(meta, q_t, key_full, value_full, blocks)
    middle = inputs + dot(att_t, output_full, ((0,), (0,)))
    scale_two = norm_scale(middle)
    normed_two_raw = middle * scale_two
    normed_two = (normed_two_raw * gain_two_f).astype(BF16)
    ff_in = jnp.concatenate(gather_four(normed_two), axis=0)

    gate_value = dot(ff_in, w_gate)
    upward = dot(ff_in, w_up)
    hidden_grad = dot(feed_grad, w_down, ((1,), (1,)))
    sigmoid_gate = jax.nn.sigmoid(gate_value)
    silu_gate = gate_value * sigmoid_gate
    hidden = (silu_gate * upward).astype(BF16)
    gate_grad = (
        hidden_grad * upward * sigmoid_gate * (1.0 + gate_value * (1.0 - sigmoid_gate))
    ).astype(BF16)
    up_grad = (hidden_grad * silu_gate).astype(BF16)
    normed_two_part = (
        dot(gate_grad, w_gate, ((1,), (1,))) + dot(up_grad, w_up, ((1,), (1,)))
    ).astype(BF16).reshape(4, tok_rows, width)
    normed_two_grad = scatter_four(normed_two_part[:2], normed_two_part[2:])
    feed_part = dot(hidden, w_down).astype(BF16).reshape(4, tok_rows, width)
    feed_out = scatter_four(feed_part[:2], feed_part[2:])
    result = ((middle + feed_out) * row_valid).astype(BF16)

    zigzag = list(range(bits))
    other = zigzag[1:2] + zigzag[:1] + zigzag[2:]
    split = lambda v: v.reshape((ctx_size, v.shape[0] // ctx_size) + v.shape[1:])
    join = lambda v: v.reshape((v.shape[0] * v.shape[1],) + v.shape[2:])
    gate_w_part = dot(ff_in, gate_grad, ((0,), (0,))).astype(BF16)
    up_w_part = dot(ff_in, up_grad, ((0,), (0,))).astype(BF16)
    down_part = dot(hidden, feed_grad, ((0,), (0,))).astype(BF16)
    gate_w_grad = join(sum_over_ctx(split(gate_w_part), zigzag)).astype(F32)
    down_grad = join(sum_over_ctx(split(down_part), other)).astype(F32)
    up_w_grad = join(sum_over_ctx(split(up_w_part), zigzag)).astype(F32)

    middle_grad = cotangent + norm_back(normed_two_grad, normed_two_raw, scale_two, gain_two_f)
    branch_grad = middle_grad.astype(BF16)
    da_t = dot(output_full, branch_grad, ((1,), (1,))).astype(BF16)
    dq_t, key_w_part, value_w_part, latent_terms = attention_backward(
        meta, q_t, da_t, key_full, value_full, blocks, mixture, log_total
    )
    latent_grad = ring_scatter(latent_terms, slots).astype(BF16)

    quarter = lambda v: v.reshape((4, v.shape[0] // 4) + v.shape[1:])
    output_part = quarter(dot(att_t, branch_grad).astype(BF16))
    output_shard = scatter_four(output_part[:2], output_part[2:])
    output_grad = join(sum_over_ctx(split(output_shard.astype(BF16)), zigzag)).astype(F32)
    query_part = quarter(dot(normed, dq_t, ((0,), (1,))).astype(BF16))
    query_shard = scatter_four(query_part[:2], query_part[2:])
    query_grad = join(sum_over_ctx(split(query_shard.astype(BF16)), other)).astype(F32)
    latent_w_part = dot(normed, latent_grad, ((0,), (0,))).astype(BF16)
    side_part = quarter(jnp.concatenate([latent_w_part, key_w_part, value_w_part], axis=1))
    side_shard = scatter_four(side_part[:2], side_part[2:])
    side_grad = join(sum_over_ctx(split(side_shard.astype(BF16)), zigzag)).astype(F32)
    lat_width = GRP * LAT
    latent_w_grad = side_grad[:, :lat_width]
    key_grad = side_grad[:, lat_width : lat_width + LAT]
    value_grad = side_grad[:, lat_width + LAT :]

    normed_grad = dot(dq_t, query_full, ((0,), (1,))) + dot(
        latent_grad, latent_full, ((1,), (1,))
    )
    input_grad = middle_grad + restore(
        norm_back(normed_grad, normed_one, scale_one, gain_one_f)
    )
    gain_one_grad = (
        jnp.sum(w_query.astype(F32) * query_grad, axis=1)
        + jnp.sum(w_latent.astype(F32) * latent_w_grad, axis=1)
    ) / norm1_gain.astype(F32)
    gain_two_part = jnp.sum(
        w_gate.astype(F32) * gate_w_grad + w_up.astype(F32) * up_w_grad, axis=1
    ).astype(BF16)
    gain_two_part = reorder(gain_two_part[None]).reshape(4, 1, piece)
    gain_two_grad = scatter_four(gain_two_part[:2], gain_two_part[2:])[0] / norm2_gain.astype(F32)
    return (
        result[None],
        input_grad[None],
        gain_one_grad,
        query_grad,
        latent_w_grad,
        key_grad,
        value_grad,
        output_grad,
        gain_two_grad,
        gate_w_grad,
        up_w_grad,
        down_grad,
    )


def solution(mesh):
    rows = P("fsdp", None)
    cols = P(None, "fsdp")
    toks = P("fsdp", "ctx", None)
    vec = P("fsdp")
    return jax.shard_map(
        on_device,
        mesh=mesh,
        in_specs=(toks, toks, rows, vec, rows, rows, rows, rows, rows, vec, cols, cols, rows),
        out_specs=(toks, toks, vec, rows, rows, rows, rows, rows, vec, cols, cols, rows),
        check_vma=False,
    )
```

```python
import functools

import jax
import jax.numpy as jnp
from jax import lax
from jax.experimental import pallas as pl
from jax.experimental.pallas import tpu as pltpu
from jax.sharding import PartitionSpec as P

NH = 16
HD = 64
LAT = 256
GRP = 2
SEQ_MAX = 4096
EPS = 1e-06
NEGATIVE = -1e30
HPG = NH // GRP
HB = 4
ORDER = (0, 2, 1, 3)
F32 = jnp.float32
BF16 = jnp.bfloat16


def dot(left, right, contract=((1,), (0,))):
    return lax.dot_general(left, right, (contract, ((), ())), preferred_element_type=F32)


def after(value, *tokens):
    return lax.optimization_barrier((value, tokens))[0]


def norm_scale(values):
    return lax.rsqrt(jnp.mean(values * values, axis=-1, keepdims=True) + EPS)


def norm_back(grad_in, normed, scale_rows, gain_full):
    scaled = grad_in * gain_full
    return scale_rows * (scaled - normed * jnp.mean(scaled * normed, axis=-1, keepdims=True))


def swap(value, axis, mask):
    size = lax.axis_size(axis)
    return lax.ppermute(value, axis, [(s, s ^ mask) for s in range(size)])


def gather_four(value):
    across = swap(value, "fsdp", 2)
    beside = swap(value, "fsdp", 1)
    both = swap(across, "fsdp", 1)
    return [value, across, beside, both]


def scatter_four(first_two, last_two):
    got = swap(last_two, "fsdp", 1)
    near = first_two.astype(F32) + got.astype(F32)
    far = swap(near[1].astype(BF16), "fsdp", 2)
    return near[0] + far.astype(F32)


def ring_members(count):
    return list(range(0, count, 2)) + list(range(count - 1, 0, -2)) if count > 1 else [0]


def ring_shift(value, slot_blocks, step):
    size = lax.axis_size("ctx")
    order = ring_members(slot_blocks)
    pairs = []
    for base in range(0, size, slot_blocks):
        for place in range(slot_blocks):
            pairs.append((base + order[place], base + order[(place + step) % slot_blocks]))
    return lax.ppermute(value, "ctx", pairs)


def ring_gather(block, slot_blocks):
    rows = block.shape[0]
    half = slot_blocks // 2
    out = [block]
    from_left, from_right = block, block
    for _ in range(half - 1):
        from_left = ring_shift(from_left, slot_blocks, 1)
        from_right = ring_shift(from_right, slot_blocks, -1)
        out += [from_left, from_right]
    top = ring_shift(from_left[: rows // 2], slot_blocks, 1)
    low = ring_shift(from_right[rows // 2 :], slot_blocks, -1)
    out.append(jnp.concatenate([top, low], axis=0))
    return out


def slot_code(rank, slots):
    bits = slots.bit_length() - 1
    code = 0
    for bit in range(bits):
        code = code | (((rank >> bit) & 1) << (bits - 1 - bit))
    return code


class SlotSum:
    def __init__(self, terms):
        self.terms, self.stage = terms, 0
        self.send()

    def send(self):
        half = self.terms.shape[0] // 2
        self.sent = self.terms[half:]
        self.got = swap(self.sent, "ctx", 1 << self.stage)

    def step(self, *tokens):
        got = after(self.got, *tokens) if tokens else self.got
        self.terms = plus(self.terms[: self.terms.shape[0] // 2], got)
        self.stage += 1
        if self.terms.shape[0] > 1:
            self.send()
        return self.sent

    def finish(self):
        while self.terms.shape[0] > 1:
            self.step()
        return self.terms[0]


def plus(*terms):
    total = terms[0].astype(F32)
    for term in terms[1:]:
        total = total + term.astype(F32)
    return total.astype(BF16)


class CtxSum:
    def __init__(self, parts, order, size):
        self.parts, self.order, self.size = parts, order, size
        self.stage, self.got = 0, []
        self.send(parts[0], order[0])

    def send(self, value, bit):
        self.sent = value
        self.got.append(swap(value, "ctx", 1 << bit))

    def step(self, *tokens):
        _, second, third, own = self.parts
        first_bit, second_bit, third_bit = self.order
        got = self.got
        if tokens:
            got[-1] = after(got[-1], *tokens)
        self.stage += 1
        if self.stage == 1:
            self.send(plus(second, got[0][2:]), second_bit)
        elif self.stage == 2:
            self.send(plus(third, got[0][1:2], got[1][1:]), third_bit)
        elif self.stage == 3:
            own = plus(own, got[0][:1], got[1][:1], got[2])
            for bit in range(self.size.bit_length() - 1):
                if bit not in self.order:
                    own = plus(own, swap(own, "ctx", 1 << bit))
            self.send(own, third_bit)
        elif self.stage == 4:
            self.send(jnp.concatenate([self.sent, got[3]], axis=0), second_bit)
        elif self.stage == 5:
            self.send(jnp.concatenate([self.sent, got[4]], axis=0), first_bit)
        return self.sent

    def finish(self):
        while self.stage < 5:
            self.step()
        return self.sent, self.got[5]


def code_of(rank, order):
    return (((rank >> order[0]) & 1) << 2) | (((rank >> order[1]) & 1) << 1) | ((rank >> order[2]) & 1)


def place_of(rank, slots):
    return jnp.where(rank % 2 == 0, rank // 2, slots - 1 - rank // 2)


def slot_of(rank, other, slots):
    if slots == 1:
        return 0
    ahead = lax.rem(place_of(other, slots) - place_of(rank, slots) + slots, slots)
    return jnp.where(ahead <= slots // 2, 2 * ahead - (ahead == slots // 2).astype(jnp.int32), 2 * (slots - ahead) - 1)


def score_mask(first_key, first_query, length, rows, width):
    key = first_key + lax.broadcasted_iota(jnp.int32, (rows, width), 0)
    query = first_query + lax.rem(lax.broadcasted_iota(jnp.int32, (rows, width), 1), rows)
    return (key <= query) & (key < length)


def forward_kernel(slots, meta, q_ref, wk_ref, wv_ref, c_ref, att_ref, ol_ref, lse_ref,
                   ct_ref, ql_ref, s_ref, m_ref, l_ref, acc_ref):
    rows = q_ref.shape[1]
    rank, length = meta[0], meta[1]
    first_query = rank * rows
    step = pl.program_id(0)
    active = first_query < length

    @pl.when(active & (step % (HPG // HB) == 0))
    def _():
        def turn(block, carry):
            slot = slot_of(rank, block, slots)
            ct_ref[block] = c_ref[slot].T
            return carry

        lax.fori_loop(0, rank + 1, turn, 0)

    m_ref[...] = jnp.full_like(m_ref, NEGATIVE)
    l_ref[...] = jnp.zeros_like(l_ref)
    acc_ref[...] = jnp.zeros_like(acc_ref)

    @pl.when(active)
    def _():
        for i in range(HB):
            part = pl.ds(i * HD, HD)
            latent_q = dot(wk_ref[part, :], q_ref[part, :], ((0,), (0,))).astype(BF16)
            ql_ref[:, i * rows : (i + 1) * rows] = latent_q * jnp.asarray(HD ** -0.5, BF16)
        queries = ql_ref[...]
        scores = dot(c_ref[0], queries)
        s_ref[0] = dot(c_ref[slot_of(rank, 0, slots)], queries)
        allowed = score_mask(first_query, first_query, length, rows, HB * rows)
        scores = jnp.where(allowed, scores, NEGATIVE)
        best = jnp.max(scores, axis=0, keepdims=True)
        weights = jnp.where(allowed, jnp.exp(scores - best), 0.0)
        m_ref[...] = best
        l_ref[...] = jnp.sum(weights, axis=0, keepdims=True)
        acc_ref[...] = dot(ct_ref[rank], weights.astype(BF16))

        def loop(block, carry):
            now = lax.rem(block, 2)
            later = jnp.minimum(block + 1, rank - 1)
            scores = s_ref[now]
            s_ref[1 - now] = dot(c_ref[slot_of(rank, later, slots)], ql_ref[...])
            best = jnp.maximum(m_ref[...], jnp.max(scores, axis=0, keepdims=True))
            weights = jnp.exp(scores - best)
            factor = jnp.exp(m_ref[...] - best)
            m_ref[...] = best
            l_ref[...] = l_ref[...] * factor + jnp.sum(weights, axis=0, keepdims=True)
            acc_ref[...] = acc_ref[...] * factor + dot(ct_ref[block], weights.astype(BF16))
            return carry

        lax.fori_loop(0, rank, loop, 0)

    total = l_ref[...]
    seen = total > 0.0
    safe = jnp.where(seen, total, 1.0)
    lse_all = jnp.where(seen, m_ref[...] + jnp.log(safe), 0.0)
    mixture = (acc_ref[...] * (1.0 / safe)).astype(BF16)
    for i in range(HB):
        part = pl.ds(i * HD, HD)
        cols = slice(i * rows, (i + 1) * rows)
        lse_ref[i] = lse_all[:, cols]
        ol_ref[i] = mixture[:, cols]
        att_ref[part, :] = dot(wv_ref[part, :], mixture[:, cols]).astype(BF16)


def backward_kernel(slots, last, meta, q_ref, da_ref, wk_ref, wv_ref, c_ref, ol_ref, lse_ref,
                    *rest):
    (dc_in, dq_ref, dwk_ref, dwv_ref, dc_ref,
     ct_ref, dc_acc, left_ref, both_ref, s_ref, dql_ref, lse_all, delta_ref) = rest if last else (None,) + rest
    rows = q_ref.shape[1]
    width = HB * rows
    rank, length = meta[0], meta[1]
    first_query = rank * rows
    scale = jnp.asarray(HD ** -0.5, BF16)
    active = first_query < length
    dc_acc[...] = dc_in[...] if last else jnp.zeros_like(dc_acc)

    @pl.when(active)
    def _():
        def turn(block, carry):
            slot = slot_of(rank, block, slots)
            ct_ref[block] = c_ref[slot].T
            return carry

        lax.fori_loop(0, rank + 1, turn, 0)

    dql_ref[...] = jnp.zeros_like(dql_ref)

    @pl.when(active)
    def _():
        for i in range(HB):
            part = pl.ds(i * HD, HD)
            cols = slice(i * rows, (i + 1) * rows)
            q_t, da_t, wk, wv = q_ref[part, :], da_ref[part, :], wk_ref[part, :], wv_ref[part, :]
            left_ref[:, cols] = dot(wk, q_t, ((0,), (0,))).astype(BF16) * scale
            both_ref[cols, :] = dot(q_t, wk, ((0,), (0,))).astype(BF16) * scale
            dol_t = dot(wv, da_t, ((0,), (0,))).astype(BF16)
            left_ref[:, width + i * rows : width + (i + 1) * rows] = dol_t
            both_ref[width + i * rows : width + (i + 1) * rows, :] = dot(da_t, wv, ((0,), (0,))).astype(BF16)
            delta_ref[:, cols] = jnp.sum(dol_t.astype(F32) * ol_ref[i].astype(F32), axis=0, keepdims=True)
            lse_all[:, cols] = lse_ref[i]

        def finish(block, pair, allowed):
            place = slot_code(rank, slots) ^ slot_code(block, slots)
            probs = jnp.exp(pair[:, :width] - lse_all[...])
            if allowed is not None:
                probs = jnp.where(allowed, probs, 0.0)
            score_grad = (probs * (pair[:, width:] - delta_ref[...])).astype(BF16)
            dql_ref[...] += dot(ct_ref[block], score_grad)
            dc_acc[place] += dot(score_grad, both_ref[:width, :]) + dot(probs.astype(BF16), both_ref[width:, :])

        pair = dot(c_ref[0], left_ref[...])
        s_ref[0] = dot(c_ref[slot_of(rank, 0, slots)], left_ref[...])
        finish(rank, pair, score_mask(first_query, first_query, length, rows, width))

        def loop(block, carry):
            now = lax.rem(block, 2)
            later = jnp.minimum(block + 1, rank - 1)
            pair = s_ref[now]
            s_ref[1 - now] = dot(c_ref[slot_of(rank, later, slots)], left_ref[...])
            finish(block, pair, None)
            return carry

        lax.fori_loop(0, rank, loop, 0)

    for i in range(HB):
        part = pl.ds(i * HD, HD)
        latent_grad = (dql_ref[:, i * rows : (i + 1) * rows] * (HD ** -0.5)).astype(BF16)
        dq_ref[part, :] = dot(wk_ref[part, :], latent_grad).astype(BF16)
        dwk_ref[part, :] = dot(q_ref[part, :], latent_grad, ((1,), (1,))).astype(BF16)
        dwv_ref[part, :] = dot(da_ref[part, :], ol_ref[i], ((1,), (1,))).astype(BF16)

    dc_ref[...] = dc_acc[...].astype(dc_ref.dtype)


def head_place(step, member):
    per_piece = NH // 4 // HB
    mask = (step // per_piece) ^ member
    return ((mask & 1) * 2 + (mask >> 1)) * per_piece + step % per_piece


def attention_forward(meta, q_t, wk, wv, blocks):
    slots, rows, _ = blocks.shape
    own = lambda s, meta: (s, 0)
    placed = lambda s, meta: (head_place(s, meta[2]), 0)
    width = HB * HD
    return pl.pallas_call(
        functools.partial(forward_kernel, slots),
        name="attention_forward",
        grid_spec=pltpu.PrefetchScalarGridSpec(
            num_scalar_prefetch=1,
            grid=(NH // HB,),
            in_specs=[
                pl.BlockSpec((width, rows), own),
                pl.BlockSpec((width, LAT), placed),
                pl.BlockSpec((width, LAT), placed),
                pl.BlockSpec((slots, rows, LAT), lambda s, meta: (0, 0, s // (HPG // HB))),
            ],
            out_specs=[
                pl.BlockSpec((width, rows), placed),
                pl.BlockSpec((HB, LAT, rows), lambda s, meta: (s, 0, 0)),
                pl.BlockSpec((HB, 1, rows), lambda s, meta: (s, 0, 0)),
            ],
            scratch_shapes=[
                pltpu.VMEM((slots, LAT, rows), BF16),
                pltpu.VMEM((LAT, HB * rows), BF16),
                pltpu.VMEM((2, rows, HB * rows), F32),
                pltpu.VMEM((1, HB * rows), F32),
                pltpu.VMEM((1, HB * rows), F32),
                pltpu.VMEM((LAT, HB * rows), F32),
            ],
        ),
        out_shape=[
            jax.ShapeDtypeStruct((NH * HD, rows), BF16),
            jax.ShapeDtypeStruct((NH, LAT, rows), BF16),
            jax.ShapeDtypeStruct((NH, 1, rows), F32),
        ],
        compiler_params=pltpu.CompilerParams(
            dimension_semantics=("arbitrary",), vmem_limit_bytes=32 << 20
        ),
    )(meta, q_t, wk, wv, blocks)


def attention_backward(part, meta, q_t, da_t, wk, wv, blocks, ol, lse, terms=None):
    slots, rows, _ = blocks.shape
    group = part * HB // HPG
    last = terms is not None
    own = lambda s, meta: (part, 0)
    placed = lambda s, meta: (head_place(part, meta[2]), 0)
    first = lambda s, meta: (0, 0)
    all_slots = lambda s, meta: (0, 0, 0)
    width = HB * HD
    return pl.pallas_call(
        functools.partial(backward_kernel, slots, last),
        name="attention_backward",
        grid_spec=pltpu.PrefetchScalarGridSpec(
            num_scalar_prefetch=1,
            grid=(1,),
            in_specs=[
                pl.BlockSpec((width, rows), own),
                pl.BlockSpec((width, rows), placed),
                pl.BlockSpec((width, LAT), placed),
                pl.BlockSpec((width, LAT), placed),
                pl.BlockSpec((slots, rows, LAT), lambda s, meta: (0, 0, group)),
                pl.BlockSpec((HB, LAT, rows), lambda s, meta: (part, 0, 0)),
                pl.BlockSpec((HB, 1, rows), lambda s, meta: (part, 0, 0)),
            ]
            + [pl.BlockSpec((slots, rows, LAT), all_slots)] * last,
            out_specs=[
                pl.BlockSpec((width, rows), first),
                pl.BlockSpec((width, LAT), first),
                pl.BlockSpec((width, LAT), first),
                pl.BlockSpec((slots, rows, LAT), all_slots),
            ],
            scratch_shapes=[
                pltpu.VMEM((slots, LAT, rows), BF16),
                pltpu.VMEM((slots, rows, LAT), F32),
                pltpu.VMEM((LAT, 2 * HB * rows), BF16),
                pltpu.VMEM((2 * HB * rows, LAT), BF16),
                pltpu.VMEM((2, rows, 2 * HB * rows), F32),
                pltpu.VMEM((LAT, HB * rows), F32),
                pltpu.VMEM((1, HB * rows), F32),
                pltpu.VMEM((1, HB * rows), F32),
            ],
        ),
        out_shape=[
            jax.ShapeDtypeStruct((width, rows), BF16),
            jax.ShapeDtypeStruct((width, LAT), BF16),
            jax.ShapeDtypeStruct((width, LAT), BF16),
            jax.ShapeDtypeStruct((slots, rows, LAT), BF16 if last else F32),
        ],
        compiler_params=pltpu.CompilerParams(
            dimension_semantics=("arbitrary",), vmem_limit_bytes=40 << 20
        ),
    )(meta, q_t, da_t, wk, wv, blocks, ol, lse, *([terms] if last else []))


def feed_kernel(h0, h1, h2, h3, df_ref, wg_ref, wu_ref, wd_ref,
                x_ref, hid_ref, dg_ref, du_ref, dh_ref, out_ref):
    for k, ref in enumerate((h0, h1, h2, h3)):

        @pl.when(pl.program_id(0) == k)
        def _():
            x_ref[...] = ref[...]

    rows = x_ref[...]
    gate = dot(wg_ref[...], rows, ((1,), (1,)))
    up = dot(wu_ref[...], rows, ((1,), (1,)))
    dhid = dot(wd_ref[...], df_ref[...], ((1,), (1,)))
    sig = jax.nn.sigmoid(gate)
    silu = gate * sig
    hid = (silu * up).astype(BF16)
    dgate = (dhid * up * sig * (1.0 + gate * (1.0 - sig))).astype(BF16)
    dup = (dhid * silu).astype(BF16)
    hid_ref[...] = hid
    dg_ref[...] = dgate
    du_ref[...] = dup
    dh_ref[0] = (dot(dgate, wg_ref[...], ((0,), (0,))) + dot(dup, wu_ref[...], ((0,), (0,)))).astype(BF16)
    out_ref[0] = dot(hid, wd_ref[...], ((0,), (0,))).astype(BF16)


def feed_forward(pieces, df, w_gate, w_up, w_down):
    rows, width = pieces[0].shape
    ff = w_gate.shape[0]
    whole = lambda t: (0, 0)
    part = lambda t: (t, 0)
    return pl.pallas_call(
        feed_kernel,
        name="feed_forward",
        grid=(4,),
        in_specs=[pl.BlockSpec((rows, width), whole)] * 4
        + [pl.BlockSpec((rows, width), part)]
        + [pl.BlockSpec((ff, width), whole)] * 3,
        out_specs=[pl.BlockSpec((rows, width), part)]
        + [pl.BlockSpec((ff, rows), lambda t: (0, t))] * 3
        + [pl.BlockSpec((1, rows, width), lambda t: (t, 0, 0))] * 2,
        out_shape=[jax.ShapeDtypeStruct((4 * rows, width), BF16)]
        + [jax.ShapeDtypeStruct((ff, 4 * rows), BF16)] * 3
        + [jax.ShapeDtypeStruct((4, rows, width), BF16)] * 2,
        compiler_params=pltpu.CompilerParams(
            dimension_semantics=("arbitrary",), vmem_limit_bytes=40 << 20
        ),
    )(*pieces, df, w_gate, w_up, w_down)


def feed_grad_kernel(count, which, codes, right_ref, *rest):
    pair = 3 - pl.program_id(0)
    swapped = (codes[which] & 1) == 1
    cut = right_ref.shape[1] // 2
    for i in range(count):
        first, second, third, own = rest[count + 4 * i : count + 4 * i + 4]
        both = dot(rest[i][...], right_ref[...]).astype(BF16)
        low = jnp.where(swapped, both[:, cut:], both[:, :cut])
        high = jnp.where(swapped, both[:, :cut], both[:, cut:])

        @pl.when(pair >= 2)
        def _():
            first[0] = low
            first[1] = high

        @pl.when(pair == 1)
        def _():
            second[0] = low
            second[1] = high

        @pl.when(pair == 0)
        def _():
            own[0] = low
            third[0] = high


def feed_weight_grads(which, codes, lefts, right):
    ff, rows = lefts[0].shape
    cut = right.shape[1] // 8
    count = len(lefts)
    one = lambda s, codes: (0, 0, 0)
    specs = [
        pl.BlockSpec((2, ff, cut), lambda s, codes: (jnp.maximum(1 - s, 0), 0, 0)),
        pl.BlockSpec((2, ff, cut), one),
        pl.BlockSpec((1, ff, cut), one),
        pl.BlockSpec((1, ff, cut), one),
    ]
    shapes = [jax.ShapeDtypeStruct((n, ff, cut), BF16) for n in (4, 2, 1, 1)]
    out = pl.pallas_call(
        functools.partial(feed_grad_kernel, count, which),
        name="feed_weight_grads",
        grid_spec=pltpu.PrefetchScalarGridSpec(
            num_scalar_prefetch=1,
            grid=(4,),
            in_specs=[pl.BlockSpec((rows, 2 * cut), lambda s, codes: (0, (3 - s) ^ (codes[which] >> 1)))]
            + [pl.BlockSpec((ff, rows), lambda s, codes: (0, 0))] * count,
            out_specs=specs * count,
        ),
        out_shape=shapes * count,
        compiler_params=pltpu.CompilerParams(
            dimension_semantics=("arbitrary",), vmem_limit_bytes=40 << 20
        ),
    )(codes, right, *lefts)
    return [out[4 * i : 4 * i + 4] for i in range(count)]


def join_kernel(which, by_rows, cuts, codes, near_ref, far_ref, *outs):
    _, tall, wide = near_ref.shape
    for i in range(8):
        position = i ^ codes[which]
        place = position & 3
        piece = jnp.where(position >= 4, far_ref[place].astype(F32), near_ref[place].astype(F32))
        if by_rows:
            low = 0
            for out, cut in zip(outs, cuts):
                out[i * tall : (i + 1) * tall, :] = piece[:, low : low + cut]
                low += cut
        else:
            outs[0][:, i * wide : (i + 1) * wide] = piece


def join(which, codes, near, far, cuts=None):
    _, tall, wide = near.shape
    vmem = pl.BlockSpec(memory_space=pltpu.VMEM)
    if cuts:
        shapes = [jax.ShapeDtypeStruct((8 * tall, cut), F32) for cut in cuts]
    else:
        shapes = [jax.ShapeDtypeStruct((tall, 8 * wide), F32)]
    return pl.pallas_call(
        functools.partial(join_kernel, which, bool(cuts), cuts),
        name="join_pieces",
        in_specs=[pl.BlockSpec(memory_space=pltpu.SMEM), vmem, vmem],
        out_specs=[vmem] * len(shapes),
        out_shape=shapes,
        compiler_params=pltpu.CompilerParams(vmem_limit_bytes=32 << 20),
    )(codes, near, far)


def spread_kernel(which, cut, contract, codes, left_ref, right_ref, last_ref, next_ref, own_ref, acc_ref):
    acc_ref[...] = dot(left_ref[...], right_ref[...], contract)
    for t in range(4):
        for position in range(8):
            start = t * 8 * cut + (position ^ codes[which]) * cut
            value = acc_ref[pl.ds(pl.multiple_of(start, cut), cut), :].astype(BF16)
            if t >= 2:
                last_ref[t - 2, position] = value
            elif t == 1:
                next_ref[position] = value
            else:
                own_ref[position] = value


def spread_product(which, codes, left, right, contract):
    tall, wide = left.shape[1 - contract[0][0]], right.shape[1 - contract[1][0]]
    cut = tall // 32
    vmem = pl.BlockSpec(memory_space=pltpu.VMEM)
    return pl.pallas_call(
        functools.partial(spread_kernel, which, cut, contract),
        name="spread_product",
        in_specs=[pl.BlockSpec(memory_space=pltpu.SMEM), vmem, vmem],
        out_specs=[vmem] * 3,
        scratch_shapes=[pltpu.VMEM((tall, wide), F32)],
        out_shape=[
            jax.ShapeDtypeStruct((2, 8, cut, wide), BF16),
            jax.ShapeDtypeStruct((8, cut, wide), BF16),
            jax.ShapeDtypeStruct((8, cut, wide), BF16),
        ],
        compiler_params=pltpu.CompilerParams(vmem_limit_bytes=32 << 20),
    )(codes, left, right)


def reduce_shards(last, near, own):
    beside = swap(last, "fsdp", 1)
    across = swap(plus(near, beside[1]), "fsdp", 2)
    return lambda low, high: plus(own[low:high], beside[0, low:high], across[low:high])


def four_parts(part):
    return part(4, 8), part(2, 4), part(1, 2), part(0, 1)


def on_device(
    tokens,
    out_grad,
    lengths,
    norm1_gain,
    w_query,
    w_latent,
    w_key_up,
    w_value_up,
    w_output,
    norm2_gain,
    w_gate,
    w_up,
    w_down,
):
    ctx_size = lax.axis_size("ctx")
    tok_rows, width = tokens.shape[1], tokens.shape[2]
    ff = w_gate.shape[1]
    group_rows = tok_rows * ctx_size
    seq_rows = min(SEQ_MAX, group_rows)
    slots = seq_rows // tok_rows
    ctx_rank = lax.axis_index("ctx")
    member = lax.axis_index("fsdp")
    slot_number = ctx_rank // slots
    rank = ctx_rank % slots
    length = jnp.sum(
        jnp.where(jnp.arange(lengths.shape[1], dtype=jnp.int32) == slot_number, lengths[0], 0)
    )
    meta = jnp.stack([rank, length, member]).astype(jnp.int32)
    query_pos = rank * tok_rows + jnp.arange(tok_rows, dtype=jnp.int32)
    row_valid = (query_pos < length).astype(F32)[:, None]
    piece = width // 4
    order_a, order_b = (0, 1, 2), (1, 0, 2)
    codes = jnp.stack([code_of(ctx_rank, order_a), code_of(ctx_rank, order_b)]).astype(jnp.int32)

    def reorder(value):
        return jnp.concatenate(
            [lax.dynamic_slice_in_dim(value, (member ^ m) * piece, piece, 1) for m in ORDER], axis=1
        )

    def restore(value):
        back = {m: t for t, m in enumerate(ORDER)}
        parts = [value[:, back[m] * piece : (back[m] + 1) * piece] for m in range(4)]
        low = (member & 1) == 1
        parts = [jnp.where(low, parts[j ^ 1], parts[j]) for j in range(4)]
        high = (member & 2) == 2
        parts = [jnp.where(high, parts[j ^ 2], parts[j]) for j in range(4)]
        return jnp.concatenate(parts, axis=1)

    gains = jnp.stack([norm1_gain, norm2_gain])
    gain_pieces = gather_four(gains)
    latent_pieces = gather_four(w_latent)
    gate_order = lax.optimization_barrier((latent_pieces[1], w_query, w_key_up, w_value_up))
    latent_pieces[1] = gate_order[0]
    query_pieces = gather_four(gate_order[1])
    side = jnp.concatenate([gate_order[2], gate_order[3]], axis=1)
    side_pieces = gather_four(side)
    gate_order = lax.optimization_barrier((query_pieces[1], side_pieces[1], w_output))
    query_pieces[1], side_pieces[1] = gate_order[0], gate_order[1]
    output_pieces = gather_four(gate_order[2])
    cotangent = out_grad[0].astype(F32) * row_valid
    gate_order = lax.optimization_barrier((output_pieces[1], cotangent.astype(BF16)))
    output_pieces[1] = gate_order[0]
    feed_grad = jnp.concatenate(gather_four(gate_order[1]), axis=0)

    gain_one = jnp.concatenate([g[0] for g in gain_pieces])
    gain_two = restore(jnp.concatenate([g[1:] for g in gain_pieces], axis=1))
    gain_one_f = gain_one.astype(F32)
    gain_two_f = gain_two.astype(F32)
    query_full = jnp.concatenate(query_pieces, axis=0)
    latent_full = jnp.concatenate(latent_pieces, axis=0)
    side_full = jnp.concatenate(side_pieces, axis=0)
    key_full, value_full = side_full[:, :LAT], side_full[:, LAT:]
    output_full = jnp.concatenate(output_pieces, axis=0)

    inputs = tokens[0].astype(F32)
    mixed = reorder(tokens[0]).astype(F32)
    scale_one = norm_scale(inputs)
    normed_one = mixed * scale_one
    normed = (normed_one * gain_one_f).astype(BF16)
    latent = dot(normed, latent_full).astype(BF16)
    blocks = jnp.stack(ring_gather(latent, slots))
    q_t = dot(query_full, normed, ((0,), (1,))).astype(BF16)
    att_t, mixture, log_total = attention_forward(meta, q_t, key_full, value_full, blocks)
    middle = inputs + dot(att_t, output_full, ((0,), (0,)))
    scale_two = norm_scale(middle)
    normed_two_raw = middle * scale_two
    normed_two = (normed_two_raw * gain_two_f).astype(BF16)
    gate_rows, up_rows = w_gate.T, w_up.T
    ff_in, hidden, gate_grad, up_grad, normed_two_part, feed_part = feed_forward(
        gather_four(normed_two), feed_grad, gate_rows, up_rows, w_down
    )
    beside = swap(normed_two_part[2:], "fsdp", 1)
    down_parts = feed_weight_grads(1, codes, [hidden], feed_grad)[0]
    home = plus(normed_two_part[1], beside[1])
    across = swap(home, "fsdp", 2)
    down_sum = CtxSum(down_parts, order_b, ctx_size)
    gate_parts, up_parts = feed_weight_grads(0, codes, [gate_grad, up_grad], after(ff_in, home, down_parts[0]))
    gate_sum = CtxSum(gate_parts, order_a, ctx_size)
    normed_two_grad = (
        normed_two_part[0].astype(F32) + beside[0].astype(F32) + after(across, gate_parts[3]).astype(F32)
    )
    middle_grad = cotangent + norm_back(normed_two_grad, normed_two_raw, scale_two, gain_two_f)
    branch_grad = middle_grad.astype(BF16)
    da_t = dot(output_full, branch_grad, ((1,), (1,))).astype(BF16)

    def back(part, terms, *tokens):
        return attention_backward(
            part, meta, q_t, after(da_t, *tokens), key_full, value_full, blocks, mixture, log_total, terms
        )

    nn, tn = ((1,), (0,)), ((0,), (0,))
    back_0 = back(0, None, gate_sum.sent)
    token = back_0[0]
    output_spread = spread_product(1, codes, att_t, after(branch_grad, token), nn)
    token = output_spread[2]
    gates = [down_sum.step(token), gate_sum.step(token)]
    up_parts = after(up_parts, gates[1])
    up_sum = CtxSum(up_parts, order_a, ctx_size)
    back_1 = back(1, back_0[3], up_parts[0], *gates)
    token = back_1[0]
    gates = [down_sum.step(token), gate_sum.step(token), up_sum.step(token)]
    output_sum = reduce_shards(*after(tuple(output_spread), token))
    sum_0 = SlotSum(back_1[3])
    back_2 = back(2, None, sum_0.sent, *gates)
    token = back_2[0]
    gates = [down_sum.step(token), gate_sum.step(token), up_sum.step(token), sum_0.step(token)]
    back_3 = back(3, back_2[3], *gates)
    token = back_3[0]
    sum_0.step(token)
    latent_0 = sum_0.finish()
    latent_1 = SlotSum(back_3[3]).finish()
    down_sum.step(token), gate_sum.step(token), up_sum.step(token)
    feed_part = after(feed_part, token)
    feed_out = scatter_four(feed_part[:2], feed_part[2:])
    backward = [back_0, back_1, back_2, back_3]
    result = ((middle + feed_out) * row_valid).astype(BF16)
    latent_grad = jnp.concatenate([latent_0, latent_1], axis=1)
    dq_t = jnp.concatenate([part[0] for part in backward], axis=0)
    query_sum = reduce_shards(*spread_product(1, codes, normed, dq_t, ((0,), (1,))))

    far_side, odd = (member & 2) == 2, (member & 1) == 1
    sides = [jnp.concatenate([part[1], part[2]], axis=1) for part in backward]
    sides = [jnp.where(odd, sides[p ^ 1], sides[p]) for p in range(4)]
    sides = [jnp.where(far_side, sides[p ^ 2], sides[p]) for p in range(4)]
    side = scatter_four(jnp.stack([sides[0], sides[2]]), jnp.stack([sides[1], sides[3]])).astype(BF16)
    side = side.reshape(8, NH * HD // 32, 2 * LAT)
    side_cuts = [lax.dynamic_slice_in_dim(side, p ^ codes[1], 1, 0) for p in range(8)]

    def mixed(low, high):
        own_side = jnp.concatenate(side_cuts[low:high], axis=0)
        return jnp.concatenate([output_sum(low, high), query_sum(low, high), own_side], axis=2)

    mixed_sum = CtxSum(four_parts(mixed), order_b, ctx_size)
    latent_sum = CtxSum(
        four_parts(reduce_shards(*spread_product(0, codes, normed, latent_grad, tn))), order_a, ctx_size
    )
    (gate_w_grad,) = join(0, codes, *gate_sum.finish())
    (up_w_grad,) = join(0, codes, *up_sum.finish())
    (down_grad,) = join(1, codes, *down_sum.finish())
    output_grad, query_grad, key_grad, value_grad = join(
        1, codes, *mixed_sum.finish(), (width, NH * HD, LAT, LAT)
    )
    (latent_w_grad,) = join(0, codes, *latent_sum.finish(), (GRP * LAT,))

    normed_grad = dot(dq_t, query_full, ((0,), (1,))) + dot(
        latent_grad, latent_full, ((1,), (1,))
    )
    input_grad = middle_grad + restore(
        norm_back(normed_grad, normed_one, scale_one, gain_one_f)
    )
    gain_one_grad = (
        jnp.sum(w_query.astype(F32) * query_grad, axis=1)
        + jnp.sum(w_latent.astype(F32) * latent_w_grad, axis=1)
    ) / norm1_gain.astype(F32)
    gain_two_part = jnp.sum(
        gate_rows.astype(F32) * gate_w_grad + up_rows.astype(F32) * up_w_grad, axis=0
    ).astype(BF16)
    gain_two_part = reorder(gain_two_part[None]).reshape(4, 1, piece)
    gain_two_grad = scatter_four(gain_two_part[:2], gain_two_part[2:])[0] / norm2_gain.astype(F32)
    return (
        result[None],
        input_grad[None],
        gain_one_grad,
        query_grad,
        latent_w_grad,
        key_grad,
        value_grad,
        output_grad,
        gain_two_grad,
        gate_w_grad.T,
        up_w_grad.T,
        down_grad,
    )


def solution(mesh):
    rows = P("fsdp", None)
    cols = P(None, "fsdp")
    toks = P("fsdp", "ctx", None)
    vec = P("fsdp")
    return jax.shard_map(
        on_device,
        mesh=mesh,
        in_specs=(toks, toks, rows, vec, rows, rows, rows, rows, rows, vec, cols, cols, rows),
        out_specs=(toks, toks, vec, rows, rows, rows, rows, rows, vec, cols, cols, rows),
        check_vma=False,
    )
```

```python
import functools

import jax
import jax.numpy as jnp
from jax import lax
from jax.experimental import pallas as pl
from jax.experimental.pallas import tpu as pltpu
from jax.sharding import PartitionSpec as P

NH = 16
HD = 64
LAT = 256
GRP = 2
SEQ_MAX = 4096
EPS = 1e-06
NEGATIVE = -1e30
HPG = NH // GRP
HB = 4
ORDER = (0, 2, 1, 3)
F32 = jnp.float32
BF16 = jnp.bfloat16


def dot(left, right, contract=((1,), (0,))):
    return lax.dot_general(left, right, (contract, ((), ())), preferred_element_type=F32)


def after(value, *tokens):
    return lax.optimization_barrier((value, tokens))[0]


def norm_scale(values):
    return lax.rsqrt(jnp.mean(values * values, axis=-1, keepdims=True) + EPS)


def norm_back(grad_in, normed, scale_rows, gain_full):
    scaled = grad_in * gain_full
    return scale_rows * (scaled - normed * jnp.mean(scaled * normed, axis=-1, keepdims=True))


def swap(value, axis, mask):
    size = lax.axis_size(axis)
    return lax.ppermute(value, axis, [(s, s ^ mask) for s in range(size)])


def gather_four(value, *tokens):
    across = swap(value, "fsdp", 2)
    beside = swap(value, "fsdp", 1)
    if tokens:
        across, beside = after((across, beside), *tokens)
    both = swap(across, "fsdp", 1)
    return [value, across, beside, both]


def gather_rows(value, *tokens):
    across = swap(value, "fsdp", 2)
    two = jnp.concatenate([value, after(across, *tokens) if tokens else across], axis=0)
    return jnp.concatenate([two, swap(two, "fsdp", 1)], axis=0)


def scatter_four(first_two, last_two):
    got = swap(last_two, "fsdp", 1)
    near = first_two.astype(F32) + got.astype(F32)
    far = swap(near[1].astype(BF16), "fsdp", 2)
    return near[0] + far.astype(F32)


def ring_members(count):
    return list(range(0, count, 2)) + list(range(count - 1, 0, -2)) if count > 1 else [0]


def ring_shift(value, slot_blocks, step):
    size = lax.axis_size("ctx")
    order = ring_members(slot_blocks)
    pairs = []
    for base in range(0, size, slot_blocks):
        for place in range(slot_blocks):
            pairs.append((base + order[place], base + order[(place + step) % slot_blocks]))
    return lax.ppermute(value, "ctx", pairs)


def ring_step(left, right, slots):
    return ring_shift(left, slots, 1), ring_shift(right, slots, -1)


def ring_last(left, right, slots):
    rows = left.shape[0]
    top, low = ring_step(left[: rows // 2], right[rows // 2 :], slots)
    return top, low


def slot_code(rank, slots):
    bits = slots.bit_length() - 1
    code = 0
    for bit in range(bits):
        code = code | (((rank >> bit) & 1) << (bits - 1 - bit))
    return code


class SlotSum:
    def __init__(self, *terms):
        self.terms, self.stage = terms, 0
        self.send()

    def send(self):
        self.half = self.terms[0].shape[0] // 2
        self.sent = plus(*[term[self.half :] for term in self.terms])
        self.got = swap(self.sent, "ctx", 1 << self.stage)

    def step(self, *tokens):
        got = after(self.got, *tokens) if tokens else self.got
        self.terms = [term[: self.half] for term in self.terms] + [got]
        self.stage += 1
        if self.half > 1:
            self.send()
        return self.sent

    def finish(self):
        while self.half > 1:
            self.step()
        self.step()
        return plus(*[term[0] for term in self.terms])


def plus_wide(*terms):
    total = terms[0].astype(F32)
    for term in terms[1:]:
        total = total + term.astype(F32)
    return total


def plus(*terms):
    return plus_wide(*terms).astype(BF16)


class CtxSum:
    def __init__(self, parts, order, size):
        self.parts, self.order, self.size = parts, order, size
        self.stage, self.got, self.sent = 0, [], parts[0]
        self.give()

    def give(self, *tokens):
        if tokens:
            self.sent = after(self.sent, *tokens)
        bits = self.order + self.order[::-1]
        self.got.append(swap(self.sent, "ctx", 1 << bits[self.stage]))
        return self.sent

    def take(self, *tokens):
        _, second, third, own = self.parts
        got = self.got
        if tokens:
            got[-1] = after(got[-1], *tokens)
        self.stage += 1
        if self.stage == 1:
            self.sent = plus(second, got[0][2:])
        elif self.stage == 2:
            self.sent = plus(third, got[0][1:2], got[1][1:])
        elif self.stage == 3:
            own = plus(own, got[0][:1], got[1][:1], got[2])
            for bit in range(self.size.bit_length() - 1):
                if bit not in self.order:
                    own = plus(own, swap(own, "ctx", 1 << bit))
            self.sent = own
        else:
            self.sent = jnp.concatenate([self.sent, got[-1]], axis=0)
        return self.sent

    def step(self, *tokens):
        self.take(*tokens)
        return self.give()

    def finish(self):
        while self.stage < 5:
            self.step()
        return self.sent, self.got[5]


def code_of(rank, order):
    return (((rank >> order[0]) & 1) << 2) | (((rank >> order[1]) & 1) << 1) | ((rank >> order[2]) & 1)


def place_of(rank, slots):
    return jnp.where(rank % 2 == 0, rank // 2, slots - 1 - rank // 2)


def slot_of(rank, other, slots):
    if slots == 1:
        return 0
    ahead = lax.rem(place_of(other, slots) - place_of(rank, slots) + slots, slots)
    return jnp.where(ahead <= slots // 2, 2 * ahead - (ahead == slots // 2).astype(jnp.int32), 2 * (slots - ahead) - 1)


def score_mask(first_key, first_query, length, rows, width):
    key = first_key + lax.broadcasted_iota(jnp.int32, (rows, width), 0)
    query = first_query + lax.rem(lax.broadcasted_iota(jnp.int32, (rows, width), 1), rows)
    return (key <= query) & (key < length)


def head_row(head, member):
    mask = (head // (NH // 4)) ^ member
    return (((mask & 1) * 2 + (mask >> 1)) * (NH // 4) + head % (NH // 4)) * HD


def other_of(rank, slot, slots):
    step = (slot + 1) // 2
    place = lax.rem(place_of(rank, slots) + (slots - step if slot % 2 else step), slots)
    return jnp.where(place < slots // 2, 2 * place, 2 * (slots - 1 - place) + 1)


def forward_kernel(slots, here, first, last, meta, q_ref, wk_ref, wv_ref, *rest):
    c_refs, rest = rest[: len(here)], rest[len(here) :]
    ins, rest = ((), rest) if first else (rest[:3], rest[3:])
    outs, rest = rest[:3], rest[3:]
    c_ref, ct_ref, ql_ref, m_ref, l_ref, acc_ref, index_ref = rest
    rows = q_ref.shape[1]
    rank, length, member = meta[0], meta[1], meta[2]
    group = pl.program_id(0)
    first_query = rank * rows
    active = first_query < length
    count = jnp.int32(0)
    for k, slot in enumerate(here):
        if slot == 0:
            need = active
        else:
            other = other_of(rank, slot, slots)
            need = active & (other < rank)
            index_ref[count] = jnp.int32(k)
            count = count + need.astype(jnp.int32)

        @pl.when(need)
        def _():
            block = c_refs[k][...]
            c_ref[k] = block
            ct_ref[k] = block.T

    if first:
        m_ref[...] = jnp.full_like(m_ref, NEGATIVE)
        l_ref[...] = jnp.zeros_like(l_ref)
        acc_ref[...] = jnp.zeros_like(acc_ref)
    else:
        m_ref[...] = ins[0][0]
        l_ref[...] = ins[1][0]
        acc_ref[...] = ins[2][0]

    @pl.when(active)
    def _():
        for i in range(HPG):
            part = pl.ds(i * HD, HD)
            row = pl.ds(pl.multiple_of(head_row(group * HPG + i, member), HD), HD)
            latent_q = dot(wk_ref[row, :], q_ref[part, :], ((0,), (0,))).astype(BF16)
            ql_ref[:, i * rows : (i + 1) * rows] = latent_q * jnp.asarray(HD ** -0.5, BF16)
        if first:
            scores = dot(c_ref[0], ql_ref[...])
            allowed = score_mask(first_query, first_query, length, rows, HPG * rows)
            scores = jnp.where(allowed, scores, NEGATIVE)
            best = jnp.max(scores, axis=0, keepdims=True)
            weights = jnp.where(allowed, jnp.exp(scores - best), 0.0)
            m_ref[...] = best
            l_ref[...] = jnp.sum(weights, axis=0, keepdims=True)
            acc_ref[...] = dot(ct_ref[0], weights.astype(BF16))

        def blocks(*which):
            scores = [dot(c_ref[k], ql_ref[...]) for k in which]
            best = m_ref[...]
            for each in scores:
                best = jnp.maximum(best, jnp.max(each, axis=0, keepdims=True))
            factor = jnp.exp(m_ref[...] - best)
            total = l_ref[...] * factor
            added = None
            for k, each in zip(which, scores):
                weights = jnp.exp(each - best)
                total = total + jnp.sum(weights, axis=0, keepdims=True)
                term = dot(ct_ref[k], weights.astype(BF16))
                added = term if added is None else added + term
            m_ref[...] = best
            l_ref[...] = total
            acc_ref[...] = acc_ref[...] * factor + added

        def loop(step, carry):
            blocks(index_ref[2 * step], index_ref[2 * step + 1])
            return carry

        lax.fori_loop(0, count // 2, loop, 0)

        @pl.when(count % 2 == 1)
        def _():
            blocks(index_ref[count - 1])

    if not last:
        outs[0][0] = m_ref[...]
        outs[1][0] = l_ref[...]
        outs[2][0] = acc_ref[...]
        return
    att_ref, ol_ref, lse_ref = outs
    total = l_ref[...]
    seen = total > 0.0
    safe = jnp.where(seen, total, 1.0)
    lse_all = jnp.where(seen, m_ref[...] + jnp.log(safe), 0.0)
    mixture = (acc_ref[...] * (1.0 / safe)).astype(BF16)
    for i in range(HPG):
        row = pl.ds(pl.multiple_of(head_row(group * HPG + i, member), HD), HD)
        cols = slice(i * rows, (i + 1) * rows)
        lse_ref[i] = lse_all[:, cols]
        ol_ref[i] = mixture[:, cols]
        att_ref[row, :] = dot(wv_ref[row, :], mixture[:, cols]).astype(BF16)


def backward_kernel(slots, meta, q_ref, da_ref, wk_ref, wv_ref, c_ref, ol_ref, lse_ref,
                    dq_ref, dwk_ref, dwv_ref, dc_ref,
                    ct_ref, left_ref, dql_ref, lse_all, delta_ref):
    rows = q_ref.shape[1]
    width = HB * rows
    rank, length = meta[0], meta[1]
    first_query = rank * rows
    scale = jnp.asarray(HD ** -0.5, BF16)
    active = first_query < length
    place_of_block = lambda block: slot_code(rank, slots) ^ slot_code(block, slots)

    def clear(block, carry):
        dc_ref[place_of_block(block)] = jnp.zeros((rows, LAT), BF16)
        return carry

    lax.fori_loop(jnp.where(active, rank + 1, 0), slots, clear, 0)

    @pl.when(jnp.logical_not(active))
    def _():
        dql_ref[...] = jnp.zeros_like(dql_ref)

    @pl.when(active)
    def _():
        def turn(block, carry):
            ct_ref[block] = c_ref[slot_of(rank, block, slots)].T
            return carry

        lax.fori_loop(0, rank + 1, turn, 0)
        for i in range(HB):
            part = pl.ds(i * HD, HD)
            cols = slice(i * rows, (i + 1) * rows)
            left_ref[:, cols] = dot(wk_ref[part, :], q_ref[part, :], ((0,), (0,))).astype(BF16) * scale
            dol_t = dot(wv_ref[part, :], da_ref[part, :], ((0,), (0,))).astype(BF16)
            left_ref[:, width + i * rows : width + (i + 1) * rows] = dol_t
            delta_ref[:, cols] = jnp.sum(dol_t.astype(F32) * ol_ref[i].astype(F32), axis=0, keepdims=True)
            lse_all[:, cols] = lse_ref[i]

        def grads(block, allowed):
            pair = dot(c_ref[slot_of(rank, block, slots)], left_ref[...])
            probs = jnp.exp(pair[:, :width] - lse_all[...])
            if allowed is not None:
                probs = jnp.where(allowed, probs, 0.0)
            score_grad = (probs * (pair[:, width:] - delta_ref[...])).astype(BF16)
            both = ((1,), (1,))
            dc_ref[place_of_block(block)] = (
                dot(score_grad, left_ref[:, :width], both) + dot(probs.astype(BF16), left_ref[:, width:], both)
            ).astype(BF16)
            return dot(ct_ref[block], score_grad)

        dql_ref[...] = grads(rank, score_mask(first_query, first_query, length, rows, width))

        def loop(step, carry):
            dql_ref[...] += grads(2 * step, None) + grads(2 * step + 1, None)
            return carry

        lax.fori_loop(0, rank // 2, loop, 0)

        @pl.when(rank % 2 == 1)
        def _():
            dql_ref[...] += grads(rank - 1, None)

    for i in range(HB):
        part = pl.ds(i * HD, HD)
        latent_grad = (dql_ref[:, i * rows : (i + 1) * rows] * (HD ** -0.5)).astype(BF16)
        dq_ref[part, :] = dot(wk_ref[part, :], latent_grad).astype(BF16)
        dwk_ref[part, :] = dot(q_ref[part, :], latent_grad, ((1,), (1,))).astype(BF16)
        dwv_ref[part, :] = dot(da_ref[part, :], ol_ref[i], ((1,), (1,))).astype(BF16)


def outside(value):
    return pltpu.with_memory_space_constraint(value, pltpu.HBM)


def once(shape, index):
    return pl.BlockSpec(shape, index, pipeline_mode=pl.Buffered(1))


def head_place(step, member):
    per_piece = NH // 4 // HB
    mask = (step // per_piece) ^ member
    return ((mask & 1) * 2 + (mask >> 1)) * per_piece + step % per_piece


def attention_forward(meta, q_t, wk, wv, pieces, here, slots, state=None, last=True):
    rows = q_t.shape[1]
    first = state is None
    wide = HPG * rows
    by_group = lambda g, meta: (g, 0, 0)
    if last:
        out_specs = [
            pl.BlockSpec((NH * HD, rows), lambda g, meta: (0, 0)),
            pl.BlockSpec((HPG, LAT, rows), by_group),
            pl.BlockSpec((HPG, 1, rows), by_group),
        ]
        out_shape = [
            jax.ShapeDtypeStruct((NH * HD, rows), BF16),
            pltpu.HBM((NH, LAT, rows), BF16),
            jax.ShapeDtypeStruct((NH, 1, rows), F32),
        ]
    else:
        out_specs = [pl.BlockSpec((1, n, wide), by_group) for n in (1, 1, LAT)]
        out_shape = [jax.ShapeDtypeStruct((GRP, n, wide), F32) for n in (1, 1, LAT)]
    return pl.pallas_call(
        functools.partial(forward_kernel, slots, here, first, last),
        name="attention_forward",
        grid_spec=pltpu.PrefetchScalarGridSpec(
            num_scalar_prefetch=1,
            grid=(GRP,),
            in_specs=[
                pl.BlockSpec((HPG * HD, rows), lambda g, meta: (g, 0)),
                once((NH * HD, LAT), lambda g, meta: (0, 0)),
                once((NH * HD, LAT), lambda g, meta: (0, 0)),
            ]
            + [pl.BlockSpec((rows, LAT), lambda g, meta: (0, g))] * len(here)
            + ([] if first else [pl.BlockSpec((1, n, wide), by_group) for n in (1, 1, LAT)]),
            out_specs=out_specs,
            scratch_shapes=[
                pltpu.VMEM((len(here), rows, LAT), BF16),
                pltpu.VMEM((len(here), LAT, rows), BF16),
                pltpu.VMEM((LAT, wide), BF16),
                pltpu.VMEM((1, wide), F32),
                pltpu.VMEM((1, wide), F32),
                pltpu.VMEM((LAT, wide), F32),
                pltpu.SMEM((len(here) + 1,), jnp.int32),
            ],
        ),
        out_shape=out_shape,
        compiler_params=pltpu.CompilerParams(
            dimension_semantics=("arbitrary",), vmem_limit_bytes=32 << 20
        ),
    )(meta, q_t, wk, wv, *pieces, *(state or ()))


def attention_backward(part, meta, q_t, da_t, wk, wv, blocks, ol, lse):
    slots, rows, _ = blocks.shape
    group = part * HB // HPG
    own = lambda s, meta: (part, 0)
    placed = lambda s, meta: (head_place(part, meta[2]), 0)
    first = lambda s, meta: (0, 0)
    all_slots = lambda s, meta: (0, 0, 0)
    width = HB * HD
    return pl.pallas_call(
        functools.partial(backward_kernel, slots),
        name="attention_backward",
        grid_spec=pltpu.PrefetchScalarGridSpec(
            num_scalar_prefetch=1,
            grid=(1,),
            in_specs=[
                once((width, rows), own),
                once((width, rows), placed),
                once((width, LAT), placed),
                once((width, LAT), placed),
                once((slots, rows, LAT), lambda s, meta: (0, 0, group)),
                once((HB, LAT, rows), lambda s, meta: (part, 0, 0)),
                once((HB, 1, rows), lambda s, meta: (part, 0, 0)),
            ],
            out_specs=[
                once((width, rows), first),
                once((width, LAT), first),
                once((width, LAT), first),
                once((slots, rows, LAT), all_slots),
            ],
            scratch_shapes=[
                pltpu.VMEM((slots, LAT, rows), BF16),
                pltpu.VMEM((LAT, 2 * HB * rows), BF16),
                pltpu.VMEM((LAT, HB * rows), F32),
                pltpu.VMEM((1, HB * rows), F32),
                pltpu.VMEM((1, HB * rows), F32),
            ],
        ),
        out_shape=[
            pltpu.HBM((width, rows), BF16),
            pltpu.HBM((width, LAT), BF16),
            pltpu.HBM((width, LAT), BF16),
            pltpu.HBM((slots, rows, LAT), BF16),
        ],
        compiler_params=pltpu.CompilerParams(
            dimension_semantics=("arbitrary",), vmem_limit_bytes=22 << 20
        ),
    )(meta, *[outside(v) for v in (q_t, da_t, wk, wv, blocks, ol)], lse)


def feed_kernel(h0, h1, h2, h3, df_ref, wg_ref, wu_ref, wd_ref,
                dh0, dh1, dh2, out_ref, x_ref, hid_ref, dg_ref, du_ref):
    step = pl.program_id(0)
    rows = h0.shape[0]
    for k, ref in enumerate((h0, h1, h2, h3)):

        @pl.when(step == k // 2)
        def _():
            x_ref[(k % 2) * rows : (k % 2 + 1) * rows, :] = ref[...]

    x = x_ref[...]
    gate = dot(wg_ref[...], x, ((1,), (1,)))
    up = dot(wu_ref[...], x, ((1,), (1,)))
    dhid = dot(wd_ref[...], df_ref[...], ((1,), (1,)))
    sig = jax.nn.sigmoid(gate)
    silu = gate * sig
    hid_ref[...] = (silu * up).astype(BF16)
    dg_ref[...] = (dhid * up * sig * (1.0 + gate * (1.0 - sig))).astype(BF16)
    du_ref[...] = (dhid * silu).astype(BF16)
    dh = (
        dot(dg_ref[...], wg_ref[...], ((0,), (0,))) + dot(du_ref[...], wu_ref[...], ((0,), (0,)))
    ).astype(BF16)

    @pl.when(step == 0)
    def _():
        dh0[...] = dh[:rows]
        dh1[...] = dh[rows:]

    @pl.when(step == 1)
    def _():
        dh2[0] = dh[:rows]
        dh2[1] = dh[rows:]

    out = dot(hid_ref[...], wd_ref[...], ((0,), (0,))).astype(BF16)
    out_ref[0] = out[:rows]
    out_ref[1] = out[rows:]


def feed_forward(pieces, df, w_gate, w_up, w_down):
    rows, width = pieces[0].shape
    ff = w_gate.shape[0]
    whole = lambda t: (0, 0)
    out = pl.pallas_call(
        feed_kernel,
        name="feed_forward",
        grid=(2,),
        in_specs=[once((rows, width), whole)] * 4
        + [pl.BlockSpec((2 * rows, width), lambda t: (t, 0))]
        + [once((ff, width), whole)] * 3,
        out_specs=[once((rows, width), whole)] * 2
        + [
            once((2, rows, width), lambda t: (0, 0, 0)),
            pl.BlockSpec((2, rows, width), lambda t: (t, 0, 0)),
            pl.BlockSpec((2 * rows, width), lambda t: (t, 0)),
        ]
        + [pl.BlockSpec((ff, 2 * rows), lambda t: (0, t))] * 3,
        out_shape=[pltpu.HBM((rows, width), BF16)] * 2
        + [pltpu.HBM((2, rows, width), BF16), pltpu.HBM((4, rows, width), BF16)]
        + [pltpu.HBM((4 * rows, width), BF16)]
        + [pltpu.HBM((ff, 4 * rows), BF16)] * 3,
        compiler_params=pltpu.CompilerParams(
            dimension_semantics=("arbitrary",), vmem_limit_bytes=56 << 20
        ),
    )(*pieces, df, w_gate, w_up, w_down)
    return out[:3], out[3], out[4], out[5:]


def feed_grad_kernel(codes, hid_ref, dg_ref, du_ref, x_ref, df_ref, *outs):
    tall, wide = outs[:2], outs[2:]
    cut = x_ref.shape[1] // 4
    parts = []
    for k in range(2):
        here = []
        for left, right, which in ((hid_ref, df_ref, 1), (dg_ref, x_ref, 0), (du_ref, x_ref, 0)):
            inner = k ^ ((codes[which] >> 1) & 1)
            both = dot(left[...], right[:, pl.ds(pl.multiple_of(inner * 2 * cut, 2 * cut), 2 * cut)]).astype(BF16)
            swapped = (codes[which] & 1) == 1
            here.append(
                (jnp.where(swapped, both[:, cut:], both[:, :cut]), jnp.where(swapped, both[:, :cut], both[:, cut:]))
            )
        parts.append(here)
    for half in range(2):

        @pl.when(pl.program_id(0) == half)
        def _():
            for k in range(2):
                for side in range(2):
                    tall[half][2 * k + side] = parts[k][0][side]
                    for i in range(2):
                        wide[half][2 * k + side, i] = parts[k][1 + i][side]


def feed_weight_grads(codes, hidden, x, df):
    ff, rows = hidden[0].shape
    cut = x.shape[1] // 8
    whole = lambda s, codes: (0, 0)
    tall = once((4, ff, cut), lambda s, codes: (0, 0, 0))
    wide = once((4, 2, ff, cut), lambda s, codes: (0, 0, 0, 0))
    low, high, low_wide, high_wide = pl.pallas_call(
        feed_grad_kernel,
        name="feed_weight_grads",
        grid_spec=pltpu.PrefetchScalarGridSpec(
            num_scalar_prefetch=1,
            grid=(2,),
            in_specs=[once((ff, rows), whole)] * 3
            + [
                pl.BlockSpec((rows, 4 * cut), lambda s, codes: (0, s ^ (codes[0] >> 2))),
                pl.BlockSpec((rows, 4 * cut), lambda s, codes: (0, s ^ (codes[1] >> 2))),
            ],
            out_specs=[tall, tall, wide, wide],
        ),
        out_shape=[pltpu.HBM((4, ff, cut), BF16)] * 2 + [pltpu.HBM((4, 2, ff, cut), BF16)] * 2,
        compiler_params=pltpu.CompilerParams(
            dimension_semantics=("arbitrary",), vmem_limit_bytes=40 << 20
        ),
    )(codes, *[outside(value) for value in (*hidden, x, df)])
    return (high, low[2:], low[1:2], low[:1]), (high_wide, low_wide[2:], low_wide[1:2], low_wide[:1])


def join_kernel(which, by_rows, cuts, codes, near_ref, far_ref, *outs):
    tall, wide = near_ref.shape[-2:]
    for i in range(8):
        position = i ^ codes[which]
        place = position & 3
        piece = jnp.where(position >= 4, far_ref[place].astype(F32), near_ref[place].astype(F32))
        if by_rows:
            low = 0
            for out, cut in zip(outs, cuts):
                out[i * tall : (i + 1) * tall, :] = piece[:, low : low + cut]
                low += cut
        elif len(outs) == 1:
            outs[0][:, i * wide : (i + 1) * wide] = piece
        else:
            for k, out in enumerate(outs):
                out[:, i * wide : (i + 1) * wide] = piece[k]


def join(which, codes, near, far, cuts=None):
    tall, wide = near.shape[-2:]
    vmem = pl.BlockSpec(memory_space=pltpu.VMEM)
    if cuts:
        shapes = [jax.ShapeDtypeStruct((8 * tall, cut), F32) for cut in cuts]
    else:
        shapes = [jax.ShapeDtypeStruct((tall, 8 * wide), F32)] * (near.shape[1] if near.ndim == 4 else 1)
    return pl.pallas_call(
        functools.partial(join_kernel, which, bool(cuts), cuts),
        name="join_pieces",
        in_specs=[pl.BlockSpec(memory_space=pltpu.SMEM), vmem, vmem],
        out_specs=[vmem] * len(shapes),
        out_shape=shapes,
        compiler_params=pltpu.CompilerParams(vmem_limit_bytes=20 << 20),
    )(codes, near, far)


def spread_kernel(which, contracts, codes, *refs):
    jobs, refs = refs[: 2 * len(contracts)], refs[2 * len(contracts) :]
    heads, (last_ref, near_ref, own_ref, acc_ref, head_ref) = refs[:-5], refs[-5:]
    cut = near_ref.shape[1]

    def put(low, width, take):
        for t in range(4):
            for position in range(8):
                value = take(t, pl.multiple_of((position ^ codes[which]) * cut, cut))
                if t >= 2:
                    last_ref[t - 2, position, :, low : low + width] = value
                else:
                    (own_ref, near_ref)[t][position, :, low : low + width] = value

    low = 0
    for i, contract in enumerate(contracts):
        right = jobs[2 * i + 1]
        width = right.shape[1 - contract[1][0]]
        acc_ref[:, :width] = dot(jobs[2 * i][...], right[...], contract)
        put(low, width, lambda t, start: acc_ref[pl.ds(t * 8 * cut + start, cut), :width].astype(BF16))
        low += width
    if heads:
        for p in range(4):
            mask = p ^ codes[2]
            place = (mask & 1) * 2 + (mask >> 1)
            head_ref[place, :, :LAT] = heads[2 * p][...]
            head_ref[place, :, LAT:] = heads[2 * p + 1][...]
        put(low, 2 * LAT, lambda t, start: head_ref[t, pl.ds(start, cut), :])


def spread_product(which, codes, jobs, heads=()):
    tall = jobs[0][0].shape[1 - jobs[0][2][0][0]]
    widths = [right.shape[1 - contract[1][0]] for _, right, contract in jobs]
    wide = sum(widths) + (2 * LAT if heads else 0)
    cut = tall // 32
    vmem = pl.BlockSpec(memory_space=pltpu.VMEM)
    operands = [x for left, right, _ in jobs for x in (left, right)] + list(heads)
    return pl.pallas_call(
        functools.partial(spread_kernel, which, [contract for _, _, contract in jobs]),
        name="spread_product",
        in_specs=[pl.BlockSpec(memory_space=pltpu.SMEM)] + [vmem] * len(operands),
        out_specs=[vmem] * 3,
        scratch_shapes=[pltpu.VMEM((tall, max(widths)), F32), pltpu.VMEM((4, tall // 4, 2 * LAT), BF16)],
        out_shape=[
            pltpu.HBM((2, 8, cut, wide), BF16),
            pltpu.HBM((8, cut, wide), BF16),
            pltpu.HBM((8, cut, wide), BF16),
        ],
        compiler_params=pltpu.CompilerParams(vmem_limit_bytes=20 << 20),
    )(codes, *operands)


class ShardSum:
    def __init__(self, last, near, own):
        self.near, self.own = near, own
        self.beside = swap(last, "fsdp", 1)

    def step(self, *tokens):
        self.beside = after(self.beside, *tokens) if tokens else self.beside
        sent = plus(self.near, self.beside[1])
        self.across = swap(sent, "fsdp", 2)
        return sent

    def part(self, low, high):
        return plus(self.own[low:high], self.beside[0, low:high], self.across[low:high])


def four_parts(part):
    return part(4, 8), part(2, 4), part(1, 2), part(0, 1)


def on_device(
    tokens,
    out_grad,
    lengths,
    norm1_gain,
    w_query,
    w_latent,
    w_key_up,
    w_value_up,
    w_output,
    norm2_gain,
    w_gate,
    w_up,
    w_down,
):
    ctx_size = lax.axis_size("ctx")
    tok_rows, width = tokens.shape[1], tokens.shape[2]
    ff = w_gate.shape[1]
    group_rows = tok_rows * ctx_size
    seq_rows = min(SEQ_MAX, group_rows)
    slots = seq_rows // tok_rows
    ctx_rank = lax.axis_index("ctx")
    member = lax.axis_index("fsdp")
    slot_number = ctx_rank // slots
    rank = ctx_rank % slots
    length = jnp.sum(
        jnp.where(jnp.arange(lengths.shape[1], dtype=jnp.int32) == slot_number, lengths[0], 0)
    )
    meta = jnp.stack([rank, length, member]).astype(jnp.int32)
    query_pos = rank * tok_rows + jnp.arange(tok_rows, dtype=jnp.int32)
    row_valid = (query_pos < length).astype(F32)[:, None]
    piece = width // 4
    order_a, order_b = (0, 1, 2), (1, 2, 0)
    codes = jnp.stack([code_of(ctx_rank, order_a), code_of(ctx_rank, order_b), member, 0 * member]).astype(jnp.int32)

    def reorder(value):
        return jnp.concatenate(
            [lax.dynamic_slice_in_dim(value, (member ^ m) * piece, piece, 1) for m in ORDER], axis=1
        )

    def restore(value):
        back = {m: t for t, m in enumerate(ORDER)}
        parts = [value[:, back[m] * piece : (back[m] + 1) * piece] for m in range(4)]
        low = (member & 1) == 1
        parts = [jnp.where(low, parts[j ^ 1], parts[j]) for j in range(4)]
        high = (member & 2) == 2
        parts = [jnp.where(high, parts[j ^ 2], parts[j]) for j in range(4)]
        return jnp.concatenate(parts, axis=1)

    latent_full = gather_rows(w_latent)
    gains = gather_rows(jnp.stack([norm1_gain, norm2_gain])[None])
    gain_one = jnp.concatenate([gains[t, 0] for t in range(4)])
    gain_two = restore(jnp.concatenate([gains[t, 1:] for t in range(4)], axis=1))
    gain_one_f = gain_one.astype(F32)
    gain_two_f = gain_two.astype(F32)
    inputs = tokens[0].astype(F32)
    mixed_in = reorder(tokens[0]).astype(F32)
    scale_one = norm_scale(inputs)
    normed_one = mixed_in * scale_one
    normed = (normed_one * gain_one_f).astype(BF16)
    latent = dot(normed, latent_full).astype(BF16)
    pieces = [latent]
    left, right = latent, latent
    side = jnp.concatenate([w_key_up, w_value_up], axis=1)
    weights = [after(w_query, latent_full), after(side, latent_full)]
    for _ in range(min(2, slots // 2 - 1)):
        left, right = ring_step(left, right, slots)
        pieces += [left, right]
    query_full = gather_rows(weights[0], *pieces[1:3])
    side_full = gather_rows(weights[1], *pieces[-2:])
    near = tuple(range(len(pieces)))
    key_full, value_full = side_full[:, :LAT], side_full[:, LAT:]
    q_t = dot(query_full, normed, ((0,), (1,))).astype(BF16)
    if len(pieces) < slots - 1:
        left, right = ring_step(left, right, slots)
        state = attention_forward(meta, q_t, key_full, value_full, pieces, near, slots, None, False)
        left, right = after((left, right), state[0])
        pieces += [left, right]
        while len(pieces) < slots - 1:
            left, right = ring_step(left, right, slots)
            pieces += [left, right]
    else:
        state = attention_forward(meta, q_t, key_full, value_full, pieces, near, slots, None, False)
    pieces.append(jnp.concatenate(ring_last(left, right, slots), axis=0))
    far = tuple(range(len(near), slots))
    att_t, mixture, log_total = attention_forward(
        meta, q_t, key_full, value_full, [pieces[k] for k in far], far, slots, state, True
    )
    blocks = jnp.stack(pieces)
    output_full = gather_rows(after(w_output, q_t), state[0])
    cotangent = out_grad[0].astype(F32) * row_valid
    feed_grad = gather_rows(after(cotangent.astype(BF16), q_t), state[0])
    middle = inputs + dot(att_t, output_full, ((0,), (0,)))
    scale_two = norm_scale(middle)
    normed_two_raw = middle * scale_two
    normed_two = (normed_two_raw * gain_two_f).astype(BF16)
    gate_rows, up_rows = w_gate.T, w_up.T
    normed_two_part, feed_part, ff_in, hidden = feed_forward(
        [after(normed_two, blocks)] + gather_four(normed_two)[1:], feed_grad, gate_rows, up_rows, w_down
    )
    beside = swap(normed_two_part[2], "fsdp", 1)
    home = plus(normed_two_part[1], beside[1])
    across = swap(home, "fsdp", 2)
    down_parts, wide_parts = feed_weight_grads(codes, hidden, after(ff_in, home), feed_grad)
    down_sum = CtxSum(down_parts, order_b, ctx_size)
    wide_sum = CtxSum(wide_parts, order_a, ctx_size)
    across = after(across, down_parts[0])
    normed_two_grad = (
        normed_two_part[0].astype(F32) + beside[0].astype(F32) + across.astype(F32)
    )
    middle_grad = cotangent + norm_back(normed_two_grad, normed_two_raw, scale_two, gain_two_f)
    branch_grad = middle_grad.astype(BF16)
    da_t = dot(output_full, branch_grad, ((1,), (1,))).astype(BF16)

    def back(part, *tokens):
        return attention_backward(
            part, meta, q_t, after(da_t, *tokens), key_full, value_full, blocks, mixture, log_total
        )

    nn, tn = ((1,), (0,)), ((0,), (0,))
    back_0 = back(0, wide_sum.sent, down_sum.sent)
    token = back_0[0]
    gates = [down_sum.step(token), wide_sum.step(token)]
    feed_part = after(feed_part, token)
    feed_beside = swap(feed_part[2:], "fsdp", 1)
    back_1 = back(1, *gates)
    token = back_1[0]
    tt = ((0,), (1,))
    early_shards = ShardSum(
        *spread_product(
            1, codes, [(att_t, after(branch_grad, token), nn), (normed, back_0[0], tt), (normed, token, tt)]
        )
    )
    sum_0 = SlotSum(back_0[3], back_1[3])
    gates = [down_sum.step(token), wide_sum.step(token)]
    gates.append(down_sum.step(early_shards.own))
    feed_home = plus(feed_part[1], after(feed_beside, token)[1])
    feed_across = swap(feed_home, "fsdp", 2)
    back_2 = back(2, sum_0.sent, early_shards.own, feed_home, *gates)
    token = back_2[0]
    gates = [sum_0.step(token), early_shards.step(token), down_sum.step(token), wide_sum.step(token)]
    back_3 = back(3, *gates)
    backward = [back_0, back_1, back_2, back_3]

    clock = [back_3[0]]

    def tick(value):
        clock[0] = value

    def ready(each):
        each.across = after(each.across, clock[0])

    sum_1 = SlotSum(back_2[3], back_3[3])
    ready(early_shards)
    early_sum = CtxSum(four_parts(early_shards.part), order_b, ctx_size)
    tick(early_sum.sent)
    heads = [x for part in backward for x in (part[1], part[2])]
    late_shards = ShardSum(
        *spread_product(0, codes, [(normed, back_2[0], tt), (normed, after(back_3[0], sum_1.sent), tt)], heads)
    )
    tick(late_shards.own)
    feed_out = plus_wide(feed_part[0], feed_beside[0], after(feed_across, clock[0]))
    result = ((middle + feed_out) * row_valid).astype(BF16)
    tick(result)
    tick(down_sum.take(clock[0]))
    tick(sum_0.step(clock[0]))
    tick(late_shards.step(clock[0]))
    tick(wide_sum.take(clock[0]))
    tick(early_sum.step(clock[0]))
    tick(sum_1.step(clock[0]))
    tick(wide_sum.give(clock[0]))
    sum_0.got = after(sum_0.got, clock[0])
    latent_0 = sum_0.finish()
    tick(latent_0)
    tick(early_sum.step(clock[0]))
    tick(sum_1.step(clock[0]))
    tick(down_sum.give(clock[0]))
    ready(late_shards)
    late_sum = CtxSum(four_parts(late_shards.part), order_a, ctx_size)
    tick(late_sum.sent)
    tick(early_sum.step(clock[0]))
    sum_1.got = after(sum_1.got, clock[0])
    latent_grad = jnp.concatenate([latent_0, sum_1.finish()], axis=1)
    latent_shards = ShardSum(*spread_product(1, codes, [(normed, latent_grad, tn)]))
    tick(latent_shards.step(latent_grad))
    tick(early_sum.step(clock[0]))
    tick(late_sum.step(clock[0]))
    tick(wide_sum.step(clock[0]))
    tick(early_sum.step(clock[0]))
    ready(latent_shards)
    latent_sum = CtxSum(four_parts(latent_shards.part), order_b, ctx_size)
    tick(latent_sum.sent)

    def tick_join(which, done, cuts=None):
        near_part, far_part = done.finish()
        out = join(which, codes, near_part, after(far_part, clock[0]), cuts)
        tick(out[0])
        return out

    half = NH * HD // 2
    tick(late_sum.step(clock[0]))
    tick(latent_sum.step(clock[0]))
    (down_grad,) = tick_join(1, down_sum)
    tick(late_sum.step(clock[0]))
    tick(latent_sum.step(clock[0]))
    output_grad, query_grad_0 = tick_join(1, early_sum, (width, half))
    tick(late_sum.step(clock[0]))
    tick(latent_sum.step(clock[0]))
    tick(late_sum.step(clock[0]))
    tick(latent_sum.step(clock[0]))
    gate_w_grad, up_w_grad = tick_join(0, wide_sum)
    tick(latent_sum.step(clock[0]))
    query_grad_1, key_grad, value_grad = tick_join(0, late_sum, (half, LAT, LAT))
    query_grad = jnp.concatenate([query_grad_0, query_grad_1], axis=1)
    (latent_w_grad,) = tick_join(1, latent_sum, (GRP * LAT,))
    dq_t = jnp.concatenate([part[0] for part in backward], axis=0)

    normed_grad = dot(dq_t, query_full, ((0,), (1,))) + dot(
        latent_grad, latent_full, ((1,), (1,))
    )
    input_grad = middle_grad + restore(
        norm_back(normed_grad, normed_one, scale_one, gain_one_f)
    )
    gain_one_grad = (
        jnp.sum(w_query.astype(F32) * query_grad, axis=1)
        + jnp.sum(w_latent.astype(F32) * latent_w_grad, axis=1)
    ) / norm1_gain.astype(F32)
    gain_two_part = jnp.sum(
        gate_rows.astype(F32) * gate_w_grad + up_rows.astype(F32) * up_w_grad, axis=0
    ).astype(BF16)
    gain_two_part = reorder(gain_two_part[None]).reshape(4, 1, piece)
    gain_two_grad = scatter_four(gain_two_part[:2], gain_two_part[2:])[0] / norm2_gain.astype(F32)
    return (
        result[None],
        input_grad[None],
        gain_one_grad,
        query_grad,
        latent_w_grad,
        key_grad,
        value_grad,
        output_grad,
        gain_two_grad,
        gate_w_grad.T,
        up_w_grad.T,
        down_grad,
    )


def solution(mesh):
    rows = P("fsdp", None)
    cols = P(None, "fsdp")
    toks = P("fsdp", "ctx", None)
    vec = P("fsdp")
    return jax.shard_map(
        on_device,
        mesh=mesh,
        in_specs=(toks, toks, rows, vec, rows, rows, rows, rows, rows, vec, cols, cols, rows),
        out_specs=(toks, toks, vec, rows, rows, rows, rows, rows, vec, cols, cols, rows),
        check_vma=False,
    )
```

```python
import functools

import jax
import jax.numpy as jnp
from jax import lax
from jax.experimental import pallas as pl
from jax.experimental.pallas import tpu as pltpu
from jax.sharding import PartitionSpec as P

NH = 16
HD = 64
LAT = 256
GRP = 2
SEQ_MAX = 4096
EPS = 1e-06
NEGATIVE = -1e30
HPG = NH // GRP
HB = 4
ORDER = (0, 2, 1, 3)
F32 = jnp.float32
BF16 = jnp.bfloat16


def dot(left, right, contract=((1,), (0,))):
    return lax.dot_general(left, right, (contract, ((), ())), preferred_element_type=F32)


def after(value, *tokens):
    return lax.optimization_barrier((value, tokens))[0]


def norm_scale(values):
    return lax.rsqrt(jnp.mean(values * values, axis=-1, keepdims=True) + EPS)


def norm_back(grad_in, normed, scale_rows, gain_full):
    scaled = grad_in * gain_full
    return scale_rows * (scaled - normed * jnp.mean(scaled * normed, axis=-1, keepdims=True))


def swap(value, axis, mask):
    size = lax.axis_size(axis)
    return lax.ppermute(value, axis, [(s, s ^ mask) for s in range(size)])


def gather_four(value, *tokens):
    across = swap(value, "fsdp", 2)
    beside = swap(value, "fsdp", 1)
    if tokens:
        across, beside = after((across, beside), *tokens)
    both = swap(across, "fsdp", 1)
    return [value, across, beside, both]


def gather_rows(value, *tokens):
    across = swap(value, "fsdp", 2)
    two = jnp.concatenate([value, after(across, *tokens) if tokens else across], axis=0)
    return jnp.concatenate([two, swap(two, "fsdp", 1)], axis=0)


def scatter_four(first_two, last_two):
    got = swap(last_two, "fsdp", 1)
    near = first_two.astype(F32) + got.astype(F32)
    far = swap(near[1].astype(BF16), "fsdp", 2)
    return near[0] + far.astype(F32)


def ring_members(count):
    return list(range(0, count, 2)) + list(range(count - 1, 0, -2)) if count > 1 else [0]


def ring_shift(value, slot_blocks, step):
    size = lax.axis_size("ctx")
    order = ring_members(slot_blocks)
    pairs = []
    for base in range(0, size, slot_blocks):
        for place in range(slot_blocks):
            pairs.append((base + order[place], base + order[(place + step) % slot_blocks]))
    return lax.ppermute(value, "ctx", pairs)


def ring_step(left, right, slots):
    return ring_shift(left, slots, 1), ring_shift(right, slots, -1)


def ring_last(left, right, slots):
    rows = left.shape[0]
    top, low = ring_step(left[: rows // 2], right[rows // 2 :], slots)
    return top, low


def slot_code(rank, slots):
    bits = slots.bit_length() - 1
    code = 0
    for bit in range(bits):
        code = code | (((rank >> bit) & 1) << (bits - 1 - bit))
    return code


class SlotSum:
    def __init__(self, *terms):
        self.terms, self.stage = terms, 0
        self.send()

    def send(self):
        self.half = self.terms[0].shape[0] // 2
        self.sent = plus(*[term[self.half :] for term in self.terms])
        self.got = swap(self.sent, "ctx", 1 << self.stage)

    def step(self, *tokens):
        got = after(self.got, *tokens) if tokens else self.got
        self.terms = [term[: self.half] for term in self.terms] + [got]
        self.stage += 1
        if self.half > 1:
            self.send()
        return self.sent

    def finish(self):
        while self.half > 1:
            self.step()
        self.step()
        return plus(*[term[0] for term in self.terms])


def plus_wide(*terms):
    total = terms[0].astype(F32)
    for term in terms[1:]:
        total = total + term.astype(F32)
    return total


def plus(*terms):
    return plus_wide(*terms).astype(BF16)


class CtxSum:
    def __init__(self, parts, order, size):
        self.parts, self.order, self.size = parts, order, size
        self.stage, self.got, self.sent = 0, [], parts[0]
        self.give()

    def give(self, *tokens):
        if tokens:
            self.sent = after(self.sent, *tokens)
        bits = self.order + self.order[::-1]
        self.got.append(swap(self.sent, "ctx", 1 << bits[self.stage]))
        return self.sent

    def take(self, *tokens):
        _, second, third, own = self.parts
        got = self.got
        if tokens:
            got[-1] = after(got[-1], *tokens)
        self.stage += 1
        if self.stage == 1:
            self.sent = plus(second, got[0][2:])
        elif self.stage == 2:
            self.sent = plus(third, got[0][1:2], got[1][1:])
        elif self.stage == 3:
            own = plus(own, got[0][:1], got[1][:1], got[2])
            for bit in range(self.size.bit_length() - 1):
                if bit not in self.order:
                    own = plus(own, swap(own, "ctx", 1 << bit))
            self.sent = own
        else:
            self.sent = jnp.concatenate([self.sent, got[-1]], axis=0)
        return self.sent

    def step(self, *tokens):
        self.take(*tokens)
        return self.give()

    def finish(self):
        while self.stage < 5:
            self.step()
        return self.sent, self.got[5]


def code_of(rank, order):
    return (((rank >> order[0]) & 1) << 2) | (((rank >> order[1]) & 1) << 1) | ((rank >> order[2]) & 1)


def place_of(rank, slots):
    return jnp.where(rank % 2 == 0, rank // 2, slots - 1 - rank // 2)


def slot_of(rank, other, slots):
    if slots == 1:
        return 0
    ahead = lax.rem(place_of(other, slots) - place_of(rank, slots) + slots, slots)
    return jnp.where(ahead <= slots // 2, 2 * ahead - (ahead == slots // 2).astype(jnp.int32), 2 * (slots - ahead) - 1)


def score_mask(first_key, first_query, length, rows, width):
    key = first_key + lax.broadcasted_iota(jnp.int32, (rows, width), 0)
    query = first_query + lax.rem(lax.broadcasted_iota(jnp.int32, (rows, width), 1), rows)
    return (key <= query) & (key < length)


def head_row(head, member):
    mask = (head // (NH // 4)) ^ member
    return (((mask & 1) * 2 + (mask >> 1)) * (NH // 4) + head % (NH // 4)) * HD


def other_of(rank, slot, slots):
    step = (slot + 1) // 2
    place = lax.rem(place_of(rank, slots) + (slots - step if slot % 2 else step), slots)
    return jnp.where(place < slots // 2, 2 * place, 2 * (slots - 1 - place) + 1)


def forward_kernel(slots, here, first, last, meta, q_ref, wk_ref, wv_ref, *rest):
    c_refs, rest = rest[: len(here)], rest[len(here) :]
    ins, rest = ((), rest) if first else (rest[:3], rest[3:])
    outs, rest = rest[:3], rest[3:]
    c_ref, ct_ref, ql_ref, m_ref, l_ref, acc_ref, index_ref = rest
    rows = q_ref.shape[1]
    rank, length, member = meta[0], meta[1], meta[2]
    group = pl.program_id(0)
    first_query = rank * rows
    active = first_query < length
    count = jnp.int32(0)
    for k, slot in enumerate(here):
        if slot == 0:
            need = active
        else:
            other = other_of(rank, slot, slots)
            need = active & (other < rank)
            index_ref[count] = jnp.int32(k)
            count = count + need.astype(jnp.int32)

        @pl.when(need)
        def _():
            block = c_refs[k][...]
            c_ref[k] = block
            ct_ref[k] = block.T

    if first:
        m_ref[...] = jnp.full_like(m_ref, NEGATIVE)
        l_ref[...] = jnp.zeros_like(l_ref)
        acc_ref[...] = jnp.zeros_like(acc_ref)
    else:
        m_ref[...] = ins[0][0]
        l_ref[...] = ins[1][0]
        acc_ref[...] = ins[2][0]

    @pl.when(active)
    def _():
        for i in range(HPG):
            part = pl.ds(i * HD, HD)
            row = pl.ds(pl.multiple_of(head_row(group * HPG + i, member), HD), HD)
            latent_q = dot(wk_ref[row, :], q_ref[part, :], ((0,), (0,))).astype(BF16)
            ql_ref[:, i * rows : (i + 1) * rows] = latent_q * jnp.asarray(HD ** -0.5, BF16)
        if first:
            scores = dot(c_ref[0], ql_ref[...])
            allowed = score_mask(first_query, first_query, length, rows, HPG * rows)
            scores = jnp.where(allowed, scores, NEGATIVE)
            best = jnp.max(scores, axis=0, keepdims=True)
            weights = jnp.where(allowed, jnp.exp(scores - best), 0.0)
            m_ref[...] = best
            l_ref[...] = jnp.sum(weights, axis=0, keepdims=True)
            acc_ref[...] = dot(ct_ref[0], weights.astype(BF16))

        def blocks(*which):
            scores = [dot(c_ref[k], ql_ref[...]) for k in which]
            best = m_ref[...]
            for each in scores:
                best = jnp.maximum(best, jnp.max(each, axis=0, keepdims=True))
            factor = jnp.exp(m_ref[...] - best)
            total = l_ref[...] * factor
            added = None
            for k, each in zip(which, scores):
                weights = jnp.exp(each - best)
                total = total + jnp.sum(weights, axis=0, keepdims=True)
                term = dot(ct_ref[k], weights.astype(BF16))
                added = term if added is None else added + term
            m_ref[...] = best
            l_ref[...] = total
            acc_ref[...] = acc_ref[...] * factor + added

        def loop(step, carry):
            blocks(index_ref[2 * step], index_ref[2 * step + 1])
            return carry

        lax.fori_loop(0, count // 2, loop, 0)

        @pl.when(count % 2 == 1)
        def _():
            blocks(index_ref[count - 1])

    if not last:
        outs[0][0] = m_ref[...]
        outs[1][0] = l_ref[...]
        outs[2][0] = acc_ref[...]
        return
    att_ref, ol_ref, lse_ref = outs
    total = l_ref[...]
    seen = total > 0.0
    safe = jnp.where(seen, total, 1.0)
    lse_all = jnp.where(seen, m_ref[...] + jnp.log(safe), 0.0)
    mixture = (acc_ref[...] * (1.0 / safe)).astype(BF16)
    for i in range(HPG):
        row = pl.ds(pl.multiple_of(head_row(group * HPG + i, member), HD), HD)
        cols = slice(i * rows, (i + 1) * rows)
        lse_ref[i] = lse_all[:, cols]
        ol_ref[i] = mixture[:, cols]
        att_ref[row, :] = dot(wv_ref[row, :], mixture[:, cols]).astype(BF16)


def backward_kernel(slots, meta, q_ref, da_ref, wk_ref, wv_ref, c_ref, ol_ref, lse_ref,
                    dq_ref, dwk_ref, dwv_ref, dc_ref,
                    ct_ref, left_ref, dql_ref, lse_all, delta_ref):
    rows = q_ref.shape[1]
    width = HB * rows
    rank, length = meta[0], meta[1]
    first_query = rank * rows
    scale = jnp.asarray(HD ** -0.5, BF16)
    active = first_query < length
    place_of_block = lambda block: slot_code(rank, slots) ^ slot_code(block, slots)

    def clear(block, carry):
        dc_ref[place_of_block(block)] = jnp.zeros((rows, LAT), BF16)
        return carry

    lax.fori_loop(jnp.where(active, rank + 1, 0), slots, clear, 0)

    @pl.when(jnp.logical_not(active))
    def _():
        dql_ref[...] = jnp.zeros_like(dql_ref)

    @pl.when(active)
    def _():
        def turn(block, carry):
            ct_ref[block] = c_ref[slot_of(rank, block, slots)].T
            return carry

        lax.fori_loop(0, rank + 1, turn, 0)
        for i in range(HB):
            part = pl.ds(i * HD, HD)
            cols = slice(i * rows, (i + 1) * rows)
            left_ref[:, cols] = dot(wk_ref[part, :], q_ref[part, :], ((0,), (0,))).astype(BF16) * scale
            dol_t = dot(wv_ref[part, :], da_ref[part, :], ((0,), (0,))).astype(BF16)
            left_ref[:, width + i * rows : width + (i + 1) * rows] = dol_t
            delta_ref[:, cols] = jnp.sum(dol_t.astype(F32) * ol_ref[i].astype(F32), axis=0, keepdims=True)
            lse_all[:, cols] = lse_ref[i]

        def grads(block, allowed):
            pair = dot(c_ref[slot_of(rank, block, slots)], left_ref[...])
            probs = jnp.exp(pair[:, :width] - lse_all[...])
            if allowed is not None:
                probs = jnp.where(allowed, probs, 0.0)
            score_grad = (probs * (pair[:, width:] - delta_ref[...])).astype(BF16)
            both = ((1,), (1,))
            dc_ref[place_of_block(block)] = (
                dot(score_grad, left_ref[:, :width], both) + dot(probs.astype(BF16), left_ref[:, width:], both)
            ).astype(BF16)
            return dot(ct_ref[block], score_grad)

        dql_ref[...] = grads(rank, score_mask(first_query, first_query, length, rows, width))

        def loop(step, carry):
            dql_ref[...] += grads(2 * step, None) + grads(2 * step + 1, None)
            return carry

        lax.fori_loop(0, rank // 2, loop, 0)

        @pl.when(rank % 2 == 1)
        def _():
            dql_ref[...] += grads(rank - 1, None)

    for i in range(HB):
        part = pl.ds(i * HD, HD)
        latent_grad = (dql_ref[:, i * rows : (i + 1) * rows] * (HD ** -0.5)).astype(BF16)
        dq_ref[part, :] = dot(wk_ref[part, :], latent_grad).astype(BF16)
        dwk_ref[part, :] = dot(q_ref[part, :], latent_grad, ((1,), (1,))).astype(BF16)
        dwv_ref[part, :] = dot(da_ref[part, :], ol_ref[i], ((1,), (1,))).astype(BF16)


def outside(value):
    return pltpu.with_memory_space_constraint(value, pltpu.HBM)


def once(shape, index):
    return pl.BlockSpec(shape, index, pipeline_mode=pl.Buffered(1))


def head_place(step, member):
    per_piece = NH // 4 // HB
    mask = (step // per_piece) ^ member
    return ((mask & 1) * 2 + (mask >> 1)) * per_piece + step % per_piece


def attention_forward(meta, q_t, wk, wv, pieces, here, slots, state=None, last=True):
    rows = q_t.shape[1]
    first = state is None
    wide = HPG * rows
    by_group = lambda g, meta: (g, 0, 0)
    if last:
        out_specs = [
            pl.BlockSpec((NH * HD, rows), lambda g, meta: (0, 0)),
            pl.BlockSpec((HPG, LAT, rows), by_group),
            pl.BlockSpec((HPG, 1, rows), by_group),
        ]
        out_shape = [
            jax.ShapeDtypeStruct((NH * HD, rows), BF16),
            pltpu.HBM((NH, LAT, rows), BF16),
            jax.ShapeDtypeStruct((NH, 1, rows), F32),
        ]
    else:
        out_specs = [pl.BlockSpec((1, n, wide), by_group) for n in (1, 1, LAT)]
        out_shape = [jax.ShapeDtypeStruct((GRP, n, wide), F32) for n in (1, 1, LAT)]
    return pl.pallas_call(
        functools.partial(forward_kernel, slots, here, first, last),
        name="attention_forward",
        grid_spec=pltpu.PrefetchScalarGridSpec(
            num_scalar_prefetch=1,
            grid=(GRP,),
            in_specs=[
                pl.BlockSpec((HPG * HD, rows), lambda g, meta: (g, 0)),
                once((NH * HD, LAT), lambda g, meta: (0, 0)),
                once((NH * HD, LAT), lambda g, meta: (0, 0)),
            ]
            + [pl.BlockSpec((rows, LAT), lambda g, meta: (0, g))] * len(here)
            + ([] if first else [pl.BlockSpec((1, n, wide), by_group) for n in (1, 1, LAT)]),
            out_specs=out_specs,
            scratch_shapes=[
                pltpu.VMEM((len(here), rows, LAT), BF16),
                pltpu.VMEM((len(here), LAT, rows), BF16),
                pltpu.VMEM((LAT, wide), BF16),
                pltpu.VMEM((1, wide), F32),
                pltpu.VMEM((1, wide), F32),
                pltpu.VMEM((LAT, wide), F32),
                pltpu.SMEM((len(here) + 1,), jnp.int32),
            ],
        ),
        out_shape=out_shape,
        compiler_params=pltpu.CompilerParams(
            dimension_semantics=("arbitrary",), vmem_limit_bytes=32 << 20
        ),
    )(meta, q_t, wk, wv, *pieces, *(state or ()))


def attention_backward(part, meta, q_t, da_t, wk, wv, blocks, ol, lse):
    slots, rows, _ = blocks.shape
    group = part * HB // HPG
    own = lambda s, meta: (part, 0)
    placed = lambda s, meta: (head_place(part, meta[2]), 0)
    first = lambda s, meta: (0, 0)
    all_slots = lambda s, meta: (0, 0, 0)
    width = HB * HD
    return pl.pallas_call(
        functools.partial(backward_kernel, slots),
        name="attention_backward",
        grid_spec=pltpu.PrefetchScalarGridSpec(
            num_scalar_prefetch=1,
            grid=(1,),
            in_specs=[
                once((width, rows), own),
                once((width, rows), placed),
                once((width, LAT), placed),
                once((width, LAT), placed),
                once((slots, rows, LAT), lambda s, meta: (0, 0, group)),
                once((HB, LAT, rows), lambda s, meta: (part, 0, 0)),
                once((HB, 1, rows), lambda s, meta: (part, 0, 0)),
            ],
            out_specs=[
                once((width, rows), first),
                once((width, LAT), first),
                once((width, LAT), first),
                once((slots, rows, LAT), all_slots),
            ],
            scratch_shapes=[
                pltpu.VMEM((slots, LAT, rows), BF16),
                pltpu.VMEM((LAT, 2 * HB * rows), BF16),
                pltpu.VMEM((LAT, HB * rows), F32),
                pltpu.VMEM((1, HB * rows), F32),
                pltpu.VMEM((1, HB * rows), F32),
            ],
        ),
        out_shape=[
            pltpu.HBM((width, rows), BF16),
            pltpu.HBM((width, LAT), BF16),
            pltpu.HBM((width, LAT), BF16),
            pltpu.HBM((slots, rows, LAT), BF16),
        ],
        compiler_params=pltpu.CompilerParams(
            dimension_semantics=("arbitrary",), vmem_limit_bytes=22 << 20
        ),
    )(meta, *[outside(v) for v in (q_t, da_t, wk, wv, blocks, ol)], lse)


def feed_kernel(h0, h1, h2, h3, df_ref, wg_ref, wu_ref, wd_ref,
                dh0, dh1, dh2, out_ref, x_ref, hid_ref, dg_ref, du_ref):
    step = pl.program_id(0)
    rows = h0.shape[0]
    for k, ref in enumerate((h0, h1, h2, h3)):

        @pl.when(step == k // 2)
        def _():
            x_ref[(k % 2) * rows : (k % 2 + 1) * rows, :] = ref[...]

    x = x_ref[...]
    gate = dot(wg_ref[...], x, ((1,), (1,)))
    up = dot(wu_ref[...], x, ((1,), (1,)))
    dhid = dot(wd_ref[...], df_ref[...], ((1,), (1,)))
    sig = jax.nn.sigmoid(gate)
    silu = gate * sig
    hid_ref[...] = (silu * up).astype(BF16)
    dg_ref[...] = (dhid * up * sig * (1.0 + gate * (1.0 - sig))).astype(BF16)
    du_ref[...] = (dhid * silu).astype(BF16)
    dh = (
        dot(dg_ref[...], wg_ref[...], ((0,), (0,))) + dot(du_ref[...], wu_ref[...], ((0,), (0,)))
    ).astype(BF16)

    @pl.when(step == 0)
    def _():
        dh0[...] = dh[:rows]
        dh1[...] = dh[rows:]

    @pl.when(step == 1)
    def _():
        dh2[0] = dh[:rows]
        dh2[1] = dh[rows:]

    out = dot(hid_ref[...], wd_ref[...], ((0,), (0,))).astype(BF16)
    out_ref[0] = out[:rows]
    out_ref[1] = out[rows:]


def feed_forward(pieces, df, w_gate, w_up, w_down):
    rows, width = pieces[0].shape
    ff = w_gate.shape[0]
    whole = lambda t: (0, 0)
    out = pl.pallas_call(
        feed_kernel,
        name="feed_forward",
        grid=(2,),
        in_specs=[once((rows, width), whole)] * 4
        + [pl.BlockSpec((2 * rows, width), lambda t: (t, 0))]
        + [once((ff, width), whole)] * 3,
        out_specs=[once((rows, width), whole)] * 2
        + [
            once((2, rows, width), lambda t: (0, 0, 0)),
            pl.BlockSpec((2, rows, width), lambda t: (t, 0, 0)),
            pl.BlockSpec((2 * rows, width), lambda t: (t, 0)),
        ]
        + [pl.BlockSpec((ff, 2 * rows), lambda t: (0, t))] * 3,
        out_shape=[pltpu.HBM((rows, width), BF16)] * 2
        + [pltpu.HBM((2, rows, width), BF16), pltpu.HBM((4, rows, width), BF16)]
        + [pltpu.HBM((4 * rows, width), BF16)]
        + [pltpu.HBM((ff, 4 * rows), BF16)] * 3,
        compiler_params=pltpu.CompilerParams(
            dimension_semantics=("arbitrary",), vmem_limit_bytes=56 << 20
        ),
    )(*pieces, df, w_gate, w_up, w_down)
    return out[:3], out[3], out[4], out[5:]


def feed_grad_kernel(which, count, codes, right_ref, *refs):
    lefts, (low_ref, high_ref) = refs[:count], refs[count:]
    cut = right_ref.shape[1] // 4
    swapped = (codes[which] & 1) == 1
    parts = []
    for k in range(2):
        inner = k ^ ((codes[which] >> 1) & 1)
        right = right_ref[:, pl.ds(pl.multiple_of(inner * 2 * cut, 2 * cut), 2 * cut)]
        here = []
        for left in lefts:
            both = dot(left[...], right).astype(BF16)
            here.append(
                (jnp.where(swapped, both[:, cut:], both[:, :cut]), jnp.where(swapped, both[:, :cut], both[:, cut:]))
            )
        parts.append(here)
    for half, out in enumerate((low_ref, high_ref)):

        @pl.when(pl.program_id(0) == half)
        def _():
            for k in range(2):
                for side in range(2):
                    for i in range(count):
                        if count == 1:
                            out[2 * k + side] = parts[k][i][side]
                        else:
                            out[2 * k + side, i] = parts[k][i][side]


def feed_weight_grads(which, codes, lefts, right):
    ff, rows = lefts[0].shape
    cut = right.shape[1] // 8
    count = len(lefts)
    shape = (4, ff, cut) if count == 1 else (4, count, ff, cut)
    low, high = pl.pallas_call(
        functools.partial(feed_grad_kernel, which, count),
        name="feed_weight_grads",
        grid_spec=pltpu.PrefetchScalarGridSpec(
            num_scalar_prefetch=1,
            grid=(2,),
            in_specs=[pl.BlockSpec((rows, 4 * cut), lambda s, codes: (0, s ^ (codes[which] >> 2)))]
            + [once((ff, rows), lambda s, codes: (0, 0))] * count,
            out_specs=[once(shape, lambda s, codes: (0,) * len(shape))] * 2,
        ),
        out_shape=[pltpu.HBM(shape, BF16)] * 2,
        compiler_params=pltpu.CompilerParams(
            dimension_semantics=("arbitrary",), vmem_limit_bytes=40 << 20
        ),
    )(codes, *[outside(value) for value in (right, *lefts)])
    return high, low[2:], low[1:2], low[:1]


def join_kernel(which, by_rows, cuts, codes, near_ref, far_ref, *outs):
    tall, wide = near_ref.shape[-2:]
    for i in range(8):
        position = i ^ codes[which]
        place = position & 3
        piece = jnp.where(position >= 4, far_ref[place].astype(F32), near_ref[place].astype(F32))
        if by_rows:
            low = 0
            for out, cut in zip(outs, cuts):
                out[i * tall : (i + 1) * tall, :] = piece[:, low : low + cut]
                low += cut
        elif len(outs) == 1:
            outs[0][:, i * wide : (i + 1) * wide] = piece
        else:
            for k, out in enumerate(outs):
                out[:, i * wide : (i + 1) * wide] = piece[k]


def join(which, codes, near, far, cuts=None):
    tall, wide = near.shape[-2:]
    vmem = pl.BlockSpec(memory_space=pltpu.VMEM)
    if cuts:
        shapes = [jax.ShapeDtypeStruct((8 * tall, cut), F32) for cut in cuts]
    else:
        shapes = [jax.ShapeDtypeStruct((tall, 8 * wide), F32)] * (near.shape[1] if near.ndim == 4 else 1)
    return pl.pallas_call(
        functools.partial(join_kernel, which, bool(cuts), cuts),
        name="join_pieces",
        in_specs=[pl.BlockSpec(memory_space=pltpu.SMEM), vmem, vmem],
        out_specs=[vmem] * len(shapes),
        out_shape=shapes,
        compiler_params=pltpu.CompilerParams(vmem_limit_bytes=20 << 20),
    )(codes, near, far)


def spread_kernel(which, contracts, codes, *refs):
    jobs, refs = refs[: 2 * len(contracts)], refs[2 * len(contracts) :]
    heads, (last_ref, near_ref, own_ref, acc_ref, head_ref) = refs[:-5], refs[-5:]
    cut = near_ref.shape[1]

    def put(low, width, take):
        for t in range(4):
            for position in range(8):
                value = take(t, pl.multiple_of((position ^ codes[which]) * cut, cut))
                if t >= 2:
                    last_ref[t - 2, position, :, low : low + width] = value
                else:
                    (own_ref, near_ref)[t][position, :, low : low + width] = value

    low = 0
    for i, contract in enumerate(contracts):
        right = jobs[2 * i + 1]
        width = right.shape[1 - contract[1][0]]
        acc_ref[:, :width] = dot(jobs[2 * i][...], right[...], contract)
        put(low, width, lambda t, start: acc_ref[pl.ds(t * 8 * cut + start, cut), :width].astype(BF16))
        low += width
    if heads:
        for p in range(4):
            mask = p ^ codes[2]
            place = (mask & 1) * 2 + (mask >> 1)
            head_ref[place, :, :LAT] = heads[2 * p][...]
            head_ref[place, :, LAT:] = heads[2 * p + 1][...]
        put(low, 2 * LAT, lambda t, start: head_ref[t, pl.ds(start, cut), :])


def spread_product(which, codes, jobs, heads=()):
    tall = jobs[0][0].shape[1 - jobs[0][2][0][0]]
    widths = [right.shape[1 - contract[1][0]] for _, right, contract in jobs]
    wide = sum(widths) + (2 * LAT if heads else 0)
    cut = tall // 32
    vmem = pl.BlockSpec(memory_space=pltpu.VMEM)
    operands = [x for left, right, _ in jobs for x in (left, right)] + list(heads)
    return pl.pallas_call(
        functools.partial(spread_kernel, which, [contract for _, _, contract in jobs]),
        name="spread_product",
        in_specs=[pl.BlockSpec(memory_space=pltpu.SMEM)] + [vmem] * len(operands),
        out_specs=[vmem] * 3,
        scratch_shapes=[pltpu.VMEM((tall, max(widths)), F32), pltpu.VMEM((4, tall // 4, 2 * LAT), BF16)],
        out_shape=[
            pltpu.HBM((2, 8, cut, wide), BF16),
            pltpu.HBM((8, cut, wide), BF16),
            pltpu.HBM((8, cut, wide), BF16),
        ],
        compiler_params=pltpu.CompilerParams(vmem_limit_bytes=20 << 20),
    )(codes, *operands)


class ShardSum:
    def __init__(self, last, near, own):
        self.near, self.own = near, own
        self.beside = swap(last, "fsdp", 1)

    def step(self, *tokens):
        self.beside = after(self.beside, *tokens) if tokens else self.beside
        sent = plus(self.near, self.beside[1])
        self.across = swap(sent, "fsdp", 2)
        return sent

    def part(self, low, high):
        return plus(self.own[low:high], self.beside[0, low:high], self.across[low:high])


def four_parts(part):
    return part(4, 8), part(2, 4), part(1, 2), part(0, 1)


def on_device(
    tokens,
    out_grad,
    lengths,
    norm1_gain,
    w_query,
    w_latent,
    w_key_up,
    w_value_up,
    w_output,
    norm2_gain,
    w_gate,
    w_up,
    w_down,
):
    ctx_size = lax.axis_size("ctx")
    tok_rows, width = tokens.shape[1], tokens.shape[2]
    ff = w_gate.shape[1]
    group_rows = tok_rows * ctx_size
    seq_rows = min(SEQ_MAX, group_rows)
    slots = seq_rows // tok_rows
    ctx_rank = lax.axis_index("ctx")
    member = lax.axis_index("fsdp")
    slot_number = ctx_rank // slots
    rank = ctx_rank % slots
    length = jnp.sum(
        jnp.where(jnp.arange(lengths.shape[1], dtype=jnp.int32) == slot_number, lengths[0], 0)
    )
    meta = jnp.stack([rank, length, member]).astype(jnp.int32)
    query_pos = rank * tok_rows + jnp.arange(tok_rows, dtype=jnp.int32)
    row_valid = (query_pos < length).astype(F32)[:, None]
    piece = width // 4
    order_a, order_b = (0, 1, 2), (1, 2, 0)
    codes = jnp.stack([code_of(ctx_rank, order_a), code_of(ctx_rank, order_b), member, 0 * member]).astype(jnp.int32)

    def reorder(value):
        return jnp.concatenate(
            [lax.dynamic_slice_in_dim(value, (member ^ m) * piece, piece, 1) for m in ORDER], axis=1
        )

    def restore(value):
        back = {m: t for t, m in enumerate(ORDER)}
        parts = [value[:, back[m] * piece : (back[m] + 1) * piece] for m in range(4)]
        low = (member & 1) == 1
        parts = [jnp.where(low, parts[j ^ 1], parts[j]) for j in range(4)]
        high = (member & 2) == 2
        parts = [jnp.where(high, parts[j ^ 2], parts[j]) for j in range(4)]
        return jnp.concatenate(parts, axis=1)

    latent_full = gather_rows(w_latent)
    gains = gather_rows(jnp.stack([norm1_gain, norm2_gain])[None])
    gain_one = jnp.concatenate([gains[t, 0] for t in range(4)])
    gain_two = restore(jnp.concatenate([gains[t, 1:] for t in range(4)], axis=1))
    gain_one_f = gain_one.astype(F32)
    gain_two_f = gain_two.astype(F32)
    inputs = tokens[0].astype(F32)
    mixed_in = reorder(tokens[0]).astype(F32)
    scale_one = norm_scale(inputs)
    normed_one = mixed_in * scale_one
    normed = (normed_one * gain_one_f).astype(BF16)
    latent = dot(normed, latent_full).astype(BF16)
    pieces = [latent]
    left, right = latent, latent
    side = jnp.concatenate([w_key_up, w_value_up], axis=1)
    weights = [after(w_query, latent_full), after(side, latent_full)]
    for _ in range(min(2, slots // 2 - 1)):
        left, right = ring_step(left, right, slots)
        pieces += [left, right]
    query_full = gather_rows(weights[0], *pieces[1:3])
    side_full = gather_rows(weights[1], *pieces[-2:])
    near = tuple(range(len(pieces)))
    key_full, value_full = side_full[:, :LAT], side_full[:, LAT:]
    q_t = dot(query_full, normed, ((0,), (1,))).astype(BF16)
    if len(pieces) < slots - 1:
        left, right = ring_step(left, right, slots)
        state = attention_forward(meta, q_t, key_full, value_full, pieces, near, slots, None, False)
        left, right = after((left, right), state[0])
        pieces += [left, right]
        while len(pieces) < slots - 1:
            left, right = ring_step(left, right, slots)
            pieces += [left, right]
    else:
        state = attention_forward(meta, q_t, key_full, value_full, pieces, near, slots, None, False)
    pieces.append(jnp.concatenate(ring_last(left, right, slots), axis=0))
    far = tuple(range(len(near), slots))
    att_t, mixture, log_total = attention_forward(
        meta, q_t, key_full, value_full, [pieces[k] for k in far], far, slots, state, True
    )
    blocks = jnp.stack(pieces)
    output_full = gather_rows(after(w_output, q_t), state[0])
    cotangent = out_grad[0].astype(F32) * row_valid
    feed_grad = gather_rows(after(cotangent.astype(BF16), q_t), state[0])
    middle = inputs + dot(att_t, output_full, ((0,), (0,)))
    scale_two = norm_scale(middle)
    normed_two_raw = middle * scale_two
    normed_two = (normed_two_raw * gain_two_f).astype(BF16)
    gate_rows, up_rows = w_gate.T, w_up.T
    normed_two_part, feed_part, ff_in, hidden = feed_forward(
        [after(normed_two, blocks)] + gather_four(normed_two)[1:], feed_grad, gate_rows, up_rows, w_down
    )
    beside = swap(normed_two_part[2], "fsdp", 1)
    wide_parts = feed_weight_grads(0, codes, hidden[1:], ff_in)
    wide_sum = CtxSum(wide_parts, order_a, ctx_size)
    beside = after(beside, wide_parts[0])
    home = plus(normed_two_part[1], beside[1])
    across = swap(home, "fsdp", 2)
    down_parts = feed_weight_grads(1, codes, hidden[:1], after(feed_grad, home))
    down_sum = CtxSum(down_parts, order_b, ctx_size)
    across = after(across, down_parts[0])
    normed_two_grad = (
        normed_two_part[0].astype(F32) + beside[0].astype(F32) + across.astype(F32)
    )
    middle_grad = cotangent + norm_back(normed_two_grad, normed_two_raw, scale_two, gain_two_f)
    gain_two_terms = reorder((normed_two_grad * normed_two_raw).astype(BF16))
    branch_grad = middle_grad.astype(BF16)
    da_t = dot(output_full, branch_grad, ((1,), (1,))).astype(BF16)

    def back(part, *tokens):
        return attention_backward(
            part, meta, q_t, after(da_t, *tokens), key_full, value_full, blocks, mixture, log_total
        )

    nn, tn = ((1,), (0,)), ((0,), (0,))
    back_0 = back(0, wide_sum.sent, down_sum.sent)
    token = back_0[0]
    gates = [down_sum.step(token), wide_sum.step(token)]
    feed_part = after(feed_part, token)
    feed_beside = swap(feed_part[2:], "fsdp", 1)
    back_1 = back(1, *gates)
    token = back_1[0]
    tt = ((0,), (1,))
    early_shards = ShardSum(
        *spread_product(
            1,
            codes,
            [
                (att_t, after(branch_grad, token), nn),
                (normed, back_0[0], tt),
                (normed, token, tt),
                (gain_two_terms, jnp.ones((tok_rows, 128), BF16), tn),
            ],
        )
    )
    sum_0 = SlotSum(back_0[3], back_1[3])
    gates = [down_sum.step(token), wide_sum.step(token)]
    gates.append(down_sum.step(early_shards.own))
    feed_home = plus(feed_part[1], after(feed_beside, token)[1])
    feed_across = swap(feed_home, "fsdp", 2)
    back_2 = back(2, sum_0.sent, early_shards.own, feed_home, *gates)
    token = back_2[0]
    gates = [sum_0.step(token), early_shards.step(token), down_sum.step(token), wide_sum.step(token)]
    back_3 = back(3, *gates)
    backward = [back_0, back_1, back_2, back_3]

    clock = [back_3[0]]

    def tick(value):
        clock[0] = value

    def ready(each):
        each.across = after(each.across, clock[0])

    sum_1 = SlotSum(back_2[3], back_3[3])
    ready(early_shards)
    early_sum = CtxSum(four_parts(early_shards.part), order_b, ctx_size)
    tick(early_sum.sent)
    heads = [x for part in backward for x in (part[1], part[2])]
    late_shards = ShardSum(
        *spread_product(0, codes, [(normed, back_2[0], tt), (normed, after(back_3[0], sum_1.sent), tt)], heads)
    )
    tick(late_shards.own)
    feed_out = plus_wide(feed_part[0], feed_beside[0], after(feed_across, clock[0]))
    result = ((middle + feed_out) * row_valid).astype(BF16)
    tick(result)
    tick(down_sum.take(clock[0]))
    tick(sum_0.step(clock[0]))
    tick(late_shards.step(clock[0]))
    tick(wide_sum.take(clock[0]))
    tick(early_sum.step(clock[0]))
    tick(sum_1.step(clock[0]))
    tick(wide_sum.give(clock[0]))
    sum_0.got = after(sum_0.got, clock[0])
    latent_0 = sum_0.finish()
    tick(latent_0)
    tick(early_sum.step(clock[0]))
    tick(sum_1.step(clock[0]))
    tick(down_sum.give(clock[0]))
    ready(late_shards)
    late_sum = CtxSum(four_parts(late_shards.part), order_a, ctx_size)
    tick(late_sum.sent)
    tick(early_sum.step(clock[0]))
    sum_1.got = after(sum_1.got, clock[0])
    latent_grad = jnp.concatenate([latent_0, sum_1.finish()], axis=1)
    latent_shards = ShardSum(*spread_product(1, codes, [(normed, latent_grad, tn)]))
    tick(latent_shards.step(latent_grad))
    tick(early_sum.step(clock[0]))
    tick(late_sum.step(clock[0]))
    tick(wide_sum.step(clock[0]))
    tick(early_sum.step(clock[0]))
    ready(latent_shards)
    latent_sum = CtxSum(four_parts(latent_shards.part), order_b, ctx_size)
    tick(latent_sum.sent)

    def tick_join(which, done, cuts=None):
        near_part, far_part = done.finish()
        out = join(which, codes, near_part, after(far_part, clock[0]), cuts)
        tick(out[0])
        return out

    half = NH * HD // 2
    tick(late_sum.step(clock[0]))
    tick(latent_sum.step(clock[0]))
    (down_grad,) = tick_join(1, down_sum)
    tick(late_sum.step(clock[0]))
    tick(latent_sum.step(clock[0]))
    output_grad, query_grad_0, gain_two_grad = tick_join(1, early_sum, (width, half, 128))
    tick(late_sum.step(clock[0]))
    tick(latent_sum.step(clock[0]))
    tick(late_sum.step(clock[0]))
    tick(latent_sum.step(clock[0]))
    gate_w_grad, up_w_grad = tick_join(0, wide_sum)
    tick(latent_sum.step(clock[0]))
    query_grad_1, key_grad, value_grad = tick_join(0, late_sum, (half, LAT, LAT))
    query_grad = jnp.concatenate([query_grad_0, query_grad_1], axis=1)
    (latent_w_grad,) = tick_join(1, latent_sum, (GRP * LAT,))
    dq_t = jnp.concatenate([part[0] for part in backward], axis=0)

    normed_grad = dot(dq_t, query_full, ((0,), (1,))) + dot(
        latent_grad, latent_full, ((1,), (1,))
    )
    input_grad = middle_grad + restore(
        norm_back(normed_grad, normed_one, scale_one, gain_one_f)
    )
    gain_one_grad = (
        jnp.sum(w_query.astype(F32) * query_grad, axis=1)
        + jnp.sum(w_latent.astype(F32) * latent_w_grad, axis=1)
    ) / norm1_gain.astype(F32)
    return (
        result[None],
        input_grad[None],
        gain_one_grad,
        query_grad,
        latent_w_grad,
        key_grad,
        value_grad,
        output_grad,
        gain_two_grad[:, 0],
        gate_w_grad.T,
        up_w_grad.T,
        down_grad,
    )


def solution(mesh):
    rows = P("fsdp", None)
    cols = P(None, "fsdp")
    toks = P("fsdp", "ctx", None)
    vec = P("fsdp")
    return jax.shard_map(
        on_device,
        mesh=mesh,
        in_specs=(toks, toks, rows, vec, rows, rows, rows, rows, rows, vec, cols, cols, rows),
        out_specs=(toks, toks, vec, rows, rows, rows, rows, rows, vec, cols, cols, rows),
        check_vma=False,
    )
```

```python
import functools

import jax
import jax.numpy as jnp
from jax import lax
from jax.experimental import pallas as pl
from jax.experimental.pallas import tpu as pltpu
from jax.sharding import PartitionSpec as P

NH = 16
HD = 64
LAT = 256
GRP = 2
SEQ_MAX = 4096
EPS = 1e-06
NEGATIVE = -1e30
HPG = NH // GRP
HB = 4
ORDER = (0, 2, 1, 3)
F32 = jnp.float32
BF16 = jnp.bfloat16


def dot(left, right, contract=((1,), (0,))):
    return lax.dot_general(left, right, (contract, ((), ())), preferred_element_type=F32)


def after(value, *tokens):
    return lax.optimization_barrier((value, tokens))[0]


def norm_scale(values):
    return lax.rsqrt(jnp.mean(values * values, axis=-1, keepdims=True) + EPS)


def norm_back(grad_in, normed, scale_rows, gain_full):
    scaled = grad_in * gain_full
    return scale_rows * (scaled - normed * jnp.mean(scaled * normed, axis=-1, keepdims=True))


def swap(value, axis, mask):
    size = lax.axis_size(axis)
    return lax.ppermute(value, axis, [(s, s ^ mask) for s in range(size)])


def gather_four(value, *tokens):
    across = swap(value, "fsdp", 2)
    beside = swap(value, "fsdp", 1)
    if tokens:
        across, beside = after((across, beside), *tokens)
    both = swap(across, "fsdp", 1)
    return [value, across, beside, both]


def gather_rows(value, *tokens):
    across = swap(value, "fsdp", 2)
    two = jnp.concatenate([value, after(across, *tokens) if tokens else across], axis=0)
    return jnp.concatenate([two, swap(two, "fsdp", 1)], axis=0)


def scatter_four(first_two, last_two):
    got = swap(last_two, "fsdp", 1)
    near = first_two.astype(F32) + got.astype(F32)
    far = swap(near[1].astype(BF16), "fsdp", 2)
    return near[0] + far.astype(F32)


def ring_members(count):
    return list(range(0, count, 2)) + list(range(count - 1, 0, -2)) if count > 1 else [0]


def ring_shift(value, slot_blocks, step):
    size = lax.axis_size("ctx")
    order = ring_members(slot_blocks)
    pairs = []
    for base in range(0, size, slot_blocks):
        for place in range(slot_blocks):
            pairs.append((base + order[place], base + order[(place + step) % slot_blocks]))
    return lax.ppermute(value, "ctx", pairs)


def ring_step(left, right, slots):
    return ring_shift(left, slots, 1), ring_shift(right, slots, -1)


def ring_last(left, right, slots):
    rows = left.shape[0]
    top, low = ring_step(left[: rows // 2], right[rows // 2 :], slots)
    return top, low


def slot_code(rank, slots):
    bits = slots.bit_length() - 1
    code = 0
    for bit in range(bits):
        code = code | (((rank >> bit) & 1) << (bits - 1 - bit))
    return code


class SlotSum:
    def __init__(self, *terms):
        self.terms, self.stage = terms, 0
        self.send()

    def send(self):
        self.half = self.terms[0].shape[0] // 2
        self.sent = plus(*[term[self.half :] for term in self.terms])
        self.got = swap(self.sent, "ctx", 1 << self.stage)

    def step(self, *tokens):
        got = after(self.got, *tokens) if tokens else self.got
        self.terms = [term[: self.half] for term in self.terms] + [got]
        self.stage += 1
        if self.half > 1:
            self.send()
        return self.sent

    def finish(self):
        while self.half > 1:
            self.step()
        self.step()
        return plus(*[term[0] for term in self.terms])


def plus_wide(*terms):
    total = terms[0].astype(F32)
    for term in terms[1:]:
        total = total + term.astype(F32)
    return total


def plus(*terms):
    return plus_wide(*terms).astype(BF16)


class CtxSum:
    def __init__(self, parts, order, size):
        self.parts, self.order, self.size = parts, order, size
        self.stage, self.got, self.sent = 0, [], parts[0]
        self.give()

    def give(self, *tokens):
        if tokens:
            self.sent = after(self.sent, *tokens)
        bits = self.order + self.order[::-1]
        self.got.append(swap(self.sent, "ctx", 1 << bits[self.stage]))
        return self.sent

    def take(self, *tokens):
        _, second, third, own = self.parts
        got = self.got
        if tokens:
            got[-1] = after(got[-1], *tokens)
        self.stage += 1
        if self.stage == 1:
            self.sent = plus(second, got[0][2:])
        elif self.stage == 2:
            self.sent = plus(third, got[0][1:2], got[1][1:])
        elif self.stage == 3:
            own = plus(own, got[0][:1], got[1][:1], got[2])
            for bit in range(self.size.bit_length() - 1):
                if bit not in self.order:
                    own = plus(own, swap(own, "ctx", 1 << bit))
            self.sent = own
        else:
            self.sent = jnp.concatenate([self.sent, got[-1]], axis=0)
        return self.sent

    def step(self, *tokens):
        self.take(*tokens)
        return self.give()

    def finish(self):
        while self.stage < 5:
            self.step()
        return self.sent, self.got[5]


def code_of(rank, order):
    return (((rank >> order[0]) & 1) << 2) | (((rank >> order[1]) & 1) << 1) | ((rank >> order[2]) & 1)


def place_of(rank, slots):
    return jnp.where(rank % 2 == 0, rank // 2, slots - 1 - rank // 2)


def slot_of(rank, other, slots):
    if slots == 1:
        return 0
    ahead = lax.rem(place_of(other, slots) - place_of(rank, slots) + slots, slots)
    return jnp.where(ahead <= slots // 2, 2 * ahead - (ahead == slots // 2).astype(jnp.int32), 2 * (slots - ahead) - 1)


def score_mask(first_key, first_query, length, rows, width):
    key = first_key + lax.broadcasted_iota(jnp.int32, (rows, width), 0)
    query = first_query + lax.rem(lax.broadcasted_iota(jnp.int32, (rows, width), 1), rows)
    return (key <= query) & (key < length)


def head_row(head, member):
    mask = (head // (NH // 4)) ^ member
    return (((mask & 1) * 2 + (mask >> 1)) * (NH // 4) + head % (NH // 4)) * HD


def other_of(rank, slot, slots):
    step = (slot + 1) // 2
    place = lax.rem(place_of(rank, slots) + (slots - step if slot % 2 else step), slots)
    return jnp.where(place < slots // 2, 2 * place, 2 * (slots - 1 - place) + 1)


def forward_kernel(slots, here, first, last, meta, q_ref, wk_ref, wv_ref, *rest):
    c_refs, rest = rest[: len(here)], rest[len(here) :]
    ins, rest = ((), rest) if first else (rest[:3], rest[3:])
    outs, rest = rest[:3], rest[3:]
    c_ref, ct_ref, ql_ref, m_ref, l_ref, acc_ref, index_ref = rest
    rows = q_ref.shape[1]
    rank, length, member = meta[0], meta[1], meta[2]
    group = pl.program_id(0)
    first_query = rank * rows
    active = first_query < length
    count = jnp.int32(0)
    for k, slot in enumerate(here):
        if slot == 0:
            need = active
        else:
            other = other_of(rank, slot, slots)
            need = active & (other < rank)
            index_ref[count] = jnp.int32(k)
            count = count + need.astype(jnp.int32)

        @pl.when(need)
        def _():
            block = c_refs[k][...]
            c_ref[k] = block
            ct_ref[k] = block.T

    if first:
        m_ref[...] = jnp.full_like(m_ref, NEGATIVE)
        l_ref[...] = jnp.zeros_like(l_ref)
        acc_ref[...] = jnp.zeros_like(acc_ref)
    else:
        m_ref[...] = ins[0][0]
        l_ref[...] = ins[1][0]
        acc_ref[...] = ins[2][0]

    @pl.when(active)
    def _():
        for i in range(HPG):
            part = pl.ds(i * HD, HD)
            row = pl.ds(pl.multiple_of(head_row(group * HPG + i, member), HD), HD)
            latent_q = dot(wk_ref[row, :], q_ref[part, :], ((0,), (0,))).astype(BF16)
            ql_ref[:, i * rows : (i + 1) * rows] = latent_q * jnp.asarray(HD ** -0.5, BF16)
        if first:
            scores = dot(c_ref[0], ql_ref[...])
            allowed = score_mask(first_query, first_query, length, rows, HPG * rows)
            scores = jnp.where(allowed, scores, NEGATIVE)
            best = jnp.max(scores, axis=0, keepdims=True)
            weights = jnp.where(allowed, jnp.exp(scores - best), 0.0)
            m_ref[...] = best
            l_ref[...] = jnp.sum(weights, axis=0, keepdims=True)
            acc_ref[...] = dot(ct_ref[0], weights.astype(BF16))

        def blocks(*which):
            scores = [dot(c_ref[k], ql_ref[...]) for k in which]
            best = m_ref[...]
            for each in scores:
                best = jnp.maximum(best, jnp.max(each, axis=0, keepdims=True))
            factor = jnp.exp(m_ref[...] - best)
            total = l_ref[...] * factor
            added = None
            for k, each in zip(which, scores):
                weights = jnp.exp(each - best)
                total = total + jnp.sum(weights, axis=0, keepdims=True)
                term = dot(ct_ref[k], weights.astype(BF16))
                added = term if added is None else added + term
            m_ref[...] = best
            l_ref[...] = total
            acc_ref[...] = acc_ref[...] * factor + added

        def loop(step, carry):
            blocks(index_ref[2 * step], index_ref[2 * step + 1])
            return carry

        lax.fori_loop(0, count // 2, loop, 0)

        @pl.when(count % 2 == 1)
        def _():
            blocks(index_ref[count - 1])

    if not last:
        outs[0][0] = m_ref[...]
        outs[1][0] = l_ref[...]
        outs[2][0] = acc_ref[...]
        return
    att_ref, ol_ref, lse_ref = outs
    total = l_ref[...]
    seen = total > 0.0
    safe = jnp.where(seen, total, 1.0)
    lse_all = jnp.where(seen, m_ref[...] + jnp.log(safe), 0.0)
    mixture = (acc_ref[...] * (1.0 / safe)).astype(BF16)
    for i in range(HPG):
        row = pl.ds(pl.multiple_of(head_row(group * HPG + i, member), HD), HD)
        cols = slice(i * rows, (i + 1) * rows)
        lse_ref[i] = lse_all[:, cols]
        ol_ref[i] = mixture[:, cols]
        att_ref[row, :] = dot(wv_ref[row, :], mixture[:, cols]).astype(BF16)


def backward_kernel(slots, meta, q_ref, da_ref, wk_ref, wv_ref, c_ref, ol_ref, lse_ref,
                    dq_ref, dwk_ref, dwv_ref, dc_ref,
                    ct_ref, left_ref, dql_ref, lse_all, delta_ref):
    rows = q_ref.shape[1]
    width = HB * rows
    rank, length = meta[0], meta[1]
    first_query = rank * rows
    scale = jnp.asarray(HD ** -0.5, BF16)
    active = first_query < length
    place_of_block = lambda block: slot_code(rank, slots) ^ slot_code(block, slots)

    def clear(block, carry):
        dc_ref[place_of_block(block)] = jnp.zeros((rows, LAT), BF16)
        return carry

    lax.fori_loop(jnp.where(active, rank + 1, 0), slots, clear, 0)

    @pl.when(jnp.logical_not(active))
    def _():
        dql_ref[...] = jnp.zeros_like(dql_ref)

    @pl.when(active)
    def _():
        def turn(block, carry):
            ct_ref[block] = c_ref[slot_of(rank, block, slots)].T
            return carry

        lax.fori_loop(0, rank + 1, turn, 0)
        for i in range(HB):
            part = pl.ds(i * HD, HD)
            cols = slice(i * rows, (i + 1) * rows)
            left_ref[:, cols] = dot(wk_ref[part, :], q_ref[part, :], ((0,), (0,))).astype(BF16) * scale
            dol_t = dot(wv_ref[part, :], da_ref[part, :], ((0,), (0,))).astype(BF16)
            left_ref[:, width + i * rows : width + (i + 1) * rows] = dol_t
            delta_ref[:, cols] = jnp.sum(dol_t.astype(F32) * ol_ref[i].astype(F32), axis=0, keepdims=True)
            lse_all[:, cols] = lse_ref[i]

        def grads(block, allowed):
            pair = dot(c_ref[slot_of(rank, block, slots)], left_ref[...])
            probs = jnp.exp(pair[:, :width] - lse_all[...])
            if allowed is not None:
                probs = jnp.where(allowed, probs, 0.0)
            score_grad = (probs * (pair[:, width:] - delta_ref[...])).astype(BF16)
            both = ((1,), (1,))
            dc_ref[place_of_block(block)] = (
                dot(score_grad, left_ref[:, :width], both) + dot(probs.astype(BF16), left_ref[:, width:], both)
            ).astype(BF16)
            return dot(ct_ref[block], score_grad)

        dql_ref[...] = grads(rank, score_mask(first_query, first_query, length, rows, width))

        def loop(block, carry):
            dql_ref[...] += grads(block, None)
            return carry

        lax.fori_loop(0, rank, loop, 0)

    for i in range(HB):
        part = pl.ds(i * HD, HD)
        latent_grad = (dql_ref[:, i * rows : (i + 1) * rows] * (HD ** -0.5)).astype(BF16)
        dq_ref[part, :] = dot(wk_ref[part, :], latent_grad).astype(BF16)
        dwk_ref[part, :] = dot(q_ref[part, :], latent_grad, ((1,), (1,))).astype(BF16)
        dwv_ref[part, :] = dot(da_ref[part, :], ol_ref[i], ((1,), (1,))).astype(BF16)


def outside(value):
    return pltpu.with_memory_space_constraint(value, pltpu.HBM)


def once(shape, index):
    return pl.BlockSpec(shape, index, pipeline_mode=pl.Buffered(1))


def head_place(step, member):
    per_piece = NH // 4 // HB
    mask = (step // per_piece) ^ member
    return ((mask & 1) * 2 + (mask >> 1)) * per_piece + step % per_piece


def attention_forward(meta, q_t, wk, wv, pieces, here, slots, state=None, last=True):
    rows = q_t.shape[1]
    first = state is None
    wide = HPG * rows
    by_group = lambda g, meta: (g, 0, 0)
    if last:
        out_specs = [
            pl.BlockSpec((NH * HD, rows), lambda g, meta: (0, 0)),
            pl.BlockSpec((HPG, LAT, rows), by_group),
            pl.BlockSpec((HPG, 1, rows), by_group),
        ]
        out_shape = [
            jax.ShapeDtypeStruct((NH * HD, rows), BF16),
            pltpu.HBM((NH, LAT, rows), BF16),
            jax.ShapeDtypeStruct((NH, 1, rows), F32),
        ]
    else:
        out_specs = [pl.BlockSpec((1, n, wide), by_group) for n in (1, 1, LAT)]
        out_shape = [jax.ShapeDtypeStruct((GRP, n, wide), F32) for n in (1, 1, LAT)]
    return pl.pallas_call(
        functools.partial(forward_kernel, slots, here, first, last),
        name="attention_forward",
        grid_spec=pltpu.PrefetchScalarGridSpec(
            num_scalar_prefetch=1,
            grid=(GRP,),
            in_specs=[
                pl.BlockSpec((HPG * HD, rows), lambda g, meta: (g, 0)),
                once((NH * HD, LAT), lambda g, meta: (0, 0)),
                once((NH * HD, LAT), lambda g, meta: (0, 0)),
            ]
            + [pl.BlockSpec((rows, LAT), lambda g, meta: (0, g))] * len(here)
            + ([] if first else [pl.BlockSpec((1, n, wide), by_group) for n in (1, 1, LAT)]),
            out_specs=out_specs,
            scratch_shapes=[
                pltpu.VMEM((len(here), rows, LAT), BF16),
                pltpu.VMEM((len(here), LAT, rows), BF16),
                pltpu.VMEM((LAT, wide), BF16),
                pltpu.VMEM((1, wide), F32),
                pltpu.VMEM((1, wide), F32),
                pltpu.VMEM((LAT, wide), F32),
                pltpu.SMEM((len(here) + 1,), jnp.int32),
            ],
        ),
        out_shape=out_shape,
        compiler_params=pltpu.CompilerParams(
            dimension_semantics=("arbitrary",), vmem_limit_bytes=32 << 20
        ),
    )(meta, q_t, wk, wv, *pieces, *(state or ()))


def attention_backward(part, meta, q_t, da_t, wk, wv, blocks, ol, lse):
    slots, rows, _ = blocks.shape
    group = part * HB // HPG
    own = lambda s, meta: (part, 0)
    placed = lambda s, meta: (head_place(part, meta[2]), 0)
    first = lambda s, meta: (0, 0)
    all_slots = lambda s, meta: (0, 0, 0)
    width = HB * HD
    return pl.pallas_call(
        functools.partial(backward_kernel, slots),
        name="attention_backward",
        grid_spec=pltpu.PrefetchScalarGridSpec(
            num_scalar_prefetch=1,
            grid=(1,),
            in_specs=[
                once((width, rows), own),
                once((width, rows), placed),
                once((width, LAT), placed),
                once((width, LAT), placed),
                once((slots, rows, LAT), lambda s, meta: (0, 0, group)),
                once((HB, LAT, rows), lambda s, meta: (part, 0, 0)),
                once((HB, 1, rows), lambda s, meta: (part, 0, 0)),
            ],
            out_specs=[
                once((width, rows), first),
                once((width, LAT), first),
                once((width, LAT), first),
                once((slots, rows, LAT), all_slots),
            ],
            scratch_shapes=[
                pltpu.VMEM((slots, LAT, rows), BF16),
                pltpu.VMEM((LAT, 2 * HB * rows), BF16),
                pltpu.VMEM((LAT, HB * rows), F32),
                pltpu.VMEM((1, HB * rows), F32),
                pltpu.VMEM((1, HB * rows), F32),
            ],
        ),
        out_shape=[
            pltpu.HBM((width, rows), BF16),
            pltpu.HBM((width, LAT), BF16),
            pltpu.HBM((width, LAT), BF16),
            pltpu.HBM((slots, rows, LAT), BF16),
        ],
        compiler_params=pltpu.CompilerParams(
            dimension_semantics=("arbitrary",), vmem_limit_bytes=22 << 20
        ),
    )(meta, *[outside(v) for v in (q_t, da_t, wk, wv, blocks, ol)], lse)


def feed_kernel(h0, h1, df_ref, wg_ref, wu_ref, wd_ref, *outs):
    dh0, dh1, out0, out1, x_ref, hid_ref, dg_ref, du_ref = outs[-8:]
    rows = h0.shape[0]
    x_ref[:rows, :] = h0[...]
    x_ref[rows:, :] = h1[...]
    x = x_ref[...]
    gate = dot(wg_ref[...], x, ((1,), (1,)))
    up = dot(wu_ref[...], x, ((1,), (1,)))
    dhid = dot(wd_ref[...], df_ref[...], ((1,), (1,)))
    sig = jax.nn.sigmoid(gate)
    silu = gate * sig
    hid_ref[...] = (silu * up).astype(BF16)
    dg_ref[...] = (dhid * up * sig * (1.0 + gate * (1.0 - sig))).astype(BF16)
    du_ref[...] = (dhid * silu).astype(BF16)
    dh = (
        dot(dg_ref[...], wg_ref[...], ((0,), (0,))) + dot(du_ref[...], wu_ref[...], ((0,), (0,)))
    ).astype(BF16)
    dh0[...] = dh[:rows]
    dh1[...] = dh[rows:]
    out = dot(hid_ref[...], wd_ref[...], ((0,), (0,))).astype(BF16)
    out0[...] = out[:rows]
    out1[...] = out[rows:]


def feed_forward(half, pieces, df, w_gate, w_up, w_down, earlier=()):
    rows, width = pieces[0].shape
    ff = w_gate.shape[0]
    whole = lambda t: (0, 0)
    any_place = pl.BlockSpec(memory_space=pl.ANY)
    return pl.pallas_call(
        feed_kernel,
        name="feed_forward",
        grid=(1,),
        in_specs=[once((rows, width), whole)] * 2
        + [once((2 * rows, width), lambda t: (half, 0))]
        + [once((ff, width), whole)] * 3
        + [any_place] * len(earlier),
        out_specs=[once((rows, width), whole)] * 4
        + [once((2 * rows, width), lambda t: (half, 0))]
        + [once((ff, 2 * rows), lambda t: (0, half))] * 3,
        out_shape=[pltpu.HBM((rows, width), BF16)] * 4
        + [pltpu.HBM((4 * rows, width), BF16)]
        + [pltpu.HBM((ff, 4 * rows), BF16)] * 3,
        input_output_aliases={6 + k: 4 + k for k in range(len(earlier))},
        compiler_params=pltpu.CompilerParams(
            dimension_semantics=("arbitrary",), vmem_limit_bytes=48 << 20
        ),
    )(*pieces, df, w_gate, w_up, w_down, *earlier)


def feed_grad_kernel(which, count, codes, right_ref, *refs):
    lefts, (low_ref, high_ref, out_ref) = refs[:count], refs[count:]
    cut = right_ref.shape[1] // 4
    swapped = (codes[which] & 1) == 1
    half = pl.program_id(0)

    def loop(k, carry):
        inner = k ^ ((codes[which] >> 1) & 1)
        right = right_ref[:, pl.ds(pl.multiple_of(inner * 2 * cut, 2 * cut), 2 * cut)]
        for i, left in enumerate(lefts):
            both = dot(left[...], right).astype(BF16)
            sides = (
                jnp.where(swapped, both[:, cut:], both[:, :cut]),
                jnp.where(swapped, both[:, :cut], both[:, cut:]),
            )
            for side in range(2):
                place = 4 * half + 2 * k + side
                if count == 1:
                    out_ref[place] = sides[side]
                else:
                    out_ref[place, i] = sides[side]
        return carry

    lax.fori_loop(0, 2, loop, 0)

    @pl.when(half == 1)
    def _():
        low_ref[...] = out_ref[:4]
        high_ref[...] = out_ref[4:]


def feed_weight_grads(which, codes, lefts, right):
    ff, rows = lefts[0].shape
    cut = right.shape[1] // 8
    count = len(lefts)
    shape = (4, ff, cut) if count == 1 else (4, count, ff, cut)
    low, high = pl.pallas_call(
        functools.partial(feed_grad_kernel, which, count),
        name="feed_weight_grads",
        grid_spec=pltpu.PrefetchScalarGridSpec(
            num_scalar_prefetch=1,
            grid=(2,),
            in_specs=[pl.BlockSpec((rows, 4 * cut), lambda s, codes: (0, s ^ (codes[which] >> 2)))]
            + [once((ff, rows), lambda s, codes: (0, 0))] * count,
            out_specs=[once(shape, lambda s, codes: (0,) * len(shape))] * 2,
            scratch_shapes=[pltpu.VMEM((8,) + shape[1:], BF16)],
        ),
        out_shape=[pltpu.HBM(shape, BF16)] * 2,
        compiler_params=pltpu.CompilerParams(
            dimension_semantics=("arbitrary",), vmem_limit_bytes=40 << 20
        ),
    )(codes, *[outside(value) for value in (right, *lefts)])
    return high, low[2:], low[1:2], low[:1]


def join_kernel(which, by_rows, cuts, codes, near_ref, far_ref, *outs):
    tall, wide = near_ref.shape[-2:]

    def put(i, carry):
        position = i ^ codes[which]
        place = position & 3
        piece = jnp.where(position >= 4, far_ref[place].astype(F32), near_ref[place].astype(F32))
        rows = pl.ds(pl.multiple_of(i * tall, 8), tall)
        columns = pl.ds(pl.multiple_of(i * wide, wide), wide)
        if by_rows:
            low = 0
            for out, cut in zip(outs, cuts):
                out[rows, :] = piece[:, low : low + cut]
                low += cut
        elif len(outs) == 1:
            outs[0][:, columns] = piece
        else:
            for k, out in enumerate(outs):
                out[:, columns] = piece[k]
        return carry

    lax.fori_loop(0, 8, put, 0)


def join(which, codes, near, far, cuts=None):
    tall, wide = near.shape[-2:]
    vmem = pl.BlockSpec(memory_space=pltpu.VMEM)
    if cuts:
        shapes = [jax.ShapeDtypeStruct((8 * tall, cut), F32) for cut in cuts]
    else:
        shapes = [jax.ShapeDtypeStruct((tall, 8 * wide), F32)] * (near.shape[1] if near.ndim == 4 else 1)
    return pl.pallas_call(
        functools.partial(join_kernel, which, bool(cuts), cuts),
        name="join_pieces",
        in_specs=[pl.BlockSpec(memory_space=pltpu.SMEM), vmem, vmem],
        out_specs=[vmem] * len(shapes),
        out_shape=shapes,
        compiler_params=pltpu.CompilerParams(vmem_limit_bytes=20 << 20),
    )(codes, near, far)


def spread_kernel(which, contracts, codes, *refs):
    jobs, refs = refs[: 2 * len(contracts)], refs[2 * len(contracts) :]
    heads, (last_ref, near_ref, own_ref, acc_ref, head_ref) = refs[:-5], refs[-5:]
    cut = near_ref.shape[1]

    def put(low, width, take):
        def place(position, carry):
            start = pl.multiple_of((position ^ codes[which]) * cut, cut)
            for t in range(4):
                value = take(t, start)
                if t >= 2:
                    last_ref[t - 2, position, :, low : low + width] = value
                else:
                    (own_ref, near_ref)[t][position, :, low : low + width] = value
            return carry

        lax.fori_loop(0, 8, place, 0)

    low = 0
    for i, contract in enumerate(contracts):
        right = jobs[2 * i + 1]
        width = right.shape[1 - contract[1][0]]
        acc_ref[:, :width] = dot(jobs[2 * i][...], right[...], contract)
        put(low, width, lambda t, start: acc_ref[pl.ds(t * 8 * cut + start, cut), :width].astype(BF16))
        low += width
    if heads:
        for p in range(4):
            mask = p ^ codes[2]
            place = (mask & 1) * 2 + (mask >> 1)
            head_ref[place, :, :LAT] = heads[2 * p][...]
            head_ref[place, :, LAT:] = heads[2 * p + 1][...]
        put(low, 2 * LAT, lambda t, start: head_ref[t, pl.ds(start, cut), :])


def spread_product(which, codes, jobs, heads=()):
    tall = jobs[0][0].shape[1 - jobs[0][2][0][0]]
    widths = [right.shape[1 - contract[1][0]] for _, right, contract in jobs]
    wide = sum(widths) + (2 * LAT if heads else 0)
    cut = tall // 32
    vmem = pl.BlockSpec(memory_space=pltpu.VMEM)
    operands = [x for left, right, _ in jobs for x in (left, right)] + list(heads)
    return pl.pallas_call(
        functools.partial(spread_kernel, which, [contract for _, _, contract in jobs]),
        name="spread_product",
        in_specs=[pl.BlockSpec(memory_space=pltpu.SMEM)] + [vmem] * len(operands),
        out_specs=[vmem] * 3,
        scratch_shapes=[pltpu.VMEM((tall, max(widths)), F32), pltpu.VMEM((4, tall // 4, 2 * LAT), BF16)],
        out_shape=[
            pltpu.HBM((2, 8, cut, wide), BF16),
            pltpu.HBM((8, cut, wide), BF16),
            pltpu.HBM((8, cut, wide), BF16),
        ],
        compiler_params=pltpu.CompilerParams(vmem_limit_bytes=20 << 20),
    )(codes, *operands)


class ShardSum:
    def __init__(self, last, near, own):
        self.near, self.own = near, own
        self.beside = swap(last, "fsdp", 1)

    def step(self, *tokens):
        self.beside = after(self.beside, *tokens) if tokens else self.beside
        sent = plus(self.near, self.beside[1])
        self.across = swap(sent, "fsdp", 2)
        return sent

    def part(self, low, high):
        return plus(self.own[low:high], self.beside[0, low:high], self.across[low:high])


def four_parts(part):
    return part(4, 8), part(2, 4), part(1, 2), part(0, 1)


def on_device(
    tokens,
    out_grad,
    lengths,
    norm1_gain,
    w_query,
    w_latent,
    w_key_up,
    w_value_up,
    w_output,
    norm2_gain,
    w_gate,
    w_up,
    w_down,
):
    ctx_size = lax.axis_size("ctx")
    tok_rows, width = tokens.shape[1], tokens.shape[2]
    ff = w_gate.shape[1]
    group_rows = tok_rows * ctx_size
    seq_rows = min(SEQ_MAX, group_rows)
    slots = seq_rows // tok_rows
    ctx_rank = lax.axis_index("ctx")
    member = lax.axis_index("fsdp")
    slot_number = ctx_rank // slots
    rank = ctx_rank % slots
    length = jnp.sum(
        jnp.where(jnp.arange(lengths.shape[1], dtype=jnp.int32) == slot_number, lengths[0], 0)
    )
    meta = jnp.stack([rank, length, member]).astype(jnp.int32)
    query_pos = rank * tok_rows + jnp.arange(tok_rows, dtype=jnp.int32)
    row_valid = (query_pos < length).astype(F32)[:, None]
    piece = width // 4
    order_a, order_b = (0, 1, 2), (1, 2, 0)
    codes = jnp.stack([code_of(ctx_rank, order_a), code_of(ctx_rank, order_b), member, 0 * member]).astype(jnp.int32)

    def reorder(value):
        return jnp.concatenate(
            [lax.dynamic_slice_in_dim(value, (member ^ m) * piece, piece, 1) for m in ORDER], axis=1
        )

    def restore(value):
        back = {m: t for t, m in enumerate(ORDER)}
        parts = [value[:, back[m] * piece : (back[m] + 1) * piece] for m in range(4)]
        low = (member & 1) == 1
        parts = [jnp.where(low, parts[j ^ 1], parts[j]) for j in range(4)]
        high = (member & 2) == 2
        parts = [jnp.where(high, parts[j ^ 2], parts[j]) for j in range(4)]
        return jnp.concatenate(parts, axis=1)

    latent_full = gather_rows(w_latent)
    gains = gather_rows(jnp.stack([norm1_gain, norm2_gain])[None])
    gain_one = jnp.concatenate([gains[t, 0] for t in range(4)])
    gain_two = restore(jnp.concatenate([gains[t, 1:] for t in range(4)], axis=1))
    gain_one_f = gain_one.astype(F32)
    gain_two_f = gain_two.astype(F32)
    inputs = tokens[0].astype(F32)
    mixed_in = reorder(tokens[0]).astype(F32)
    scale_one = norm_scale(inputs)
    normed_one = mixed_in * scale_one
    normed = (normed_one * gain_one_f).astype(BF16)
    latent = dot(normed, latent_full).astype(BF16)
    pieces = [latent]
    left, right = latent, latent
    side = jnp.concatenate([w_key_up, w_value_up], axis=1)
    weights = [after(w_query, latent_full), after(side, latent_full)]
    for _ in range(min(2, slots // 2 - 1)):
        left, right = ring_step(left, right, slots)
        pieces += [left, right]
    query_full = gather_rows(weights[0], *pieces[1:3])
    side_full = gather_rows(weights[1], *pieces[-2:])
    near = tuple(range(len(pieces)))
    key_full, value_full = side_full[:, :LAT], side_full[:, LAT:]
    q_t = dot(query_full, normed, ((0,), (1,))).astype(BF16)
    if len(pieces) < slots - 1:
        left, right = ring_step(left, right, slots)
        state = attention_forward(meta, q_t, key_full, value_full, pieces, near, slots, None, False)
        left, right = after((left, right), state[0])
        pieces += [left, right]
        while len(pieces) < slots - 1:
            left, right = ring_step(left, right, slots)
            pieces += [left, right]
    else:
        state = attention_forward(meta, q_t, key_full, value_full, pieces, near, slots, None, False)
    pieces.append(jnp.concatenate(ring_last(left, right, slots), axis=0))
    far = tuple(range(len(near), slots))
    att_t, mixture, log_total = attention_forward(
        meta, q_t, key_full, value_full, [pieces[k] for k in far], far, slots, state, True
    )
    blocks = jnp.stack(pieces)
    output_full = gather_rows(after(w_output, q_t), state[0])
    cotangent = out_grad[0].astype(F32) * row_valid
    feed_grad = gather_rows(after(cotangent.astype(BF16), q_t), state[0]).reshape(2, 2, tok_rows, width)
    feed_grad = jnp.swapaxes(feed_grad, 0, 1).reshape(4 * tok_rows, width)
    middle = inputs + dot(att_t, output_full, ((0,), (0,)))
    scale_two = norm_scale(middle)
    normed_two_raw = middle * scale_two
    normed_two = (normed_two_raw * gain_two_f).astype(BF16)
    gate_rows, up_rows = w_gate.T, w_up.T
    far_rows = swap(normed_two, "fsdp", 2)
    near_rows = swap(normed_two, "fsdp", 1)
    first = feed_forward(0, [after(normed_two, blocks), near_rows], feed_grad, gate_rows, up_rows, w_down)
    far_rows = after(far_rows, first[0])
    both_rows = swap(far_rows, "fsdp", 1)
    second = feed_forward(1, [far_rows, both_rows], feed_grad, gate_rows, up_rows, w_down, first[4:])
    normed_two_part = [first[0], second[0], jnp.stack([first[1], second[1]])]
    feed_part = [first[2], second[2], jnp.stack([first[3], second[3]])]
    ff_in, hidden = second[4], second[5:]
    beside = swap(normed_two_part[2], "fsdp", 1)
    wide_parts = feed_weight_grads(0, codes, hidden[1:], ff_in)
    wide_sum = CtxSum(wide_parts, order_a, ctx_size)
    beside = after(beside, wide_parts[0])
    home = plus(normed_two_part[1], beside[1])
    across = swap(home, "fsdp", 2)
    down_parts = feed_weight_grads(1, codes, hidden[:1], after(feed_grad, home))
    down_sum = CtxSum(down_parts, order_b, ctx_size)
    across = after(across, down_parts[0])
    normed_two_grad = (
        normed_two_part[0].astype(F32) + beside[0].astype(F32) + across.astype(F32)
    )
    middle_grad = cotangent + norm_back(normed_two_grad, normed_two_raw, scale_two, gain_two_f)
    gain_two_terms = reorder((normed_two_grad * normed_two_raw).astype(BF16))
    branch_grad = middle_grad.astype(BF16)
    da_t = dot(output_full, branch_grad, ((1,), (1,))).astype(BF16)

    def back(part, *tokens):
        return attention_backward(
            part, meta, q_t, after(da_t, *tokens), key_full, value_full, blocks, mixture, log_total
        )

    nn, tn = ((1,), (0,)), ((0,), (0,))
    back_0 = back(0, wide_sum.sent, down_sum.sent)
    token = back_0[0]
    gates = [down_sum.step(token), wide_sum.step(token)]
    feed_part = after(feed_part, token)
    feed_beside = swap(feed_part[2], "fsdp", 1)
    back_1 = back(1, *gates)
    token = back_1[0]
    tt = ((0,), (1,))
    early_shards = ShardSum(
        *spread_product(
            1,
            codes,
            [
                (att_t, after(branch_grad, token), nn),
                (normed, back_0[0], tt),
                (normed, token, tt),
                (gain_two_terms, jnp.ones((tok_rows, 128), BF16), tn),
            ],
        )
    )
    sum_0 = SlotSum(back_0[3], back_1[3])
    gates = [down_sum.step(token), wide_sum.step(token)]
    gates.append(down_sum.step(early_shards.own))
    feed_home = plus(feed_part[1], after(feed_beside, token)[1])
    feed_across = swap(feed_home, "fsdp", 2)
    back_2 = back(2, sum_0.sent, early_shards.own, feed_home, *gates)
    token = back_2[0]
    gates = [sum_0.step(token), early_shards.step(token), down_sum.step(token), wide_sum.step(token)]
    back_3 = back(3, *gates)
    backward = [back_0, back_1, back_2, back_3]

    clock = [back_3[0]]

    def tick(value):
        clock[0] = value

    def ready(each):
        each.across = after(each.across, clock[0])

    sum_1 = SlotSum(back_2[3], back_3[3])
    ready(early_shards)
    early_sum = CtxSum(four_parts(early_shards.part), order_b, ctx_size)
    tick(early_sum.sent)
    heads = [x for part in backward for x in (part[1], part[2])]
    late_shards = ShardSum(
        *spread_product(0, codes, [(normed, back_2[0], tt), (normed, after(back_3[0], sum_1.sent), tt)], heads)
    )
    tick(late_shards.own)
    feed_out = plus_wide(feed_part[0], feed_beside[0], after(feed_across, clock[0]))
    result = ((middle + feed_out) * row_valid).astype(BF16)
    tick(result)
    tick(down_sum.take(clock[0]))
    tick(sum_0.step(clock[0]))
    tick(late_shards.step(clock[0]))
    tick(wide_sum.take(clock[0]))
    tick(early_sum.step(clock[0]))
    tick(sum_1.step(clock[0]))
    tick(wide_sum.give(clock[0]))
    sum_0.got = after(sum_0.got, clock[0])
    latent_0 = sum_0.finish()
    tick(latent_0)
    tick(early_sum.step(clock[0]))
    tick(sum_1.step(clock[0]))
    tick(down_sum.give(clock[0]))
    ready(late_shards)
    late_sum = CtxSum(four_parts(late_shards.part), order_a, ctx_size)
    tick(late_sum.sent)
    tick(early_sum.step(clock[0]))
    sum_1.got = after(sum_1.got, clock[0])
    latent_grad = jnp.concatenate([latent_0, sum_1.finish()], axis=1)
    latent_shards = ShardSum(*spread_product(1, codes, [(normed, latent_grad, tn)]))
    tick(latent_shards.step(latent_grad))
    tick(early_sum.step(clock[0]))
    tick(late_sum.step(clock[0]))
    tick(wide_sum.step(clock[0]))
    tick(early_sum.step(clock[0]))
    ready(latent_shards)
    latent_sum = CtxSum(four_parts(latent_shards.part), order_b, ctx_size)
    tick(latent_sum.sent)

    def tick_join(which, done, cuts=None):
        near_part, far_part = done.finish()
        out = join(which, codes, near_part, after(far_part, clock[0]), cuts)
        tick(out[0])
        return out

    half = NH * HD // 2
    tick(late_sum.step(clock[0]))
    tick(latent_sum.step(clock[0]))
    (down_grad,) = tick_join(1, down_sum)
    tick(late_sum.step(clock[0]))
    tick(latent_sum.step(clock[0]))
    output_grad, query_grad_0, gain_two_grad = tick_join(1, early_sum, (width, half, 128))
    tick(late_sum.step(clock[0]))
    tick(latent_sum.step(clock[0]))
    tick(late_sum.step(clock[0]))
    tick(latent_sum.step(clock[0]))
    gate_w_grad, up_w_grad = tick_join(0, wide_sum)
    tick(latent_sum.step(clock[0]))
    query_grad_1, key_grad, value_grad = tick_join(0, late_sum, (half, LAT, LAT))
    query_grad = jnp.concatenate([query_grad_0, query_grad_1], axis=1)
    (latent_w_grad,) = tick_join(1, latent_sum, (GRP * LAT,))
    dq_t = jnp.concatenate([part[0] for part in backward], axis=0)

    normed_grad = dot(dq_t, query_full, ((0,), (1,))) + dot(
        latent_grad, latent_full, ((1,), (1,))
    )
    input_grad = middle_grad + restore(
        norm_back(normed_grad, normed_one, scale_one, gain_one_f)
    )
    gain_one_grad = (
        jnp.sum(w_query.astype(F32) * query_grad, axis=1)
        + jnp.sum(w_latent.astype(F32) * latent_w_grad, axis=1)
    ) / norm1_gain.astype(F32)
    return (
        result[None],
        input_grad[None],
        gain_one_grad,
        query_grad,
        latent_w_grad,
        key_grad,
        value_grad,
        output_grad,
        gain_two_grad[:, 0],
        gate_w_grad.T,
        up_w_grad.T,
        down_grad,
    )


def solution(mesh):
    rows = P("fsdp", None)
    cols = P(None, "fsdp")
    toks = P("fsdp", "ctx", None)
    vec = P("fsdp")
    return jax.shard_map(
        on_device,
        mesh=mesh,
        in_specs=(toks, toks, rows, vec, rows, rows, rows, rows, rows, vec, cols, cols, rows),
        out_specs=(toks, toks, vec, rows, rows, rows, rows, rows, vec, cols, cols, rows),
        check_vma=False,
    )
```

```python
import functools

import jax
import jax.numpy as jnp
from jax import lax
from jax.experimental import pallas as pl
from jax.experimental.pallas import tpu as pltpu
from jax.sharding import PartitionSpec as P

NH = 16
HD = 64
LAT = 256
GRP = 2
SEQ_MAX = 4096
EPS = 1e-06
NEGATIVE = -1e30
HPG = NH // GRP
HB = 4
ORDER = (0, 2, 1, 3)
F32 = jnp.float32
BF16 = jnp.bfloat16


def dot(left, right, contract=((1,), (0,))):
    return lax.dot_general(left, right, (contract, ((), ())), preferred_element_type=F32)


def after(value, *tokens):
    return lax.optimization_barrier((value, tokens))[0]


def norm_scale(values):
    return lax.rsqrt(jnp.mean(values * values, axis=-1, keepdims=True) + EPS)


def norm_back(grad_in, normed, scale_rows, gain_full):
    scaled = grad_in * gain_full
    return scale_rows * (scaled - normed * jnp.mean(scaled * normed, axis=-1, keepdims=True))


def swap(value, axis, mask):
    size = lax.axis_size(axis)
    return lax.ppermute(value, axis, [(s, s ^ mask) for s in range(size)])


def gather_four(value, *tokens):
    across = swap(value, "fsdp", 2)
    beside = swap(value, "fsdp", 1)
    if tokens:
        across, beside = after((across, beside), *tokens)
    both = swap(across, "fsdp", 1)
    return [value, across, beside, both]


def gather_rows(value, *tokens):
    across = swap(value, "fsdp", 2)
    two = jnp.concatenate([value, after(across, *tokens) if tokens else across], axis=0)
    return jnp.concatenate([two, swap(two, "fsdp", 1)], axis=0)


def scatter_four(first_two, last_two):
    got = swap(last_two, "fsdp", 1)
    near = first_two.astype(F32) + got.astype(F32)
    far = swap(near[1].astype(BF16), "fsdp", 2)
    return near[0] + far.astype(F32)


def ring_members(count):
    return list(range(0, count, 2)) + list(range(count - 1, 0, -2)) if count > 1 else [0]


def ring_shift(value, slot_blocks, step):
    size = lax.axis_size("ctx")
    order = ring_members(slot_blocks)
    pairs = []
    for base in range(0, size, slot_blocks):
        for place in range(slot_blocks):
            pairs.append((base + order[place], base + order[(place + step) % slot_blocks]))
    return lax.ppermute(value, "ctx", pairs)


def ring_step(left, right, slots):
    return ring_shift(left, slots, 1), ring_shift(right, slots, -1)


def ring_last(left, right, slots):
    rows = left.shape[0]
    top, low = ring_step(left[: rows // 2], right[rows // 2 :], slots)
    return top, low


def slot_code(rank, slots):
    bits = slots.bit_length() - 1
    code = 0
    for bit in range(bits):
        code = code | (((rank >> bit) & 1) << (bits - 1 - bit))
    return code


class SlotSum:
    def __init__(self, *terms):
        self.terms, self.stage = terms, 0
        self.send()

    def send(self):
        self.half = self.terms[0].shape[0] // 2
        self.sent = plus(*[term[self.half :] for term in self.terms])
        self.got = swap(self.sent, "ctx", 1 << self.stage)

    def step(self, *tokens):
        got = after(self.got, *tokens) if tokens else self.got
        self.terms = [term[: self.half] for term in self.terms] + [got]
        self.stage += 1
        if self.half > 1:
            self.send()
        return self.sent

    def finish(self):
        while self.half > 1:
            self.step()
        self.step()
        return plus(*[term[0] for term in self.terms])


def plus_wide(*terms):
    total = terms[0].astype(F32)
    for term in terms[1:]:
        total = total + term.astype(F32)
    return total


def plus(*terms):
    return plus_wide(*terms).astype(BF16)


class CtxSum:
    def __init__(self, parts, order, size):
        self.parts, self.order, self.size = parts, order, size
        self.stage, self.got, self.sent = 0, [], parts[0]
        self.give()

    def give(self, *tokens):
        if tokens:
            self.sent = after(self.sent, *tokens)
        bits = self.order + self.order[::-1]
        self.got.append(swap(self.sent, "ctx", 1 << bits[self.stage]))
        return self.sent

    def take(self, *tokens):
        _, second, third, own = self.parts
        got = self.got
        if tokens:
            got[-1] = after(got[-1], *tokens)
        self.stage += 1
        if self.stage == 1:
            self.sent = plus(second, got[0][2:])
        elif self.stage == 2:
            self.sent = plus(third, got[0][1:2], got[1][1:])
        elif self.stage == 3:
            own = plus(own, got[0][:1], got[1][:1], got[2])
            for bit in range(self.size.bit_length() - 1):
                if bit not in self.order:
                    own = plus(own, swap(own, "ctx", 1 << bit))
            self.sent = own
        else:
            self.sent = jnp.concatenate([self.sent, got[-1]], axis=0)
        return self.sent

    def step(self, *tokens):
        self.take(*tokens)
        return self.give()

    def finish(self):
        while self.stage < 5:
            self.step()
        return self.sent, self.got[5]


def code_of(rank, order):
    return (((rank >> order[0]) & 1) << 2) | (((rank >> order[1]) & 1) << 1) | ((rank >> order[2]) & 1)


def place_of(rank, slots):
    return jnp.where(rank % 2 == 0, rank // 2, slots - 1 - rank // 2)


def slot_of(rank, other, slots):
    if slots == 1:
        return 0
    ahead = lax.rem(place_of(other, slots) - place_of(rank, slots) + slots, slots)
    return jnp.where(ahead <= slots // 2, 2 * ahead - (ahead == slots // 2).astype(jnp.int32), 2 * (slots - ahead) - 1)


def score_mask(first_key, first_query, length, rows, width):
    key = first_key + lax.broadcasted_iota(jnp.int32, (rows, width), 0)
    query = first_query + lax.rem(lax.broadcasted_iota(jnp.int32, (rows, width), 1), rows)
    return (key <= query) & (key < length)


def head_row(head, member):
    mask = (head // (NH // 4)) ^ member
    return (((mask & 1) * 2 + (mask >> 1)) * (NH // 4) + head % (NH // 4)) * HD


def other_of(rank, slot, slots):
    step = (slot + 1) // 2
    place = lax.rem(place_of(rank, slots) + (slots - step if slot % 2 else step), slots)
    return jnp.where(place < slots // 2, 2 * place, 2 * (slots - 1 - place) + 1)


def forward_kernel(slots, here, first, last, meta, q_ref, wk_ref, wv_ref, *rest):
    c_refs, rest = rest[: len(here)], rest[len(here) :]
    ins, rest = ((), rest) if first else (rest[:3], rest[3:])
    outs, rest = rest[:3], rest[3:]
    c_ref, ct_ref, ql_ref, m_ref, l_ref, acc_ref, index_ref = rest
    rows = q_ref.shape[1]
    rank, length, member = meta[0], meta[1], meta[2]
    group = pl.program_id(0)
    first_query = rank * rows
    active = first_query < length
    count = jnp.int32(0)
    for k, slot in enumerate(here):
        if slot == 0:
            need = active
        else:
            other = other_of(rank, slot, slots)
            need = active & (other < rank)
            index_ref[count] = jnp.int32(k)
            count = count + need.astype(jnp.int32)

        @pl.when(need)
        def _():
            block = c_refs[k][...]
            c_ref[k] = block
            ct_ref[k] = block.T

    if first:
        m_ref[...] = jnp.full_like(m_ref, NEGATIVE)
        l_ref[...] = jnp.zeros_like(l_ref)
        acc_ref[...] = jnp.zeros_like(acc_ref)
    else:
        m_ref[...] = ins[0][0]
        l_ref[...] = ins[1][0]
        acc_ref[...] = ins[2][0]

    @pl.when(active)
    def _():
        for i in range(HPG):
            part = pl.ds(i * HD, HD)
            row = pl.ds(pl.multiple_of(head_row(group * HPG + i, member), HD), HD)
            latent_q = dot(wk_ref[row, :], q_ref[part, :], ((0,), (0,))).astype(BF16)
            ql_ref[:, i * rows : (i + 1) * rows] = latent_q * jnp.asarray(HD ** -0.5, BF16)
        if first:
            scores = dot(c_ref[0], ql_ref[...])
            allowed = score_mask(first_query, first_query, length, rows, HPG * rows)
            scores = jnp.where(allowed, scores, NEGATIVE)
            best = jnp.max(scores, axis=0, keepdims=True)
            weights = jnp.where(allowed, jnp.exp(scores - best), 0.0)
            m_ref[...] = best
            l_ref[...] = jnp.sum(weights, axis=0, keepdims=True)
            acc_ref[...] = dot(ct_ref[0], weights.astype(BF16))

        def blocks(*which):
            scores = [dot(c_ref[k], ql_ref[...]) for k in which]
            best = m_ref[...]
            for each in scores:
                best = jnp.maximum(best, jnp.max(each, axis=0, keepdims=True))
            factor = jnp.exp(m_ref[...] - best)
            total = l_ref[...] * factor
            added = None
            for k, each in zip(which, scores):
                weights = jnp.exp(each - best)
                total = total + jnp.sum(weights, axis=0, keepdims=True)
                term = dot(ct_ref[k], weights.astype(BF16))
                added = term if added is None else added + term
            m_ref[...] = best
            l_ref[...] = total
            acc_ref[...] = acc_ref[...] * factor + added

        def loop(step, carry):
            blocks(index_ref[2 * step], index_ref[2 * step + 1])
            return carry

        lax.fori_loop(0, count // 2, loop, 0)

        @pl.when(count % 2 == 1)
        def _():
            blocks(index_ref[count - 1])

    if not last:
        outs[0][0] = m_ref[...]
        outs[1][0] = l_ref[...]
        outs[2][0] = acc_ref[...]
        return
    att_ref, ol_ref, lse_ref = outs
    total = l_ref[...]
    seen = total > 0.0
    safe = jnp.where(seen, total, 1.0)
    lse_all = jnp.where(seen, m_ref[...] + jnp.log(safe), 0.0)
    mixture = (acc_ref[...] * (1.0 / safe)).astype(BF16)
    for i in range(HPG):
        row = pl.ds(pl.multiple_of(head_row(group * HPG + i, member), HD), HD)
        cols = slice(i * rows, (i + 1) * rows)
        lse_ref[i] = lse_all[:, cols]
        ol_ref[i] = mixture[:, cols]
        att_ref[row, :] = dot(wv_ref[row, :], mixture[:, cols]).astype(BF16)


def backward_kernel(slots, meta, q_ref, da_ref, wk_ref, wv_ref, c_ref, ol_ref, lse_ref,
                    dq_ref, dwk_ref, dwv_ref, dc_ref,
                    ct_ref, left_ref, dql_ref, lse_all, delta_ref):
    rows = q_ref.shape[1]
    width = HB * rows
    rank, length = meta[0], meta[1]
    first_query = rank * rows
    scale = jnp.asarray(HD ** -0.5, BF16)
    active = first_query < length
    place_of_block = lambda block: slot_code(rank, slots) ^ slot_code(block, slots)

    def clear(block, carry):
        dc_ref[place_of_block(block)] = jnp.zeros((rows, LAT), BF16)
        return carry

    lax.fori_loop(jnp.where(active, rank + 1, 0), slots, clear, 0)

    @pl.when(jnp.logical_not(active))
    def _():
        dql_ref[...] = jnp.zeros_like(dql_ref)

    @pl.when(active)
    def _():
        def turn(block, carry):
            ct_ref[block] = c_ref[slot_of(rank, block, slots)].T
            return carry

        lax.fori_loop(0, rank + 1, turn, 0)
        for i in range(HB):
            part = pl.ds(i * HD, HD)
            cols = slice(i * rows, (i + 1) * rows)
            left_ref[:, cols] = dot(wk_ref[part, :], q_ref[part, :], ((0,), (0,))).astype(BF16) * scale
            dol_t = dot(wv_ref[part, :], da_ref[part, :], ((0,), (0,))).astype(BF16)
            left_ref[:, width + i * rows : width + (i + 1) * rows] = dol_t
            delta_ref[:, cols] = jnp.sum(dol_t.astype(F32) * ol_ref[i].astype(F32), axis=0, keepdims=True)
            lse_all[:, cols] = lse_ref[i]

        def grads(block, allowed):
            pair = dot(c_ref[slot_of(rank, block, slots)], left_ref[...])
            probs = jnp.exp(pair[:, :width] - lse_all[...])
            if allowed is not None:
                probs = jnp.where(allowed, probs, 0.0)
            score_grad = (probs * (pair[:, width:] - delta_ref[...])).astype(BF16)
            both = ((1,), (1,))
            dc_ref[place_of_block(block)] = (
                dot(score_grad, left_ref[:, :width], both) + dot(probs.astype(BF16), left_ref[:, width:], both)
            ).astype(BF16)
            return dot(ct_ref[block], score_grad)

        dql_ref[...] = grads(rank, score_mask(first_query, first_query, length, rows, width))

        def loop(block, carry):
            dql_ref[...] += grads(block, None)
            return carry

        lax.fori_loop(0, rank, loop, 0)

    for i in range(HB):
        part = pl.ds(i * HD, HD)
        latent_grad = (dql_ref[:, i * rows : (i + 1) * rows] * (HD ** -0.5)).astype(BF16)
        dq_ref[part, :] = dot(wk_ref[part, :], latent_grad).astype(BF16)
        dwk_ref[part, :] = dot(q_ref[part, :], latent_grad, ((1,), (1,))).astype(BF16)
        dwv_ref[part, :] = dot(da_ref[part, :], ol_ref[i], ((1,), (1,))).astype(BF16)


def outside(value):
    return pltpu.with_memory_space_constraint(value, pltpu.HBM)


def once(shape, index):
    return pl.BlockSpec(shape, index, pipeline_mode=pl.Buffered(1))


def head_place(step, member):
    per_piece = NH // 4 // HB
    mask = (step // per_piece) ^ member
    return ((mask & 1) * 2 + (mask >> 1)) * per_piece + step % per_piece


def attention_forward(meta, q_t, wk, wv, pieces, here, slots, state=None, last=True):
    rows = q_t.shape[1]
    first = state is None
    wide = HPG * rows
    by_group = lambda g, meta: (g, 0, 0)
    if last:
        out_specs = [
            pl.BlockSpec((NH * HD, rows), lambda g, meta: (0, 0)),
            pl.BlockSpec((HPG, LAT, rows), by_group),
            pl.BlockSpec((HPG, 1, rows), by_group),
        ]
        out_shape = [
            jax.ShapeDtypeStruct((NH * HD, rows), BF16),
            pltpu.HBM((NH, LAT, rows), BF16),
            jax.ShapeDtypeStruct((NH, 1, rows), F32),
        ]
    else:
        out_specs = [pl.BlockSpec((1, n, wide), by_group) for n in (1, 1, LAT)]
        out_shape = [jax.ShapeDtypeStruct((GRP, n, wide), F32) for n in (1, 1, LAT)]
    return pl.pallas_call(
        functools.partial(forward_kernel, slots, here, first, last),
        name="attention_forward",
        grid_spec=pltpu.PrefetchScalarGridSpec(
            num_scalar_prefetch=1,
            grid=(GRP,),
            in_specs=[
                pl.BlockSpec((HPG * HD, rows), lambda g, meta: (g, 0)),
                once((NH * HD, LAT), lambda g, meta: (0, 0)),
                once((NH * HD, LAT), lambda g, meta: (0, 0)),
            ]
            + [pl.BlockSpec((rows, LAT), lambda g, meta: (0, g))] * len(here)
            + ([] if first else [pl.BlockSpec((1, n, wide), by_group) for n in (1, 1, LAT)]),
            out_specs=out_specs,
            scratch_shapes=[
                pltpu.VMEM((len(here), rows, LAT), BF16),
                pltpu.VMEM((len(here), LAT, rows), BF16),
                pltpu.VMEM((LAT, wide), BF16),
                pltpu.VMEM((1, wide), F32),
                pltpu.VMEM((1, wide), F32),
                pltpu.VMEM((LAT, wide), F32),
                pltpu.SMEM((len(here) + 1,), jnp.int32),
            ],
        ),
        out_shape=out_shape,
        compiler_params=pltpu.CompilerParams(
            dimension_semantics=("arbitrary",), vmem_limit_bytes=32 << 20
        ),
    )(meta, q_t, wk, wv, *pieces, *(state or ()))


def attention_backward(part, meta, q_t, da_t, wk, wv, blocks, ol, lse):
    slots, rows, _ = blocks.shape
    group = part * HB // HPG
    own = lambda s, meta: (part, 0)
    placed = lambda s, meta: (head_place(part, meta[2]), 0)
    first = lambda s, meta: (0, 0)
    all_slots = lambda s, meta: (0, 0, 0)
    width = HB * HD
    return pl.pallas_call(
        functools.partial(backward_kernel, slots),
        name="attention_backward",
        grid_spec=pltpu.PrefetchScalarGridSpec(
            num_scalar_prefetch=1,
            grid=(1,),
            in_specs=[
                once((width, rows), own),
                once((width, rows), placed),
                once((width, LAT), placed),
                once((width, LAT), placed),
                once((slots, rows, LAT), lambda s, meta: (0, 0, group)),
                once((HB, LAT, rows), lambda s, meta: (part, 0, 0)),
                once((HB, 1, rows), lambda s, meta: (part, 0, 0)),
            ],
            out_specs=[
                once((width, rows), first),
                once((width, LAT), first),
                once((width, LAT), first),
                once((slots, rows, LAT), all_slots),
            ],
            scratch_shapes=[
                pltpu.VMEM((slots, LAT, rows), BF16),
                pltpu.VMEM((LAT, 2 * HB * rows), BF16),
                pltpu.VMEM((LAT, HB * rows), F32),
                pltpu.VMEM((1, HB * rows), F32),
                pltpu.VMEM((1, HB * rows), F32),
            ],
        ),
        out_shape=[
            pltpu.HBM((width, rows), BF16),
            pltpu.HBM((width, LAT), BF16),
            pltpu.HBM((width, LAT), BF16),
            pltpu.HBM((slots, rows, LAT), BF16),
        ],
        compiler_params=pltpu.CompilerParams(
            dimension_semantics=("arbitrary",), vmem_limit_bytes=22 << 20
        ),
    )(meta, *[outside(v) for v in (q_t, da_t, wk, wv, blocks, ol)], lse)


def feed_kernel(h0, h1, df_ref, wg_ref, wu_ref, wd_ref, *outs):
    dh0, dh1, out0, out1, x_ref, hid_ref, dg_ref, du_ref = outs[-8:]
    rows = h0.shape[0]
    x_ref[:rows, :] = h0[...]
    x_ref[rows:, :] = h1[...]
    x = x_ref[...]
    gate = dot(wg_ref[...], x, ((1,), (1,)))
    up = dot(wu_ref[...], x, ((1,), (1,)))
    dhid = dot(wd_ref[...], df_ref[...], ((1,), (1,)))
    sig = jax.nn.sigmoid(gate)
    silu = gate * sig
    hid_ref[...] = (silu * up).astype(BF16)
    dg_ref[...] = (dhid * up * sig * (1.0 + gate * (1.0 - sig))).astype(BF16)
    du_ref[...] = (dhid * silu).astype(BF16)
    dh = (
        dot(dg_ref[...], wg_ref[...], ((0,), (0,))) + dot(du_ref[...], wu_ref[...], ((0,), (0,)))
    ).astype(BF16)
    dh0[...] = dh[:rows]
    dh1[...] = dh[rows:]
    out = dot(hid_ref[...], wd_ref[...], ((0,), (0,))).astype(BF16)
    out0[...] = out[:rows]
    out1[...] = out[rows:]


def feed_forward(half, pieces, df, w_gate, w_up, w_down, earlier=()):
    rows, width = pieces[0].shape
    ff = w_gate.shape[0]
    whole = lambda t: (0, 0)
    any_place = pl.BlockSpec(memory_space=pl.ANY)
    return pl.pallas_call(
        feed_kernel,
        name="feed_forward",
        grid=(1,),
        in_specs=[once((rows, width), whole)] * 2
        + [once((2 * rows, width), lambda t: (half, 0))]
        + [once((ff, width), whole)] * 3
        + [any_place] * len(earlier),
        out_specs=[once((rows, width), whole)] * 4
        + [once((2 * rows, width), lambda t: (half, 0))]
        + [once((ff, 2 * rows), lambda t: (0, half))] * 3,
        out_shape=[pltpu.HBM((rows, width), BF16)] * 4
        + [pltpu.HBM((4 * rows, width), BF16)]
        + [pltpu.HBM((ff, 4 * rows), BF16)] * 3,
        input_output_aliases={6 + k: 4 + k for k in range(len(earlier))},
        compiler_params=pltpu.CompilerParams(
            dimension_semantics=("arbitrary",), vmem_limit_bytes=48 << 20
        ),
    )(*pieces, df, w_gate, w_up, w_down, *earlier)


def feed_grad_kernel(which, count, codes, right_ref, *refs):
    lefts, (low_ref, high_ref, out_ref) = refs[:count], refs[count:]
    cut = right_ref.shape[1] // 4
    swapped = (codes[which] & 1) == 1
    half = pl.program_id(0)

    def loop(k, carry):
        inner = k ^ ((codes[which] >> 1) & 1)
        right = right_ref[:, pl.ds(pl.multiple_of(inner * 2 * cut, 2 * cut), 2 * cut)]
        for i, left in enumerate(lefts):
            both = dot(left[...], right).astype(BF16)
            sides = (
                jnp.where(swapped, both[:, cut:], both[:, :cut]),
                jnp.where(swapped, both[:, :cut], both[:, cut:]),
            )
            for side in range(2):
                place = 4 * half + 2 * k + side
                if count == 1:
                    out_ref[place] = sides[side]
                else:
                    out_ref[place, i] = sides[side]
        return carry

    lax.fori_loop(0, 2, loop, 0)

    @pl.when(half == 1)
    def _():
        low_ref[...] = out_ref[:4]
        high_ref[...] = out_ref[4:]


def feed_weight_grads(which, codes, lefts, right):
    ff, rows = lefts[0].shape
    cut = right.shape[1] // 8
    count = len(lefts)
    shape = (4, ff, cut) if count == 1 else (4, count, ff, cut)
    low, high = pl.pallas_call(
        functools.partial(feed_grad_kernel, which, count),
        name="feed_weight_grads",
        grid_spec=pltpu.PrefetchScalarGridSpec(
            num_scalar_prefetch=1,
            grid=(2,),
            in_specs=[pl.BlockSpec((rows, 4 * cut), lambda s, codes: (0, s ^ (codes[which] >> 2)))]
            + [once((ff, rows), lambda s, codes: (0, 0))] * count,
            out_specs=[once(shape, lambda s, codes: (0,) * len(shape))] * 2,
            scratch_shapes=[pltpu.VMEM((8,) + shape[1:], BF16)],
        ),
        out_shape=[pltpu.HBM(shape, BF16)] * 2,
        compiler_params=pltpu.CompilerParams(
            dimension_semantics=("arbitrary",), vmem_limit_bytes=40 << 20
        ),
    )(codes, *[outside(value) for value in (right, *lefts)])
    return high, low[2:], low[1:2], low[:1]


def join_kernel(which, by_rows, cuts, codes, near_ref, far_ref, *outs):
    tall, wide = near_ref.shape[-2:]

    def put(i, carry):
        position = i ^ codes[which]
        place = position & 3
        piece = jnp.where(position >= 4, far_ref[place].astype(F32), near_ref[place].astype(F32))
        rows = pl.ds(pl.multiple_of(i * tall, 8), tall)
        columns = pl.ds(pl.multiple_of(i * wide, wide), wide)
        if by_rows:
            low = 0
            for out, cut in zip(outs, cuts):
                out[rows, :] = piece[:, low : low + cut]
                low += cut
        elif len(outs) == 1:
            outs[0][:, columns] = piece
        else:
            for k, out in enumerate(outs):
                out[:, columns] = piece[k]
        return carry

    lax.fori_loop(0, 8, put, 0)


def join(which, codes, near, far, cuts=None):
    tall, wide = near.shape[-2:]
    vmem = pl.BlockSpec(memory_space=pltpu.VMEM)
    if cuts:
        shapes = [jax.ShapeDtypeStruct((8 * tall, cut), F32) for cut in cuts]
    else:
        shapes = [jax.ShapeDtypeStruct((tall, 8 * wide), F32)] * (near.shape[1] if near.ndim == 4 else 1)
    return pl.pallas_call(
        functools.partial(join_kernel, which, bool(cuts), cuts),
        name="join_pieces",
        in_specs=[pl.BlockSpec(memory_space=pltpu.SMEM), vmem, vmem],
        out_specs=[vmem] * len(shapes),
        out_shape=shapes,
        compiler_params=pltpu.CompilerParams(vmem_limit_bytes=20 << 20),
    )(codes, near, far)


def spread_kernel(which, contracts, codes, *refs):
    jobs, refs = refs[: 2 * len(contracts)], refs[2 * len(contracts) :]
    heads, (last_ref, near_ref, own_ref, acc_ref, head_ref) = refs[:-5], refs[-5:]
    cut = near_ref.shape[1]

    def put(low, width, take):
        def place(position, carry):
            start = pl.multiple_of((position ^ codes[which]) * cut, cut)
            for t in range(4):
                value = take(t, start)
                if t >= 2:
                    last_ref[t - 2, position, :, low : low + width] = value
                else:
                    (own_ref, near_ref)[t][position, :, low : low + width] = value
            return carry

        lax.fori_loop(0, 8, place, 0, unroll=4)

    low = 0
    for i, contract in enumerate(contracts):
        right = jobs[2 * i + 1]
        width = right.shape[1 - contract[1][0]]
        acc_ref[:, :width] = dot(jobs[2 * i][...], right[...], contract)
        put(low, width, lambda t, start: acc_ref[pl.ds(t * 8 * cut + start, cut), :width].astype(BF16))
        low += width
    if heads:
        for p in range(4):
            mask = p ^ codes[2]
            place = (mask & 1) * 2 + (mask >> 1)
            head_ref[place, :, :LAT] = heads[2 * p][...]
            head_ref[place, :, LAT:] = heads[2 * p + 1][...]
        put(low, 2 * LAT, lambda t, start: head_ref[t, pl.ds(start, cut), :])


def spread_product(which, codes, jobs, heads=()):
    tall = jobs[0][0].shape[1 - jobs[0][2][0][0]]
    widths = [right.shape[1 - contract[1][0]] for _, right, contract in jobs]
    wide = sum(widths) + (2 * LAT if heads else 0)
    cut = tall // 32
    vmem = pl.BlockSpec(memory_space=pltpu.VMEM)
    operands = [x for left, right, _ in jobs for x in (left, right)] + list(heads)
    return pl.pallas_call(
        functools.partial(spread_kernel, which, [contract for _, _, contract in jobs]),
        name="spread_product",
        in_specs=[pl.BlockSpec(memory_space=pltpu.SMEM)] + [vmem] * len(operands),
        out_specs=[vmem] * 3,
        scratch_shapes=[pltpu.VMEM((tall, max(widths)), F32), pltpu.VMEM((4, tall // 4, 2 * LAT), BF16)],
        out_shape=[
            pltpu.HBM((2, 8, cut, wide), BF16),
            pltpu.HBM((8, cut, wide), BF16),
            pltpu.HBM((8, cut, wide), BF16),
        ],
        compiler_params=pltpu.CompilerParams(vmem_limit_bytes=20 << 20),
    )(codes, *operands)


class ShardSum:
    def __init__(self, last, near, own):
        self.near, self.own = near, own
        self.beside = swap(last, "fsdp", 1)

    def step(self, *tokens):
        self.beside = after(self.beside, *tokens) if tokens else self.beside
        sent = plus(self.near, self.beside[1])
        self.across = swap(sent, "fsdp", 2)
        return sent

    def part(self, low, high):
        return plus(self.own[low:high], self.beside[0, low:high], self.across[low:high])


def four_parts(part):
    return part(4, 8), part(2, 4), part(1, 2), part(0, 1)


def on_device(
    tokens,
    out_grad,
    lengths,
    norm1_gain,
    w_query,
    w_latent,
    w_key_up,
    w_value_up,
    w_output,
    norm2_gain,
    w_gate,
    w_up,
    w_down,
):
    ctx_size = lax.axis_size("ctx")
    tok_rows, width = tokens.shape[1], tokens.shape[2]
    ff = w_gate.shape[1]
    group_rows = tok_rows * ctx_size
    seq_rows = min(SEQ_MAX, group_rows)
    slots = seq_rows // tok_rows
    ctx_rank = lax.axis_index("ctx")
    member = lax.axis_index("fsdp")
    slot_number = ctx_rank // slots
    rank = ctx_rank % slots
    length = jnp.sum(
        jnp.where(jnp.arange(lengths.shape[1], dtype=jnp.int32) == slot_number, lengths[0], 0)
    )
    meta = jnp.stack([rank, length, member]).astype(jnp.int32)
    query_pos = rank * tok_rows + jnp.arange(tok_rows, dtype=jnp.int32)
    row_valid = (query_pos < length).astype(F32)[:, None]
    piece = width // 4
    order_a, order_b = (0, 1, 2), (1, 2, 0)
    codes = jnp.stack([code_of(ctx_rank, order_a), code_of(ctx_rank, order_b), member, 0 * member]).astype(jnp.int32)

    def reorder(value):
        return jnp.concatenate(
            [lax.dynamic_slice_in_dim(value, (member ^ m) * piece, piece, 1) for m in ORDER], axis=1
        )

    def restore(value):
        back = {m: t for t, m in enumerate(ORDER)}
        parts = [value[:, back[m] * piece : (back[m] + 1) * piece] for m in range(4)]
        low = (member & 1) == 1
        parts = [jnp.where(low, parts[j ^ 1], parts[j]) for j in range(4)]
        high = (member & 2) == 2
        parts = [jnp.where(high, parts[j ^ 2], parts[j]) for j in range(4)]
        return jnp.concatenate(parts, axis=1)

    latent_full = gather_rows(w_latent)
    gains = gather_rows(jnp.stack([norm1_gain, norm2_gain])[None])
    gain_one = jnp.concatenate([gains[t, 0] for t in range(4)])
    gain_two = restore(jnp.concatenate([gains[t, 1:] for t in range(4)], axis=1))
    gain_one_f = gain_one.astype(F32)
    gain_two_f = gain_two.astype(F32)
    inputs = tokens[0].astype(F32)
    mixed_in = reorder(tokens[0]).astype(F32)
    scale_one = norm_scale(inputs)
    normed_one = mixed_in * scale_one
    normed = (normed_one * gain_one_f).astype(BF16)
    latent = dot(normed, latent_full).astype(BF16)
    pieces = [latent]
    left, right = latent, latent
    side = jnp.concatenate([w_key_up, w_value_up], axis=1)
    weights = [after(w_query, latent_full), after(side, latent_full)]
    for _ in range(min(2, slots // 2 - 1)):
        left, right = ring_step(left, right, slots)
        pieces += [left, right]
    query_full = gather_rows(weights[0], *pieces[1:3])
    side_full = gather_rows(weights[1], *pieces[-2:])
    near = tuple(range(len(pieces)))
    key_full, value_full = side_full[:, :LAT], side_full[:, LAT:]
    q_t = dot(query_full, normed, ((0,), (1,))).astype(BF16)
    if len(pieces) < slots - 1:
        left, right = ring_step(left, right, slots)
        state = attention_forward(meta, q_t, key_full, value_full, pieces, near, slots, None, False)
        left, right = after((left, right), state[0])
        pieces += [left, right]
        while len(pieces) < slots - 1:
            left, right = ring_step(left, right, slots)
            pieces += [left, right]
    else:
        state = attention_forward(meta, q_t, key_full, value_full, pieces, near, slots, None, False)
    pieces.append(jnp.concatenate(ring_last(left, right, slots), axis=0))
    far = tuple(range(len(near), slots))
    att_t, mixture, log_total = attention_forward(
        meta, q_t, key_full, value_full, [pieces[k] for k in far], far, slots, state, True
    )
    blocks = jnp.stack(pieces)
    output_full = gather_rows(after(w_output, q_t), state[0])
    cotangent = out_grad[0].astype(F32) * row_valid
    feed_grad = gather_rows(after(cotangent.astype(BF16), q_t), state[0]).reshape(2, 2, tok_rows, width)
    feed_grad = jnp.swapaxes(feed_grad, 0, 1).reshape(4 * tok_rows, width)
    middle = inputs + dot(att_t, output_full, ((0,), (0,)))
    scale_two = norm_scale(middle)
    normed_two_raw = middle * scale_two
    normed_two = (normed_two_raw * gain_two_f).astype(BF16)
    gate_rows, up_rows = w_gate.T, w_up.T
    far_rows = swap(normed_two, "fsdp", 2)
    near_rows = swap(normed_two, "fsdp", 1)
    first = feed_forward(0, [after(normed_two, blocks), near_rows], feed_grad, gate_rows, up_rows, w_down)
    far_rows = after(far_rows, first[0])
    both_rows = swap(far_rows, "fsdp", 1)
    second = feed_forward(1, [far_rows, both_rows], feed_grad, gate_rows, up_rows, w_down, first[4:])
    normed_two_part = [first[0], second[0], jnp.stack([first[1], second[1]])]
    feed_part = [first[2], second[2], jnp.stack([first[3], second[3]])]
    ff_in, hidden = second[4], second[5:]
    beside = swap(normed_two_part[2], "fsdp", 1)
    wide_parts = feed_weight_grads(0, codes, hidden[1:], ff_in)
    wide_sum = CtxSum(wide_parts, order_a, ctx_size)
    beside = after(beside, wide_parts[0])
    home = plus(normed_two_part[1], beside[1])
    across = swap(home, "fsdp", 2)
    down_parts = feed_weight_grads(1, codes, hidden[:1], after(feed_grad, home))
    down_sum = CtxSum(down_parts, order_b, ctx_size)
    across = after(across, down_parts[0])
    normed_two_grad = (
        normed_two_part[0].astype(F32) + beside[0].astype(F32) + across.astype(F32)
    )
    middle_grad = cotangent + norm_back(normed_two_grad, normed_two_raw, scale_two, gain_two_f)
    gain_two_terms = reorder((normed_two_grad * normed_two_raw).astype(BF16))
    branch_grad = middle_grad.astype(BF16)
    da_t = dot(output_full, branch_grad, ((1,), (1,))).astype(BF16)

    def back(part, *tokens):
        return attention_backward(
            part, meta, q_t, after(da_t, *tokens), key_full, value_full, blocks, mixture, log_total
        )

    nn, tn = ((1,), (0,)), ((0,), (0,))
    back_0 = back(0, wide_sum.sent, down_sum.sent)
    token = back_0[0]
    gates = [down_sum.step(token), wide_sum.step(token)]
    feed_part = after(feed_part, token)
    feed_beside = swap(feed_part[2], "fsdp", 1)
    back_1 = back(1, *gates)
    token = back_1[0]
    tt = ((0,), (1,))
    early_shards = ShardSum(
        *spread_product(
            1,
            codes,
            [
                (att_t, after(branch_grad, token), nn),
                (normed, back_0[0], tt),
                (normed, token, tt),
                (gain_two_terms, jnp.ones((tok_rows, 128), BF16), tn),
            ],
        )
    )
    sum_0 = SlotSum(back_0[3], back_1[3])
    gates = [down_sum.step(token), wide_sum.step(token)]
    gates.append(down_sum.step(early_shards.own))
    feed_home = plus(feed_part[1], after(feed_beside, token)[1])
    feed_across = swap(feed_home, "fsdp", 2)
    back_2 = back(2, sum_0.sent, early_shards.own, feed_home, *gates)
    token = back_2[0]
    gates = [sum_0.step(token), early_shards.step(token), down_sum.step(token), wide_sum.step(token)]
    back_3 = back(3, *gates)
    backward = [back_0, back_1, back_2, back_3]

    clock = [back_3[0]]

    def tick(value):
        clock[0] = value

    def ready(each):
        each.across = after(each.across, clock[0])

    sum_1 = SlotSum(back_2[3], back_3[3])
    ready(early_shards)
    early_sum = CtxSum(four_parts(early_shards.part), order_b, ctx_size)
    tick(early_sum.sent)
    heads = [x for part in backward for x in (part[1], part[2])]
    late_shards = ShardSum(
        *spread_product(0, codes, [(normed, back_2[0], tt), (normed, after(back_3[0], sum_1.sent), tt)], heads)
    )
    tick(late_shards.own)
    feed_out = plus_wide(feed_part[0], feed_beside[0], after(feed_across, clock[0]))
    result = ((middle + feed_out) * row_valid).astype(BF16)
    tick(result)
    tick(down_sum.take(clock[0]))
    tick(sum_0.step(clock[0]))
    tick(late_shards.step(clock[0]))
    tick(wide_sum.take(clock[0]))
    tick(early_sum.step(clock[0]))
    tick(sum_1.step(clock[0]))
    tick(wide_sum.give(clock[0]))
    sum_0.got = after(sum_0.got, clock[0])
    latent_0 = sum_0.finish()
    tick(latent_0)
    tick(early_sum.step(clock[0]))
    tick(sum_1.step(clock[0]))
    tick(down_sum.give(clock[0]))
    ready(late_shards)
    late_sum = CtxSum(four_parts(late_shards.part), order_a, ctx_size)
    tick(late_sum.sent)
    tick(early_sum.step(clock[0]))
    sum_1.got = after(sum_1.got, clock[0])
    latent_grad = jnp.concatenate([latent_0, sum_1.finish()], axis=1)
    latent_shards = ShardSum(*spread_product(1, codes, [(normed, latent_grad, tn)]))
    tick(latent_shards.step(latent_grad))
    tick(early_sum.step(clock[0]))
    tick(late_sum.step(clock[0]))
    tick(wide_sum.step(clock[0]))
    tick(early_sum.step(clock[0]))
    ready(latent_shards)
    latent_sum = CtxSum(four_parts(latent_shards.part), order_b, ctx_size)
    tick(latent_sum.sent)

    def tick_join(which, done, cuts=None):
        near_part, far_part = done.finish()
        out = join(which, codes, near_part, after(far_part, clock[0]), cuts)
        tick(out[0])
        return out

    half = NH * HD // 2
    tick(late_sum.step(clock[0]))
    tick(latent_sum.step(clock[0]))
    (down_grad,) = tick_join(1, down_sum)
    tick(late_sum.step(clock[0]))
    tick(latent_sum.step(clock[0]))
    output_grad, query_grad_0, gain_two_grad = tick_join(1, early_sum, (width, half, 128))
    tick(late_sum.step(clock[0]))
    tick(latent_sum.step(clock[0]))
    tick(late_sum.step(clock[0]))
    tick(latent_sum.step(clock[0]))
    gate_w_grad, up_w_grad = tick_join(0, wide_sum)
    tick(latent_sum.step(clock[0]))
    query_grad_1, key_grad, value_grad = tick_join(0, late_sum, (half, LAT, LAT))
    query_grad = jnp.concatenate([query_grad_0, query_grad_1], axis=1)
    (latent_w_grad,) = tick_join(1, latent_sum, (GRP * LAT,))
    dq_t = jnp.concatenate([part[0] for part in backward], axis=0)

    normed_grad = dot(dq_t, query_full, ((0,), (1,))) + dot(
        latent_grad, latent_full, ((1,), (1,))
    )
    input_grad = middle_grad + restore(
        norm_back(normed_grad, normed_one, scale_one, gain_one_f)
    )
    gain_one_grad = (
        jnp.sum(w_query.astype(F32) * query_grad, axis=1)
        + jnp.sum(w_latent.astype(F32) * latent_w_grad, axis=1)
    ) / norm1_gain.astype(F32)
    return (
        result[None],
        input_grad[None],
        gain_one_grad,
        query_grad,
        latent_w_grad,
        key_grad,
        value_grad,
        output_grad,
        gain_two_grad[:, 0],
        gate_w_grad.T,
        up_w_grad.T,
        down_grad,
    )


def solution(mesh):
    rows = P("fsdp", None)
    cols = P(None, "fsdp")
    toks = P("fsdp", "ctx", None)
    vec = P("fsdp")
    return jax.shard_map(
        on_device,
        mesh=mesh,
        in_specs=(toks, toks, rows, vec, rows, rows, rows, rows, rows, vec, cols, cols, rows),
        out_specs=(toks, toks, vec, rows, rows, rows, rows, rows, vec, cols, cols, rows),
        check_vma=False,
    )
```
